128 devices in a mesh: front: 2 (over core), row: 8 (over y, x_hi), col: 8 (over z, x_lo).
Axes of the slice: x: 4 (x_hi: 2, x_lo: 2; x = x_hi * 2 + x_lo), y: 4, z: 4, core: 2. Of those that a mesh axis runs over, the one named last changes fastest.
Arguments:
- front_matrix: bfloat16 [2, 3, 8, 256, 3, 8, 256], P('front', None, 'row', None, None, 'col'), as said below
- contributions: bfloat16 [2, 8, 8, 32, 256, 256], P('front', 'row', 'col'), may hold values from -3 to 3
- target_front: int32 [2, 8, 8, 32], P('front', 'row', 'col'), may hold values from 0 to 1, as said below
- target_row: int32 [2, 8, 8, 32], P('front', 'row', 'col'), may hold values from 8 to 23, as said below
- target_col: int32 [2, 8, 8, 32], P('front', 'row', 'col'), may hold values from 0 to 22, as said below
- live_count: int32 [2, 8, 8], P('front', 'row', 'col'), may hold values from 24 to 32
Outputs:
- factor: float32 [2, 3, 8, 256, 3, 8, 256], P('front', None, 'row', None, None, 'col')
The draws below stay inside these ranges and needn't reach their ends.
Inputs may be any that keep to these rules, and one draw needn't show every extreme that they name: `front_matrix`: Symmetric; its leading 2 * 2 * 256 rows and columns form a strictly diagonally dominant block with a positive diagonal. `target_front`: among one device's live slots at most 2 aim at one pair of parent front and target_row modulo the number of row devices, and on every device one such pair takes exactly 2. `target_row`: never one of the first 4 tile rows, nor one of the first tile rows as many as the col devices. `target_col`: below the slot's target_row, and congruent to the holding device's col index modulo the number of col devices.
All inputs are finite; a program needn't handle non-finite values.
Results may differ from the reference program's by a relative error of at most 0.0003.
Values may be sent and summed in bfloat16 or wider, within the bound.
No kernel may reach another device: no remote copies, remote signals or barrier semaphores. Data moves between devices by JAX's collectives and lax.ppermute only.
A program may use at most 128 MiB of HBM per device.

```python
import jax
import jax.numpy as jnp
from jax import lax

F = 6144
TS = 256
PANEL_TILES = 2
PANELS = 2
SLOTS = 32
FRONTS = 2
NT = 24
RT = 3
CT = 3
CAP = 2
N_ROW = 8
N_COL = 8


def draw_front_matrix(key, part):
    lead_size = 2 * PANEL_TILES * TS
    key_raw, key_lead, key_rest = jax.random.split(jax.random.fold_in(key, 3), 3)
    raw = jax.random.uniform(key_raw, (FRONTS, F, F), jnp.float32, -1.0, 1.0)
    diag_lead = jax.random.uniform(key_lead, (FRONTS, F), jnp.float32, 16.0, 32.0)
    diag_rest = jax.random.uniform(key_rest, (FRONTS, F), jnp.float32, 4.0, 12.0)
    mirrored = 0.5 * (raw + jnp.swapaxes(raw, 1, 2))
    positions = jnp.arange(F)
    in_lead = positions < lead_size
    both_lead = in_lead[:, None] & in_lead[None, :]
    offdiag = jnp.where(both_lead[None], mirrored * (0.9 * 16.0 / lead_size), mirrored)
    diagonal = jnp.where(in_lead[None, :], diag_lead, diag_rest)
    identity = positions[:, None] == positions[None, :]
    matrix = jnp.where(identity[None], diagonal[:, :, None], offdiag)
    return matrix.reshape(FRONTS, RT, N_ROW, TS, CT, N_COL, TS).astype(jnp.bfloat16)


def route_draw(key):
    base_key = jax.random.fold_in(key, 11)
    key_hot, key_order, key_row, key_col = jax.random.split(base_key, 4)
    grid = (FRONTS, N_ROW, N_COL)
    others = FRONTS * N_ROW
    spread = max(others - 1, 1)
    hottest = jax.random.randint(key_hot, grid + (1,), 0, others)
    scores = jax.random.randint(key_order, grid + (spread,), 0, 1 << 20) * spread + jnp.arange(spread)
    ordering = jnp.argsort(scores, axis=-1)
    slot_ids = jnp.arange(SLOTS)
    cycle = jnp.maximum(slot_ids - CAP, 0) % spread
    picked = jnp.take(ordering, cycle, axis=-1)
    destination = jnp.where(slot_ids < CAP, hottest, (hottest + 1 + picked) % others)
    own_front = jnp.arange(FRONTS).reshape(FRONTS, 1, 1, 1)
    fronts_to = (own_front + destination // N_ROW) % FRONTS
    row_class = destination % N_ROW
    lowest = max(2 * PANEL_TILES, N_COL)
    smallest = (lowest - row_class + N_ROW - 1) // N_ROW
    local_row = jax.random.randint(key_row, grid + (SLOTS,), smallest, RT)
    rows_to = local_row * N_ROW + row_class
    column_class = jnp.arange(N_COL).reshape(1, 1, N_COL, 1)
    largest = (rows_to - column_class + N_COL - 1) // N_COL
    local_col = jax.random.randint(key_col, grid + (SLOTS,), 0, largest)
    cols_to = local_col * N_COL + column_class
    return (fronts_to.astype(jnp.int32), rows_to.astype(jnp.int32), cols_to.astype(jnp.int32))


def draw_target_front(key, part):
    return route_draw(key)[0]


def draw_target_row(key, part):
    return route_draw(key)[1]


def draw_target_col(key, part):
    return route_draw(key)[2]


def place_ends(array, stream_key, low, top_value):
    shape = array.shape
    spot = [jax.random.randint(jax.random.fold_in(stream_key, axis), (), 0, shape[axis]) for axis in range(len(shape))]
    array = array.at[tuple(spot)].set(low)
    longest = shape.index(max(shape))
    spot[longest] = (spot[longest] + 1) % shape[longest]
    return array.at[tuple(spot)].set(top_value)


def block_scale(own_key, extent, shards, low, top_value):
    gain = 1.0
    for dim, shards_of in shards:
        heights = jax.random.uniform(jax.random.fold_in(jax.random.fold_in(own_key, 6), dim), (shards_of,), jnp.float32, low / len(shards), top_value / len(shards))
        gain = gain * jnp.repeat(jnp.exp(heights), extent[dim] // shards_of).reshape((-1,) + (1,) * (len(extent) - 1 - dim))
    return gain


def normal_values(key, dims, width, bound, shards=(), kind=jnp.bfloat16):
    gain = block_scale(key, dims, shards, -0.22, 0.18) if shards else 1.0
    result = jax.random.normal(key, dims, jnp.float32) * width * gain
    return jnp.minimum(jnp.maximum(result, -bound), bound).astype(kind)


def setup_inputs(seed: int = 0) -> dict:
    seeds = jax.random.split(jax.random.key(seed), 7)
    return {
        "front_matrix": draw_front_matrix(jax.random.fold_in(seeds[6], 71), 0),
        "contributions": normal_values(seeds[1], (FRONTS, N_ROW, N_COL, SLOTS, TS, TS), 0.5, 3.0, ((0, 2), (1, 8), (2, 8))),
        "target_front": draw_target_front(jax.random.fold_in(seeds[6], 71), 0),
        "target_row": draw_target_row(jax.random.fold_in(seeds[6], 71), 0),
        "target_col": draw_target_col(jax.random.fold_in(seeds[6], 71), 0),
        "live_count": place_ends(jax.random.randint(seeds[5], (FRONTS, N_ROW, N_COL), 3 * SLOTS // 4, SLOTS + 1), jax.random.fold_in(seeds[5], 1), 3 * SLOTS // 4, SLOTS).astype(jnp.int32),
    }


def mirror_tiles(square, tile_size):
    tile_ids = jnp.arange(square.shape[0]) // tile_size
    return jnp.where(tile_ids[:, None] >= tile_ids[None, :], square, square.T)

def panel_factor(square, tile_size):
    return jnp.linalg.cholesky(mirror_tiles(square, tile_size))

def below_solve(lead_factor, row_block):
    return lax.linalg.triangular_solve(lead_factor, row_block, left_side=False, lower=True, transpose_a=True)

def reference(front_matrix, contributions, target_front, target_row, target_col, live_count):
    sources = FRONTS * N_ROW * N_COL
    contrib_tiles = contributions.reshape(sources, SLOTS, TS, TS)
    fronts_to = target_front.reshape(sources, SLOTS)
    flat_tile = (target_row * NT + target_col).reshape(sources, SLOTS)
    live_slots = (jnp.arange(SLOTS, dtype=jnp.int32)[None, None, None, :] < live_count[..., None]).reshape(sources, SLOTS)
    panel_width = PANEL_TILES * TS

    def one_front(front_number):
        matrix = front_matrix[front_number].astype(jnp.float32).reshape(F, F)
        pieces = matrix.reshape(NT, TS, NT, TS).transpose(0, 2, 1, 3).reshape(NT * NT, TS, TS)
        pieces = jnp.concatenate([pieces, jnp.zeros((1, TS, TS), jnp.float32)], axis=0)

        def add_source(source, totals):
            arrives = live_slots[source] & (fronts_to[source] == front_number)
            where_to = jnp.where(arrives, flat_tile[source], NT * NT).astype(jnp.int32)
            return totals.at[where_to].add(contrib_tiles[source].astype(jnp.float32))
        pieces = lax.fori_loop(0, sources, add_source, pieces)
        matrix = pieces[:NT * NT].reshape(NT, NT, TS, TS).transpose(0, 2, 1, 3).reshape(F, F)
        for panel_number in range(PANELS):
            first_row = panel_number * panel_width
            after_row = first_row + panel_width
            lead_factor = panel_factor(matrix[first_row:after_row, first_row:after_row], TS)
            solved = below_solve(lead_factor, matrix[after_row:, first_row:after_row])
            product = jnp.dot(solved.astype(jnp.float32), solved.T.astype(jnp.float32), precision=lax.Precision.HIGHEST, preferred_element_type=jnp.float32)
            matrix = matrix.at[after_row:, after_row:].set(matrix[after_row:, after_row:] - product)
            column = jnp.concatenate([jnp.zeros((first_row, panel_width), jnp.float32), lead_factor, solved], axis=0)
            matrix = matrix.at[:, first_row:after_row].set(column)
        tile_ids = jnp.arange(F) // TS
        matrix = jnp.where(tile_ids[:, None] >= tile_ids[None, :], matrix, 0.0)
        return matrix.reshape(RT, N_ROW, TS, CT, N_COL, TS)
    return lax.map(one_front, jnp.arange(FRONTS, dtype=jnp.int32))
```

```python
import jax
import jax.numpy as jnp
from jax import lax
from jax.experimental import pallas as pl
from jax.experimental.pallas import tpu as pltpu
from jax.sharding import PartitionSpec as P

LEAD_TILES = 4
BLOCK = 128
STRIP = 8
VMEM_BYTES = 56 * 1024 * 1024


def vmem():
    return pl.BlockSpec(memory_space=pltpu.VMEM)


def smem():
    return pl.BlockSpec(memory_space=pltpu.SMEM)


def hbm():
    return pl.BlockSpec(memory_space=pl.ANY)


def nt(left, right, precision=None):
    return lax.dot_general(
        left, right, (((1,), (1,)), ((), ())), precision=precision, preferred_element_type=jnp.float32
    )


def split(value):
    high = value.astype(jnp.bfloat16)
    return high, (value - high.astype(jnp.float32)).astype(jnp.bfloat16)


def nt3(left, right):
    return nt(left[0], right[0]) + (nt(left[0], right[1]) + nt(left[1], right[0]))


def pack(contributions, target_front, target_row, target_col, live_count, n_front, n_row, n_col, tile_cols):
    slots, size, _ = contributions.shape
    capacity = max(2, -(-slots // (n_front * n_row)))
    buckets = n_front * n_row * capacity

    def kernel(front_ref, row_ref, col_ref, live_ref, tiles_ref, packed_ref, targets_ref, counts, sems):
        live = live_ref[0]

        def clear(i, carry):
            targets_ref[i] = -1
            return carry

        lax.fori_loop(0, buckets, clear, 0)

        def clear_counts(i, carry):
            counts[i] = 0
            return carry

        lax.fori_loop(0, n_front * n_row, clear_counts, 0)

        def copy(slot, bucket):
            return pltpu.make_async_copy(tiles_ref.at[slot], packed_ref.at[bucket], sems.at[slot])

        def send(slot, carry):
            row, col = row_ref[slot], col_ref[slot]
            destination = front_ref[slot] * n_row + lax.rem(row, n_row)
            position = counts[destination]
            counts[destination] = position + 1
            bucket = destination * capacity + position
            targets_ref[bucket] = lax.div(row, n_row) * tile_cols + lax.div(col, n_col)
            copy(slot, bucket).start()
            return carry

        lax.fori_loop(0, live, send, 0)

        def finish(slot, carry):
            copy(slot, 0).wait()
            return carry

        lax.fori_loop(0, live, finish, 0)

    return pl.pallas_call(
        kernel,
        name="pack",
        out_shape=(
            jax.ShapeDtypeStruct((buckets, size, size), contributions.dtype),
            jax.ShapeDtypeStruct((buckets,), jnp.int32),
        ),
        in_specs=[smem()] * 4 + [hbm()],
        out_specs=(hbm(), smem()),
        scratch_shapes=[pltpu.SMEM((n_front * n_row,), jnp.int32), pltpu.SemaphoreType.DMA((slots,))],
    )(target_front, target_row, target_col, live_count, contributions)


EXTENDED = ((1, 0), (1, 1), (2, 0), (2, 1), (2, 2))


def assemble(received, arrived, front):
    total, size, _ = received.shape

    def kernel(arrived_ref, received_ref, front_ref, ext_ref, panel_ref, landed, sems):
        def copy(i):
            return pltpu.make_async_copy(received_ref.at[i], landed.at[i], sems.at[i])

        def fetch(i, carry):
            @pl.when(arrived_ref[i] >= 0)
            def _():
                copy(i).start()

            return carry

        lax.fori_loop(0, total, fetch, 0)
        for slot, (a, b) in enumerate(EXTENDED):
            ext_ref[slot] = front_ref[a, b].astype(jnp.float32)

        def add(i, carry):
            target = arrived_ref[i]

            @pl.when(target >= 0)
            def _():
                copy(i).wait()
                slot = jnp.where(target >= 6, target - 4, target - 3)
                ext_ref[slot] = ext_ref[slot] + landed[i].astype(jnp.float32)

            return carry

        lax.fori_loop(0, total, add, 0)
        panel_ref[0:size] = ext_ref[0]
        panel_ref[size : 2 * size] = ext_ref[2]

    return pl.pallas_call(
        kernel,
        name="assemble",
        out_shape=(
            jax.ShapeDtypeStruct((len(EXTENDED), size, size), jnp.float32),
            jax.ShapeDtypeStruct((2 * size, size), jnp.float32),
        ),
        in_specs=[smem(), hbm(), vmem()],
        out_specs=(vmem(), vmem()),
        scratch_shapes=[pltpu.VMEM((total, size, size), jnp.bfloat16), pltpu.SemaphoreType.DMA((total,))],
        compiler_params=pltpu.CompilerParams(vmem_limit_bytes=VMEM_BYTES),
    )(arrived, received, front)


def pick_lane(value, lane):
    index = jnp.full(value.shape, lane, jnp.int32)
    return jnp.take_along_axis(value, index, axis=1, mode="promise_in_bounds")


def factor_block(work):
    rows = lax.broadcasted_iota(jnp.int32, (BLOCK, BLOCK), 0)
    lanes = lax.broadcasted_iota(jnp.int32, (STRIP, BLOCK), 1)
    strip_rows = lax.broadcasted_iota(jnp.int32, (STRIP, BLOCK), 0)

    def spread(value, i):
        return jnp.broadcast_to(value[i : i + 1, :], value.shape)

    def step(number, carry):
        base = pl.multiple_of(number * STRIP, STRIP)
        strip = work[pl.ds(base, STRIP), :]
        own = [pick_lane(strip, base + i) for i in range(STRIP)]
        whole = work[...]
        below = rows >= base + STRIP
        columns = [jnp.where(below, pick_lane(whole, base + i), 0.0) for i in range(STRIP)]
        for i in range(STRIP):
            pivot = spread(own[i], i)
            inverse = 1.0 / pivot
            factors = jnp.where(strip_rows > i, own[i] * inverse, 0.0)
            line = jnp.where(lanes == base + i, pivot + pivot, spread(strip, i))
            strip = strip - factors * line
            lower = columns[i] * jnp.broadcast_to(inverse[0:1], whole.shape)
            for j in range(i + 1, STRIP):
                entry = spread(own[j], i)
                own[j] = own[j] - factors * entry
                columns[j] = columns[j] - lower * jnp.broadcast_to(entry[0:1], whole.shape)
            whole = whole - lower * jnp.broadcast_to(line[0:1], whole.shape)
        work[...] = whole
        work[pl.ds(base, STRIP), :] = strip
        return carry

    lax.fori_loop(0, BLOCK // STRIP, step, 0)


HIGHEST = lax.Precision.HIGHEST


def factorize(lead, ids, size):
    order = LEAD_TILES * size
    pairs = [(i, j) for i in range(LEAD_TILES) for j in range(i + 1)]
    blocks = order // BLOCK

    def kernel(ids_ref, lead_ref, high_ref, low_ref, inv_high_ref, inv_low_ref, own_ref, full, inverses, work):
        r = lax.broadcasted_iota(jnp.int32, (BLOCK, BLOCK), 0)
        c = lax.broadcasted_iota(jnp.int32, (BLOCK, BLOCK), 1)
        for number, (i, j) in enumerate(pairs):
            full[i * size : (i + 1) * size, j * size : (j + 1) * size] = (
                lead_ref[:, number].astype(jnp.float32).reshape(size, size)
            )
        for k in range(blocks):
            s, e = k * BLOCK, (k + 1) * BLOCK
            work[...] = full[s:e, s:e]
            factor_block(work)
            done = work[...]
            diagonal = jnp.where(r == c, done, 0.0)
            root = lax.rsqrt(jnp.sum(diagonal, axis=1, keepdims=True))
            inverse = jnp.where(r >= c, done, 0.0) * root * (1.0 / jnp.sum(diagonal, axis=0, keepdims=True))
            inverses[k] = inverse
            full[s:e, s:e] = (jnp.where(r <= c, done, 0.0) * root).T
            if e < order:
                panel = nt(full[e:order, s:e], inverse, HIGHEST)
                full[e:order, s:e] = panel
                for j in range(k + 1, blocks):
                    o = j * BLOCK
                    full[o:order, o : o + BLOCK] = full[o:order, o : o + BLOCK] - nt(
                        panel[o - e :], panel[o - e : o - e + BLOCK], HIGHEST
                    )
        half = size // BLOCK
        for q in range(LEAD_TILES):
            s = q * size
            full[s : s + BLOCK, s + BLOCK : s + size] = jnp.zeros((BLOCK, size - BLOCK), jnp.float32)
            first, second = inverses[q * half], inverses[q * half + 1]
            corner = -jnp.dot(
                second,
                jnp.dot(
                    full[s + BLOCK : s + size, s : s + BLOCK], first,
                    precision=HIGHEST, preferred_element_type=jnp.float32,
                ),
                precision=HIGHEST, preferred_element_type=jnp.float32,
            )
            for (y, x, part) in ((0, 0, first), (0, 1, jnp.zeros_like(first)), (1, 0, corner), (1, 1, second)):
                high, low = split(part)
                inv_high_ref[q, y * BLOCK : (y + 1) * BLOCK, x * BLOCK : (x + 1) * BLOCK] = high
                inv_low_ref[q, y * BLOCK : (y + 1) * BLOCK, x * BLOCK : (x + 1) * BLOCK] = low
        for number, (i, j) in enumerate(pairs):
            tile = full[i * size : (i + 1) * size, j * size : (j + 1) * size]
            high, low = split(tile)
            high_ref[i * size : (i + 1) * size, j * size : (j + 1) * size] = high
            low_ref[i * size : (i + 1) * size, j * size : (j + 1) * size] = low

            @pl.when((ids_ref[0] == i) & (ids_ref[1] == j))
            def _():
                own_ref[...] = tile

    wide = jax.ShapeDtypeStruct((order, order), jnp.bfloat16)
    inv = jax.ShapeDtypeStruct((LEAD_TILES, size, size), jnp.bfloat16)
    return pl.pallas_call(
        kernel,
        name="factorize",
        out_shape=(wide, wide, inv, inv, jax.ShapeDtypeStruct((size, size), jnp.float32)),
        in_specs=[smem(), vmem()],
        out_specs=(vmem(),) * 5,
        scratch_shapes=[
            pltpu.VMEM((order, order), jnp.float32),
            pltpu.VMEM((blocks, BLOCK, BLOCK), jnp.float32),
            pltpu.VMEM((BLOCK, BLOCK), jnp.float32),
        ],
        compiler_params=pltpu.CompilerParams(vmem_limit_bytes=VMEM_BYTES),
    )(ids, lead)


def finish(ids, rows, cols, early, factors, own, extended, front):
    size = own.shape[0]
    order = LEAD_TILES * size
    tile_rows, tile_cols = front.shape[:2]
    lanes = 128
    parts = size // lanes
    total = 6 * size

    def kernel(
        ids_ref, rows_ref, cols_ref, early_ref, high_ref, low_ref, ih_ref, il_ref, own_ref, ext_ref, front_ref,
        out_ref, xh, xl, panel,
    ):
        row, col = ids_ref[0], ids_ref[1]

        def put(a, b, tile):
            for part in range(parts):
                start = (a * size * tile_cols + b) * parts + part
                out_ref[pl.ds(start, size, stride=tile_cols * parts), :] = tile[:, part * lanes : (part + 1) * lanes]

        for q in range(LEAD_TILES):
            s, e = q * size, (q + 1) * size
            acc = jnp.concatenate(
                [
                    rows_ref[:, q].reshape(2 * size, size),
                    cols_ref[:, q].reshape(2 * size, size),
                    early_ref[:, q].astype(jnp.float32).reshape(size, size),
                    early_ref[:, LEAD_TILES + q].astype(jnp.float32).reshape(size, size),
                ],
                axis=0,
            )
            if q:
                acc = acc - nt3((xh[:, 0:s], xl[:, 0:s]), (high_ref[s:e, 0:s], low_ref[s:e, 0:s]))
            x = nt3(split(acc), (ih_ref[q], il_ref[q]))
            high, low = split(x)
            xh[:, s:e] = high
            xl[:, s:e] = low

            @pl.when(col == q)
            def _():
                panel[0 : 2 * size] = x[0 : 2 * size]
                panel[2 * size :] = x[4 * size : 5 * size]

        zero = jnp.zeros((size, size), jnp.float32)
        for a, b in ((0, 1), (0, 2), (1, 2)):
            put(a, b, zero)

        def update(a, b, base, x, y):
            def take(ref, n):
                return ref[n * size : (n + 1) * size, :]

            put(a, b, base - nt3((take(xh, x), take(xl, x)), (take(xh, y), take(xl, y))))

        in_panel = col < LEAD_TILES

        @pl.when(in_panel)
        def _():
            put(1, 0, panel[0:size])
            put(2, 0, panel[size : 2 * size])

        @pl.when(jnp.logical_not(in_panel))
        def _():
            update(1, 0, ext_ref[0], 0, 5)
            update(2, 0, ext_ref[2], 1, 5)

        lead_row = row < LEAD_TILES

        @pl.when(row < col)
        def _():
            put(0, 0, zero)
            put(1, 1, zero)
            put(2, 2, zero)

        @pl.when(row >= col)
        def _():
            @pl.when(lead_row)
            def _():
                put(0, 0, own_ref[...])

            @pl.when(jnp.logical_not(lead_row) & in_panel)
            def _():
                put(0, 0, panel[2 * size :])

            @pl.when(jnp.logical_not(in_panel))
            def _():
                update(0, 0, front_ref[0, 0].astype(jnp.float32), 4, 5)

            update(1, 1, ext_ref[1], 0, 2)
            update(2, 2, ext_ref[4], 1, 3)

        update(2, 1, ext_ref[3], 1, 2)

    return pl.pallas_call(
        kernel,
        name="finish",
        out_shape=jax.ShapeDtypeStruct((tile_rows * size * tile_cols * parts, lanes), jnp.float32),
        in_specs=[smem()] + [vmem()] * 10,
        out_specs=vmem(),
        scratch_shapes=[
            pltpu.VMEM((total, order), jnp.bfloat16),
            pltpu.VMEM((total, order), jnp.bfloat16),
            pltpu.VMEM((3 * size, size), jnp.float32),
        ],
        compiler_params=pltpu.CompilerParams(vmem_limit_bytes=VMEM_BYTES),
    )(ids, rows, cols, early, *factors, own, extended, front)


def exchange(value, axis):
    return lax.all_to_all(value, axis, split_axis=0, concat_axis=0, tiled=True)


def gather(value, axis):
    count = lax.axis_size(axis)
    return exchange(jnp.broadcast_to(value[None], (count,) + value.shape), axis)


def per_device(front_matrix, contributions, target_front, target_row, target_col, live_count):
    _, tile_rows, _, size, tile_cols, _, _ = front_matrix.shape
    n_front, n_row, n_col = (lax.axis_size(name) for name in ("front", "row", "col"))
    slots = contributions.shape[3]
    front = front_matrix.reshape(tile_rows, size, tile_cols, size).transpose(0, 2, 1, 3)
    ids = jnp.stack([lax.axis_index("row"), lax.axis_index("col")]).astype(jnp.int32)

    packed, targets = pack(
        contributions.reshape(slots, size, size),
        target_front.reshape(slots), target_row.reshape(slots), target_col.reshape(slots),
        live_count.reshape(1), n_front, n_row, n_col, tile_cols,
    )
    arrived = exchange(targets, ("front", "row"))
    received = exchange(packed, ("front", "row"))

    thin = size // n_col
    chunk = exchange(front[0, 0].reshape(n_col, thin, size), "col")[:LEAD_TILES]
    leading = gather(chunk, "row")
    lower = jnp.stack([leading[i, j] for i in range(LEAD_TILES) for j in range(i + 1)])
    lead = gather(lower, "col")
    aimed = jnp.concatenate([jnp.broadcast_to(chunk[None], leading.shape), leading], axis=1)
    early = exchange(aimed, "col")
    *factors, own = factorize(lead, ids, size)

    extended, panel = assemble(received, arrived, front)
    mine = exchange(panel.reshape(n_col, 2 * size // n_col, size), "col")[:LEAD_TILES]
    rows = gather(mine, "col")
    turned = lax.ppermute(
        mine, ("row", "col"), [(r * n_col + c, c * n_col + r) for r in range(n_row) for c in range(n_col)]
    )
    cols = gather(turned, "row")
    factor = finish(ids, rows, cols, early, factors, own, extended, front)
    return factor.reshape(1, tile_rows, 1, size, tile_cols, 1, size)


def solution(mesh):
    in_specs = (
        P("front", None, "row", None, None, "col", None),
        P("front", "row", "col", None, None, None),
        P("front", "row", "col", None),
        P("front", "row", "col", None),
        P("front", "row", "col", None),
        P("front", "row", "col"),
    )
    out_specs = P("front", None, "row", None, None, "col", None)
    return jax.shard_map(per_device, mesh=mesh, in_specs=in_specs, out_specs=out_specs, check_vma=False)
```

```python
import jax
import jax.numpy as jnp
from jax import lax
from jax.experimental import pallas as pl
from jax.experimental.pallas import tpu as pltpu
from jax.sharding import PartitionSpec as P

LEAD_TILES = 4
BLOCK = 128
STRIP = 8
FIRST_STEPS = 4
VMEM_BYTES = 56 * 1024 * 1024


def vmem():
    return pl.BlockSpec(memory_space=pltpu.VMEM)


def smem():
    return pl.BlockSpec(memory_space=pltpu.SMEM)


def hbm():
    return pl.BlockSpec(memory_space=pl.ANY)


def nt(left, right, precision=None):
    return lax.dot_general(
        left, right, (((1,), (1,)), ((), ())), precision=precision, preferred_element_type=jnp.float32
    )


def split(value):
    high = value.astype(jnp.bfloat16)
    return high, (value - high.astype(jnp.float32)).astype(jnp.bfloat16)


def nt3(left, right):
    return nt(left[0], right[0]) + (nt(left[0], right[1]) + nt(left[1], right[0]))


def pack(contributions, target_front, target_row, target_col, live_count, n_front, n_row, n_col, tile_cols):
    slots, size, _ = contributions.shape
    capacity = max(2, -(-slots // (n_front * n_row)))
    buckets = n_front * n_row * capacity

    def kernel(
        front_ref, row_ref, col_ref, live_ref, tiles_ref, packed_ref, targets_ref, counts, bucket_of, stage, sems_in, sems_out
    ):
        live = live_ref[0]

        def clear(i, carry):
            targets_ref[i] = -1
            return carry

        lax.fori_loop(0, buckets, clear, 0)

        def clear_counts(i, carry):
            counts[i] = 0
            return carry

        lax.fori_loop(0, n_front * n_row, clear_counts, 0)

        def fetch(slot, bucket):
            return pltpu.make_async_copy(tiles_ref.at[slot], stage.at[bucket], sems_in.at[slot])

        def store(slot, bucket):
            return pltpu.make_async_copy(stage.at[bucket], packed_ref.at[bucket], sems_out.at[slot])

        def send(slot, carry):
            row, col = row_ref[slot], col_ref[slot]
            destination = front_ref[slot] * n_row + lax.rem(row, n_row)
            position = counts[destination]
            counts[destination] = position + 1
            bucket = destination * capacity + position
            targets_ref[bucket] = lax.div(row, n_row) * tile_cols + lax.div(col, n_col)
            bucket_of[slot] = bucket
            fetch(slot, bucket).start()
            return carry

        lax.fori_loop(0, live, send, 0)

        def forward(slot, carry):
            bucket = bucket_of[slot]
            fetch(slot, bucket).wait()
            store(slot, bucket).start()
            return carry

        lax.fori_loop(0, live, forward, 0)

        def drain(slot, carry):
            store(slot, bucket_of[slot]).wait()
            return carry

        lax.fori_loop(0, live, drain, 0)

    return pl.pallas_call(
        kernel,
        name="pack",
        out_shape=(
            jax.ShapeDtypeStruct((buckets, size, size), contributions.dtype),
            jax.ShapeDtypeStruct((buckets,), jnp.int32),
        ),
        in_specs=[smem()] * 4 + [hbm()],
        out_specs=(hbm(), smem()),
        scratch_shapes=[
            pltpu.SMEM((n_front * n_row,), jnp.int32),
            pltpu.SMEM((slots,), jnp.int32),
            pltpu.VMEM((buckets, size, size), contributions.dtype),
            pltpu.SemaphoreType.DMA((slots,)),
            pltpu.SemaphoreType.DMA((slots,)),
        ],
        compiler_params=pltpu.CompilerParams(vmem_limit_bytes=VMEM_BYTES),
    )(target_front, target_row, target_col, live_count, contributions)


SCALE_ROWS = 8
SCALE_STEPS = 64


def encode(values):
    n, m = values.shape
    top = jnp.max(jnp.abs(values), axis=1, keepdims=True)
    code = jnp.floor(jnp.log2(jnp.maximum(top, 2.0**-110)) * SCALE_STEPS) + 1.0
    coded = jnp.round(values * jnp.exp2(15.0 - 1e-3 - code / SCALE_STEPS))
    picked = lax.broadcasted_iota(jnp.int32, (n, m), 0) == lax.broadcasted_iota(jnp.int32, (n, m), 1)
    line = jnp.sum(jnp.where(picked, code, 0.0), axis=0, keepdims=True)
    lines = jnp.broadcast_to(line, (SCALE_ROWS, m))
    return jnp.concatenate([coded, lines], axis=0).astype(jnp.int32).astype(jnp.int16)


def decode(coded):
    wide = coded.astype(jnp.int32).astype(jnp.float32)
    n, m = wide.shape[0] - SCALE_ROWS, wide.shape[1]
    values, line = wide[:n], wide[n : n + 1]
    picked = lax.broadcasted_iota(jnp.int32, (n, m), 0) == lax.broadcasted_iota(jnp.int32, (n, m), 1)
    code = jnp.sum(jnp.where(picked, jnp.broadcast_to(line, (n, m)), 0.0), axis=1, keepdims=True)
    return values * jnp.exp2(code / SCALE_STEPS - 15.0 + 1e-3)


EXTENDED = ((1, 0), (1, 1), (2, 0), (2, 1), (2, 2))


def assemble(received, arrived, front, chunks):
    total, size, _ = received.shape
    thin = 2 * size // chunks

    def kernel(arrived_ref, received_ref, front_ref, ext_ref, panel_ref, landed, sems):
        def copy(i):
            return pltpu.make_async_copy(received_ref.at[i], landed.at[i], sems.at[i])

        def fetch(i, carry):
            @pl.when(arrived_ref[i] >= 0)
            def _():
                copy(i).start()

            return carry

        lax.fori_loop(0, total, fetch, 0)
        for slot, (a, b) in enumerate(EXTENDED):
            ext_ref[slot] = front_ref[a, b].astype(jnp.float32)

        def add(i, carry):
            target = arrived_ref[i]

            @pl.when(target >= 0)
            def _():
                copy(i).wait()
                slot = jnp.where(target >= 6, target - 4, target - 3)
                ext_ref[slot] = ext_ref[slot] + landed[i].astype(jnp.float32)

            return carry

        lax.fori_loop(0, total, add, 0)
        for chunk in range(chunks):
            start = chunk * thin
            panel_ref[chunk] = encode(ext_ref[2 * (start // size), pl.ds(start % size, thin), :])

    return pl.pallas_call(
        kernel,
        name="assemble",
        out_shape=(
            jax.ShapeDtypeStruct((len(EXTENDED), size, size), jnp.float32),
            jax.ShapeDtypeStruct((chunks, thin + SCALE_ROWS, size), jnp.int16),
        ),
        in_specs=[smem(), hbm(), vmem()],
        out_specs=(vmem(), vmem()),
        scratch_shapes=[pltpu.VMEM((total, size, size), jnp.bfloat16), pltpu.SemaphoreType.DMA((total,))],
        compiler_params=pltpu.CompilerParams(vmem_limit_bytes=VMEM_BYTES),
    )(arrived, received, front)


def pick_lane(value, lane):
    index = jnp.full(value.shape, lane, jnp.int32)
    return jnp.take_along_axis(value, index, axis=1, mode="promise_in_bounds")


def factor_block(work):
    rows = lax.broadcasted_iota(jnp.int32, (BLOCK, BLOCK), 0)
    lanes = lax.broadcasted_iota(jnp.int32, (STRIP, BLOCK), 1)
    strip_rows = lax.broadcasted_iota(jnp.int32, (STRIP, BLOCK), 0)

    def spread(value, i):
        return jnp.broadcast_to(value[i : i + 1, :], value.shape)

    def step(number, carry):
        base = pl.multiple_of(number * STRIP, STRIP)
        strip = work[pl.ds(base, STRIP), :]
        own = [pick_lane(strip, base + i) for i in range(STRIP)]
        whole = work[...]
        below = rows >= base + STRIP
        columns = [jnp.where(below, pick_lane(whole, base + i), 0.0) for i in range(STRIP)]
        for i in range(STRIP):
            pivot = spread(own[i], i)
            inverse = 1.0 / pivot
            factors = jnp.where(strip_rows > i, own[i] * inverse, 0.0)
            line = jnp.where(lanes == base + i, pivot + pivot, spread(strip, i))
            strip = strip - factors * line
            lower = columns[i] * jnp.broadcast_to(inverse[0:1], whole.shape)
            for j in range(i + 1, STRIP):
                entry = spread(own[j], i)
                own[j] = own[j] - factors * entry
                columns[j] = columns[j] - lower * jnp.broadcast_to(entry[0:1], whole.shape)
            whole = whole - lower * jnp.broadcast_to(line[0:1], whole.shape)
        work[...] = whole
        work[pl.ds(base, STRIP), :] = strip
        return carry

    lax.fori_loop(0, BLOCK // STRIP, step, 0)


HIGHEST = lax.Precision.HIGHEST


def eliminate(full, inverses, work, blocks):
    order = full.shape[0]
    r = lax.broadcasted_iota(jnp.int32, (BLOCK, BLOCK), 0)
    c = lax.broadcasted_iota(jnp.int32, (BLOCK, BLOCK), 1)
    for k in blocks:
        s, e = k * BLOCK, (k + 1) * BLOCK
        work[...] = full[s:e, s:e]
        factor_block(work)
        done = work[...]
        diagonal = jnp.where(r == c, done, 0.0)
        root = lax.rsqrt(jnp.sum(diagonal, axis=1, keepdims=True))
        inverse = jnp.where(r >= c, done, 0.0) * root * (1.0 / jnp.sum(diagonal, axis=0, keepdims=True))
        inverses[k] = inverse
        full[s:e, s:e] = (jnp.where(r <= c, done, 0.0) * root).T
        if e < order:
            panel = nt(full[e:order, s:e], inverse, HIGHEST)
            full[e:order, s:e] = panel
            for o in range(e, order, BLOCK):
                full[o:order, o : o + BLOCK] = full[o:order, o : o + BLOCK] - nt(
                    panel[o - e :], panel[o - e : o - e + BLOCK], HIGHEST
                )


PAIRS = tuple((i, j) for i in range(LEAD_TILES) for j in range(i + 1))


def factorize_first(lead, size, blocks):
    order = LEAD_TILES * size

    def kernel(lead_ref, full, inverses, work):
        for number, (i, j) in enumerate(PAIRS):
            full[i * size : (i + 1) * size, j * size : (j + 1) * size] = (
                lead_ref[:, number].astype(jnp.float32).reshape(size, size)
            )
        eliminate(full, inverses, work, blocks)

    return pl.pallas_call(
        kernel,
        name="factorize_first",
        out_shape=(
            jax.ShapeDtypeStruct((order, order), jnp.float32),
            jax.ShapeDtypeStruct((order // BLOCK, BLOCK, BLOCK), jnp.float32),
        ),
        in_specs=[vmem()],
        out_specs=(vmem(),) * 2,
        scratch_shapes=[pltpu.VMEM((BLOCK, BLOCK), jnp.float32)],
        compiler_params=pltpu.CompilerParams(vmem_limit_bytes=VMEM_BYTES),
    )(lead)


def factorize_last(begun, begun_inverses, ids, size, blocks):
    order = LEAD_TILES * size

    def kernel(ids_ref, begun_ref, begun_inv_ref, high_ref, low_ref, inv_high_ref, inv_low_ref, own_ref, full, inverses, work):
        full[...] = begun_ref[...]
        inverses[...] = begun_inv_ref[...]
        eliminate(full, inverses, work, blocks)
        half = size // BLOCK
        for q in range(LEAD_TILES):
            s = q * size
            full[s : s + BLOCK, s + BLOCK : s + size] = jnp.zeros((BLOCK, size - BLOCK), jnp.float32)
            first, second = inverses[q * half], inverses[q * half + 1]
            corner = -jnp.dot(
                second,
                jnp.dot(
                    full[s + BLOCK : s + size, s : s + BLOCK], first,
                    precision=HIGHEST, preferred_element_type=jnp.float32,
                ),
                precision=HIGHEST, preferred_element_type=jnp.float32,
            )
            for (y, x, part) in ((0, 0, first), (0, 1, jnp.zeros_like(first)), (1, 0, corner), (1, 1, second)):
                high, low = split(part)
                inv_high_ref[q, y * BLOCK : (y + 1) * BLOCK, x * BLOCK : (x + 1) * BLOCK] = high
                inv_low_ref[q, y * BLOCK : (y + 1) * BLOCK, x * BLOCK : (x + 1) * BLOCK] = low
        for i, j in PAIRS:
            tile = full[i * size : (i + 1) * size, j * size : (j + 1) * size]
            high, low = split(tile)
            high_ref[i * size : (i + 1) * size, j * size : (j + 1) * size] = high
            low_ref[i * size : (i + 1) * size, j * size : (j + 1) * size] = low

            @pl.when((ids_ref[0] == i) & (ids_ref[1] == j))
            def _():
                own_ref[...] = tile

    wide = jax.ShapeDtypeStruct((order, order), jnp.bfloat16)
    inv = jax.ShapeDtypeStruct((LEAD_TILES, size, size), jnp.bfloat16)
    return pl.pallas_call(
        kernel,
        name="factorize_last",
        out_shape=(wide, wide, inv, inv, jax.ShapeDtypeStruct((size, size), jnp.float32)),
        in_specs=[smem(), vmem(), vmem()],
        out_specs=(vmem(),) * 5,
        scratch_shapes=[
            pltpu.VMEM((order, order), jnp.float32),
            pltpu.VMEM((order // BLOCK, BLOCK, BLOCK), jnp.float32),
            pltpu.VMEM((BLOCK, BLOCK), jnp.float32),
        ],
        compiler_params=pltpu.CompilerParams(vmem_limit_bytes=VMEM_BYTES),
    )(ids, begun, begun_inverses)


def finish(ids, rows, cols, early, factors, own, extended, front):
    size = own.shape[0]
    order = LEAD_TILES * size
    tile_rows, tile_cols = front.shape[:2]
    lanes = 128
    parts = size // lanes
    total = 6 * size

    def kernel(
        ids_ref, rows_ref, cols_ref, early_ref, high_ref, low_ref, ih_ref, il_ref, own_ref, ext_ref, front_ref,
        out_ref, xh, xl, panel,
    ):
        row, col = ids_ref[0], ids_ref[1]

        def put(a, b, tile):
            for part in range(parts):
                start = (a * size * tile_cols + b) * parts + part
                out_ref[pl.ds(start, size, stride=tile_cols * parts), :] = tile[:, part * lanes : (part + 1) * lanes]

        for q in range(LEAD_TILES):
            s, e = q * size, (q + 1) * size
            acc = jnp.concatenate(
                [
                    *[decode(rows_ref[k, q]) for k in range(rows_ref.shape[0])],
                    *[decode(cols_ref[k, q]) for k in range(cols_ref.shape[0])],
                    early_ref[:, q].astype(jnp.float32).reshape(size, size),
                    early_ref[:, LEAD_TILES + q].astype(jnp.float32).reshape(size, size),
                ],
                axis=0,
            )
            if q:
                acc = acc - nt3((xh[:, 0:s], xl[:, 0:s]), (high_ref[s:e, 0:s], low_ref[s:e, 0:s]))
            x = nt3(split(acc), (ih_ref[q], il_ref[q]))
            high, low = split(x)
            xh[:, s:e] = high
            xl[:, s:e] = low

            @pl.when(col == q)
            def _():
                panel[0 : 2 * size] = x[0 : 2 * size]
                panel[2 * size :] = x[4 * size : 5 * size]

        zero = jnp.zeros((size, size), jnp.float32)
        for a, b in ((0, 1), (0, 2), (1, 2)):
            put(a, b, zero)

        def update(a, b, base, x, y):
            def take(ref, n):
                return ref[n * size : (n + 1) * size, :]

            put(a, b, base - nt3((take(xh, x), take(xl, x)), (take(xh, y), take(xl, y))))

        in_panel = col < LEAD_TILES

        @pl.when(in_panel)
        def _():
            put(1, 0, panel[0:size])
            put(2, 0, panel[size : 2 * size])

        @pl.when(jnp.logical_not(in_panel))
        def _():
            update(1, 0, ext_ref[0], 0, 5)
            update(2, 0, ext_ref[2], 1, 5)

        lead_row = row < LEAD_TILES

        @pl.when(row < col)
        def _():
            put(0, 0, zero)
            put(1, 1, zero)
            put(2, 2, zero)

        @pl.when(row >= col)
        def _():
            @pl.when(lead_row)
            def _():
                put(0, 0, own_ref[...])

            @pl.when(jnp.logical_not(lead_row) & in_panel)
            def _():
                put(0, 0, panel[2 * size :])

            @pl.when(jnp.logical_not(in_panel))
            def _():
                update(0, 0, front_ref[0, 0].astype(jnp.float32), 4, 5)

            update(1, 1, ext_ref[1], 0, 2)
            update(2, 2, ext_ref[4], 1, 3)

        update(2, 1, ext_ref[3], 1, 2)

    return pl.pallas_call(
        kernel,
        name="finish",
        out_shape=jax.ShapeDtypeStruct((tile_rows * size * tile_cols * parts, lanes), jnp.float32),
        in_specs=[smem()] + [vmem()] * 10,
        out_specs=vmem(),
        scratch_shapes=[
            pltpu.VMEM((total, order), jnp.bfloat16),
            pltpu.VMEM((total, order), jnp.bfloat16),
            pltpu.VMEM((3 * size, size), jnp.float32),
        ],
        compiler_params=pltpu.CompilerParams(vmem_limit_bytes=VMEM_BYTES),
    )(ids, rows, cols, early, *factors, own, extended, front)


def exchange(value, axis):
    return lax.all_to_all(value, axis, split_axis=0, concat_axis=0, tiled=True)


def gather(value, axis):
    count = lax.axis_size(axis)
    return exchange(jnp.broadcast_to(value[None], (count,) + value.shape), axis)


def per_device(front_matrix, contributions, target_front, target_row, target_col, live_count):
    _, tile_rows, _, size, tile_cols, _, _ = front_matrix.shape
    n_front, n_row, n_col = (lax.axis_size(name) for name in ("front", "row", "col"))
    slots = contributions.shape[3]
    front = front_matrix.reshape(tile_rows, size, tile_cols, size).transpose(0, 2, 1, 3)
    ids = jnp.stack([lax.axis_index("row"), lax.axis_index("col")]).astype(jnp.int32)

    packed, targets = pack(
        contributions.reshape(slots, size, size),
        target_front.reshape(slots), target_row.reshape(slots), target_col.reshape(slots),
        live_count.reshape(1), n_front, n_row, n_col, tile_cols,
    )
    arrived = exchange(targets, ("front", "row"))
    received = exchange(packed, ("front", "row"))

    thin = size // n_col
    chunk = exchange(front[0, 0].reshape(n_col, thin, size), "col")[:LEAD_TILES]
    leading = gather(chunk, "row")
    lower = jnp.stack([leading[i, j] for i in range(LEAD_TILES) for j in range(i + 1)])
    lead = gather(lower, "col")
    aimed = jnp.concatenate([jnp.broadcast_to(chunk[None], leading.shape), leading], axis=1)
    early = exchange(aimed, "col")
    steps = LEAD_TILES * size // BLOCK
    begun, inverses = factorize_first(lead, size, range(FIRST_STEPS))
    arrived, begun = lax.optimization_barrier((arrived, begun))

    extended, panel = assemble(received, arrived, front, n_col)
    mine = exchange(panel, "col")[:LEAD_TILES]
    rows = gather(mine, "col")
    turned = lax.ppermute(
        mine, ("row", "col"), [(r * n_col + c, c * n_col + r) for r in range(n_row) for c in range(n_col)]
    )
    turned, begun = lax.optimization_barrier((turned, begun))
    cols = gather(turned, "row")
    *factors, own = factorize_last(begun, inverses, ids, size, range(FIRST_STEPS, steps))
    factor = finish(ids, rows, cols, early, factors, own, extended, front)
    return factor.reshape(1, tile_rows, 1, size, tile_cols, 1, size)


def solution(mesh):
    in_specs = (
        P("front", None, "row", None, None, "col", None),
        P("front", "row", "col", None, None, None),
        P("front", "row", "col", None),
        P("front", "row", "col", None),
        P("front", "row", "col", None),
        P("front", "row", "col"),
    )
    out_specs = P("front", None, "row", None, None, "col", None)
    return jax.shard_map(per_device, mesh=mesh, in_specs=in_specs, out_specs=out_specs, check_vma=False)
```

```python
import jax
import jax.numpy as jnp
from jax import lax
from jax.experimental import pallas as pl
from jax.experimental.pallas import tpu as pltpu
from jax.sharding import PartitionSpec as P


LEAD_TILES = 4
BLOCK = 128
RUN = 32
STRIP = 8
FIRST_STEPS = 6
VMEM_BYTES = 56 * 1024 * 1024


def vmem():
    return pl.BlockSpec(memory_space=pltpu.VMEM)


def smem():
    return pl.BlockSpec(memory_space=pltpu.SMEM)


def hbm():
    return pl.BlockSpec(memory_space=pl.ANY)


def nt(left, right, precision=None):
    return lax.dot_general(
        left, right, (((1,), (1,)), ((), ())), precision=precision, preferred_element_type=jnp.float32
    )


def split(value):
    high = value.astype(jnp.bfloat16)
    return high, (value - high.astype(jnp.float32)).astype(jnp.bfloat16)


def nt3(left, right):
    return nt(left[0], right[0]) + (nt(left[0], right[1]) + nt(left[1], right[0]))


def plan(target_front, target_row, target_col, live_count, n_front, n_row, n_col, tile_cols):
    slots = target_front.shape[0]
    capacity = max(2, -(-slots // (n_front * n_row)))
    buckets = n_front * n_row * capacity

    def kernel(front_ref, row_ref, col_ref, live_ref, targets_ref, bucket_ref, counts):
        def clear(i, carry):
            targets_ref[i] = -1
            return carry

        lax.fori_loop(0, buckets, clear, 0)

        def clear_slots(i, carry):
            bucket_ref[i] = -1
            return carry

        lax.fori_loop(0, slots, clear_slots, 0)

        def clear_counts(i, carry):
            counts[i] = 0
            return carry

        lax.fori_loop(0, n_front * n_row, clear_counts, 0)

        def assign(slot, carry):
            row, col = row_ref[slot], col_ref[slot]
            destination = front_ref[slot] * n_row + lax.rem(row, n_row)
            position = counts[destination]
            counts[destination] = position + 1
            bucket = destination * capacity + position
            targets_ref[bucket] = lax.div(row, n_row) * tile_cols + lax.div(col, n_col)
            bucket_ref[slot] = bucket
            return carry

        lax.fori_loop(0, live_ref[0], assign, 0)

    return pl.pallas_call(
        kernel,
        name="plan",
        out_shape=(jax.ShapeDtypeStruct((buckets,), jnp.int32), jax.ShapeDtypeStruct((slots,), jnp.int32)),
        in_specs=[smem()] * 4,
        out_specs=(smem(), smem()),
        scratch_shapes=[pltpu.SMEM((n_front * n_row,), jnp.int32)],
    )(target_front, target_row, target_col, live_count)


def move(contributions, bucket_of, buckets):
    slots, size, _ = contributions.shape

    def kernel(bucket_ref, tiles_ref, packed_ref, stage, sems_in, sems_out):
        def fetch(slot):
            return pltpu.make_async_copy(tiles_ref.at[slot], stage.at[slot], sems_in.at[slot])

        def store(slot, bucket):
            return pltpu.make_async_copy(stage.at[slot], packed_ref.at[bucket], sems_out.at[slot])

        for slot in range(slots):
            fetch(slot).start()

        def forward(slot, carry):
            fetch(slot).wait()
            bucket = bucket_ref[slot]

            @pl.when(bucket >= 0)
            def _():
                store(slot, bucket).start()

            return carry

        lax.fori_loop(0, slots, forward, 0)

        def drain(slot, carry):
            bucket = bucket_ref[slot]

            @pl.when(bucket >= 0)
            def _():
                store(slot, bucket).wait()

            return carry

        lax.fori_loop(0, slots, drain, 0)

    return pl.pallas_call(
        kernel,
        name="move",
        out_shape=jax.ShapeDtypeStruct((buckets, size, size), contributions.dtype),
        in_specs=[smem(), hbm()],
        out_specs=hbm(),
        scratch_shapes=[
            pltpu.VMEM((slots, size, size), contributions.dtype),
            pltpu.SemaphoreType.DMA((slots,)),
            pltpu.SemaphoreType.DMA((slots,)),
        ],
        compiler_params=pltpu.CompilerParams(vmem_limit_bytes=VMEM_BYTES),
    )(bucket_of, contributions)


SCALE_ROWS = 8
SCALE_STEPS = 64


def encode(values):
    n, m = values.shape
    top = jnp.max(jnp.abs(values), axis=1, keepdims=True)
    code = jnp.floor(jnp.log2(jnp.maximum(top, 2.0**-110)) * SCALE_STEPS) + 1.0
    coded = jnp.round(values * jnp.exp2(15.0 - 1e-3 - code / SCALE_STEPS))
    picked = lax.broadcasted_iota(jnp.int32, (n, m), 0) == lax.broadcasted_iota(jnp.int32, (n, m), 1)
    line = jnp.sum(jnp.where(picked, code, 0.0), axis=0, keepdims=True)
    lines = jnp.broadcast_to(line, (SCALE_ROWS, m))
    return jnp.concatenate([coded, lines], axis=0).astype(jnp.int32).astype(jnp.int16)


def decode(coded):
    wide = coded.astype(jnp.int32).astype(jnp.float32)
    n, m = wide.shape[0] - SCALE_ROWS, wide.shape[1]
    values, line = wide[:n], wide[n : n + 1]
    picked = lax.broadcasted_iota(jnp.int32, (n, m), 0) == lax.broadcasted_iota(jnp.int32, (n, m), 1)
    code = jnp.sum(jnp.where(picked, jnp.broadcast_to(line, (n, m)), 0.0), axis=1, keepdims=True)
    return values * jnp.exp2(code / SCALE_STEPS - 15.0 + 1e-3)


EXTENDED = ((1, 0), (1, 1), (2, 0), (2, 1), (2, 2))


def assemble(received, arrived, front, chunks):
    total, size, _ = received.shape
    thin = front.shape[0] * size // chunks

    def kernel(arrived_ref, received_ref, front_ref, ext_ref, panel_ref, landed, column, sems):
        def copy(i):
            return pltpu.make_async_copy(received_ref.at[i], landed.at[i], sems.at[i])

        def fetch(i, carry):
            @pl.when(arrived_ref[i] >= 0)
            def _():
                copy(i).start()

            return carry

        lax.fori_loop(0, total, fetch, 0)
        for slot, (a, b) in enumerate(EXTENDED):
            ext_ref[slot] = front_ref[a, b].astype(jnp.float32)

        def add(i, carry):
            target = arrived_ref[i]

            @pl.when(target >= 0)
            def _():
                copy(i).wait()
                slot = jnp.where(target >= 6, target - 4, target - 3)
                ext_ref[slot] = ext_ref[slot] + landed[i].astype(jnp.float32)

            return carry

        lax.fori_loop(0, total, add, 0)
        column[0:size] = front_ref[0, 0].astype(jnp.float32)
        column[size : 2 * size] = ext_ref[0]
        column[2 * size : 3 * size] = ext_ref[2]
        for chunk in range(chunks):
            panel_ref[chunk] = encode(column[chunk * thin : (chunk + 1) * thin, :])

    return pl.pallas_call(
        kernel,
        name="assemble",
        out_shape=(
            jax.ShapeDtypeStruct((len(EXTENDED), size, size), jnp.float32),
            jax.ShapeDtypeStruct((chunks, thin + SCALE_ROWS, size), jnp.int16),
        ),
        in_specs=[smem(), hbm(), vmem()],
        out_specs=(vmem(), vmem()),
        scratch_shapes=[
            pltpu.VMEM((total, size, size), jnp.bfloat16),
            pltpu.VMEM((3 * size, size), jnp.float32),
            pltpu.SemaphoreType.DMA((total,)),
        ],
        compiler_params=pltpu.CompilerParams(vmem_limit_bytes=VMEM_BYTES),
    )(arrived, received, front)


def pick_lane(value, lane):
    index = jnp.full(value.shape, lane, jnp.int32)
    return jnp.take_along_axis(value, index, axis=1, mode="promise_in_bounds")


def factor_block(work):
    lanes = lax.broadcasted_iota(jnp.int32, (STRIP, BLOCK), 1)
    strip_rows = lax.broadcasted_iota(jnp.int32, (STRIP, BLOCK), 0)

    def spread(value, i):
        return jnp.broadcast_to(value[i : i + 1, :], value.shape)

    def step(number, top):
        base = pl.multiple_of(number * STRIP, STRIP)
        strip = work[pl.ds(base, STRIP), :]
        own = [pick_lane(strip, base + i) for i in range(STRIP)]
        whole = work[top:BLOCK, :]
        below = lax.broadcasted_iota(jnp.int32, whole.shape, 0) + top >= base + STRIP
        columns = [jnp.where(below, pick_lane(whole, base + i), 0.0) for i in range(STRIP)]
        for i in range(STRIP):
            pivot = spread(own[i], i)
            inverse = 1.0 / pivot
            factors = jnp.where(strip_rows > i, own[i] * inverse, 0.0)
            line = jnp.where(lanes == base + i, pivot + pivot, spread(strip, i))
            strip = strip - factors * line
            lower = columns[i] * jnp.broadcast_to(inverse[0:1], whole.shape)
            for j in range(i + 1, STRIP):
                entry = spread(own[j], i)
                own[j] = own[j] - factors * entry
                columns[j] = columns[j] - lower * jnp.broadcast_to(entry[0:1], whole.shape)
            whole = whole - lower * jnp.broadcast_to(line[0:1], whole.shape)
        work[top:BLOCK, :] = whole
        work[pl.ds(base, STRIP), :] = strip
        return top

    for top in range(0, BLOCK, RUN):
        lax.fori_loop(top // STRIP, (top + RUN) // STRIP, lambda number, carry: step(number, top) * 0 + carry, 0)


HIGHEST = lax.Precision.HIGHEST


def eliminate(full, inverses, work, blocks):
    order = full.shape[0]
    r = lax.broadcasted_iota(jnp.int32, (BLOCK, BLOCK), 0)
    c = lax.broadcasted_iota(jnp.int32, (BLOCK, BLOCK), 1)
    for k in blocks:
        s, e = k * BLOCK, (k + 1) * BLOCK
        work[...] = full[s:e, s:e]
        factor_block(work)
        done = work[...]
        diagonal = jnp.where(r == c, done, 0.0)
        root = lax.rsqrt(jnp.sum(diagonal, axis=1, keepdims=True))
        inverse = jnp.where(r >= c, done, 0.0) * root * (1.0 / jnp.sum(diagonal, axis=0, keepdims=True))
        inverses[k] = inverse
        full[s:e, s:e] = (jnp.where(r <= c, done, 0.0) * root).T
        if e < order:
            panel = nt(full[e:order, s:e], inverse, HIGHEST)
            full[e:order, s:e] = panel
            for o in range(e, order, BLOCK):
                full[o:order, o : o + BLOCK] = full[o:order, o : o + BLOCK] - nt(
                    panel[o - e :], panel[o - e : o - e + BLOCK], HIGHEST
                )


PAIRS = tuple((i, j) for i in range(LEAD_TILES) for j in range(i + 1))


def factorize_first(ids, lead, size, blocks):
    order = LEAD_TILES * size

    def kernel(place_ref, *refs):
        *pieces, full, inverses, work = refs
        for ref, inner, chunk in pair_pieces(pieces, place_ref[1]):
            for number, (i, j) in enumerate(PAIRS):
                tile = ref[inner, number].astype(jnp.float32)
                thin = tile.shape[0]
                start = pl.multiple_of(i * size + chunk * thin, thin)
                full[pl.ds(start, thin), j * size : (j + 1) * size] = tile
        eliminate(full, inverses, work, blocks)

    return pl.pallas_call(
        kernel,
        name="factorize_first",
        out_shape=(
            jax.ShapeDtypeStruct((order, order), jnp.float32),
            jax.ShapeDtypeStruct((order // BLOCK, BLOCK, BLOCK), jnp.float32),
        ),
        in_specs=[smem()] + [vmem()] * len(lead),
        out_specs=(vmem(),) * 2,
        scratch_shapes=[pltpu.VMEM((BLOCK, BLOCK), jnp.float32)],
        compiler_params=pltpu.CompilerParams(vmem_limit_bytes=VMEM_BYTES),
    )(ids, *lead)


def factorize_last(begun, begun_inverses, ids, size, blocks):
    order = LEAD_TILES * size

    def kernel(ids_ref, begun_ref, begun_inv_ref, high_ref, low_ref, inv_high_ref, inv_low_ref, own_ref, full, inverses, work):
        full[...] = begun_ref[...]
        inverses[...] = begun_inv_ref[...]
        eliminate(full, inverses, work, blocks)
        half = size // BLOCK
        for q in range(LEAD_TILES):
            s = q * size
            full[s : s + BLOCK, s + BLOCK : s + size] = jnp.zeros((BLOCK, size - BLOCK), jnp.float32)
            first, second = inverses[q * half], inverses[q * half + 1]
            corner = -jnp.dot(
                second,
                jnp.dot(
                    full[s + BLOCK : s + size, s : s + BLOCK], first,
                    precision=HIGHEST, preferred_element_type=jnp.float32,
                ),
                precision=HIGHEST, preferred_element_type=jnp.float32,
            )
            for (y, x, part) in ((0, 0, first), (0, 1, jnp.zeros_like(first)), (1, 0, corner), (1, 1, second)):
                high, low = split(part)
                inv_high_ref[q, y * BLOCK : (y + 1) * BLOCK, x * BLOCK : (x + 1) * BLOCK] = high
                inv_low_ref[q, y * BLOCK : (y + 1) * BLOCK, x * BLOCK : (x + 1) * BLOCK] = low
        for i, j in PAIRS:
            tile = full[i * size : (i + 1) * size, j * size : (j + 1) * size]
            high, low = split(tile)
            high_ref[i * size : (i + 1) * size, j * size : (j + 1) * size] = high
            low_ref[i * size : (i + 1) * size, j * size : (j + 1) * size] = low

            @pl.when((ids_ref[0] == i) & (ids_ref[1] == j))
            def _():
                own_ref[...] = tile

    wide = jax.ShapeDtypeStruct((order, order), jnp.bfloat16)
    inv = jax.ShapeDtypeStruct((LEAD_TILES, size, size), jnp.bfloat16)
    return pl.pallas_call(
        kernel,
        name="factorize_last",
        out_shape=(wide, wide, inv, inv, jax.ShapeDtypeStruct((size, size), jnp.float32)),
        in_specs=[smem(), vmem(), vmem()],
        out_specs=(vmem(),) * 5,
        scratch_shapes=[
            pltpu.VMEM((order, order), jnp.float32),
            pltpu.VMEM((order // BLOCK, BLOCK, BLOCK), jnp.float32),
            pltpu.VMEM((BLOCK, BLOCK), jnp.float32),
        ],
        compiler_params=pltpu.CompilerParams(vmem_limit_bytes=VMEM_BYTES),
    )(ids, begun, begun_inverses)


def solve(panel, factors):
    _, coded_rows, size = panel.shape
    thin, order = coded_rows - SCALE_ROWS, LEAD_TILES * size

    def kernel(panel_ref, high_ref, low_ref, ih_ref, il_ref, out_ref, xh, xl):
        for q in range(LEAD_TILES):
            s, e = q * size, (q + 1) * size
            acc = decode(panel_ref[q])
            if q:
                acc = acc - nt3((xh[:, 0:s], xl[:, 0:s]), (high_ref[s:e, 0:s], low_ref[s:e, 0:s]))
            x = nt3(split(acc), (ih_ref[q], il_ref[q]))
            xh[:, s:e], xl[:, s:e] = split(x)
            out_ref[q] = encode(x)

    return pl.pallas_call(
        kernel,
        name="solve",
        out_shape=jax.ShapeDtypeStruct((LEAD_TILES, coded_rows, size), jnp.int16),
        in_specs=[vmem()] * 5,
        out_specs=vmem(),
        scratch_shapes=[pltpu.VMEM((thin, order), jnp.bfloat16)] * 2,
        compiler_params=pltpu.CompilerParams(vmem_limit_bytes=VMEM_BYTES),
    )(panel, *factors)


def finish(ids, rows, cols, own, extended, front):
    size = own.shape[0]
    order = LEAD_TILES * size
    tile_rows, tile_cols = front.shape[:2]
    lanes = 128
    parts = size // lanes
    half = len(rows)

    def kernel(ids_ref, *refs):
        row_pieces, col_pieces = refs[:half], refs[half : 2 * half]
        own_ref, ext_ref, front_ref, out_ref, xh, xl = refs[2 * half :]
        row, col = ids_ref[0], ids_ref[1]

        def put(a, b, tile):
            for part in range(parts):
                start = (a * size * tile_cols + b) * parts + part
                out_ref[pl.ds(start, size, stride=tile_cols * parts), :] = tile[:, part * lanes : (part + 1) * lanes]

        for pieces, place, first in ((row_pieces, col, 0), (col_pieces, row, tile_rows * size)):
            for ref, inner, chunk in pair_pieces(pieces, place):
                for q in range(LEAD_TILES):
                    value = decode(ref[inner, q])
                    thin = value.shape[0]
                    start = pl.multiple_of(first + chunk * thin, 32)
                    high, low = split(value)
                    xh[pl.ds(start, thin), q * size : (q + 1) * size] = high
                    xl[pl.ds(start, thin), q * size : (q + 1) * size] = low

        def take(ref, n):
            return ref[n * size : (n + 1) * size, :]

        def update(a, b, base):
            x, y = a, tile_rows + b
            put(a, b, base - nt3((take(xh, x), take(xl, x)), (take(xh, y), take(xl, y))))

        def put_panel(a):
            for q in range(LEAD_TILES):

                @pl.when(col == q)
                def _():
                    high = xh[a * size : (a + 1) * size, q * size : (q + 1) * size].astype(jnp.float32)
                    low = xl[a * size : (a + 1) * size, q * size : (q + 1) * size].astype(jnp.float32)
                    put(a, 0, high + low)

        zero = jnp.zeros((size, size), jnp.float32)
        for a, b in ((0, 1), (0, 2), (1, 2)):
            put(a, b, zero)
        in_panel = col < LEAD_TILES
        lead_row = row < LEAD_TILES
        put_panel(1)
        put_panel(2)

        @pl.when(jnp.logical_not(in_panel))
        def _():
            update(1, 0, ext_ref[0])
            update(2, 0, ext_ref[2])

        @pl.when(row < col)
        def _():
            put(0, 0, zero)
            put(1, 1, zero)
            put(2, 2, zero)

        @pl.when(row >= col)
        def _():
            @pl.when(lead_row)
            def _():
                put(0, 0, own_ref[...])

            @pl.when(jnp.logical_not(lead_row))
            def _():
                put_panel(0)

            @pl.when(jnp.logical_not(in_panel))
            def _():
                update(0, 0, front_ref[0, 0].astype(jnp.float32))

            update(1, 1, ext_ref[1])
            update(2, 2, ext_ref[4])

        update(2, 1, ext_ref[3])

    return pl.pallas_call(
        kernel,
        name="finish",
        out_shape=jax.ShapeDtypeStruct((tile_rows * size * tile_cols * parts, lanes), jnp.float32),
        in_specs=[smem()] + [vmem()] * (2 * half + 3),
        out_specs=vmem(),
        scratch_shapes=[pltpu.VMEM((2 * tile_rows * size, order), jnp.bfloat16)] * 2,
        compiler_params=pltpu.CompilerParams(vmem_limit_bytes=VMEM_BYTES),
    )(ids, *rows, *cols, own, extended, front)


SHIFTS = (1, 3, 2)


def exchange(value, axis):
    return lax.all_to_all(value, axis, split_axis=0, concat_axis=0, tiled=True)


def permute(value, axis, target):
    return lax.ppermute(value, axis, [(i, target(i)) for i in range(lax.axis_size(axis))])


def pair_gather(value, axis):
    ring = lax.axis_size(axis) // 2
    partner = permute(value, axis, lambda i: i ^ 1)
    pair = jnp.stack([value, partner])
    shifted = [permute(pair, axis, lambda i: (i // 2 + shift) % ring * 2 + i % 2) for shift in SHIFTS]
    return (pair, *shifted)


def pair_pieces(pieces, place):
    ring = len(SHIFTS) + 1
    for ref, shift in zip(pieces, (0,) + SHIFTS, strict=True):
        source = lax.rem(lax.div(place, 2) + (ring - shift), ring) * 2
        side = lax.rem(place, 2)
        yield ref, 0, source + side
        yield ref, 1, source + 1 - side


def per_device(front_matrix, contributions, target_front, target_row, target_col, live_count):
    _, tile_rows, _, size, tile_cols, _, _ = front_matrix.shape
    n_front, n_row, n_col = (lax.axis_size(name) for name in ("front", "row", "col"))
    slots = contributions.shape[3]
    front = front_matrix.reshape(tile_rows, size, tile_cols, size).transpose(0, 2, 1, 3)
    ids = jnp.stack([lax.axis_index("row"), lax.axis_index("col")]).astype(jnp.int32)

    thin = size // n_col
    chunk = exchange(front[0, 0].reshape(n_col, thin, size), "col")[:LEAD_TILES]

    targets, bucket_of = plan(
        target_front.reshape(slots), target_row.reshape(slots), target_col.reshape(slots),
        live_count.reshape(1), n_front, n_row, n_col, tile_cols,
    )
    packed = move(contributions.reshape(slots, size, size), bucket_of, targets.shape[0])
    received = exchange(packed, ("front", "row"))

    capacity = targets.shape[0] // (n_front * n_row)
    other = permute(targets, "front", lambda i: 1 - i)
    front_index = lax.axis_index("front")
    by_source = [jnp.where(front_index == source, targets, other) for source in range(n_front)]
    aimed = lax.dynamic_index_in_dim(
        jnp.stack(by_source).reshape(n_front, n_front, n_row, capacity), front_index, axis=1, keepdims=False
    )
    notes = aimed.transpose(1, 0, 2).reshape(n_row, 1, n_front * capacity).astype(jnp.bfloat16)
    notes = jnp.pad(notes, ((0, 0), (0, 7), (0, size - n_front * capacity)))
    flat = chunk.reshape(LEAD_TILES * thin, size)
    sent = jnp.concatenate([jnp.broadcast_to(flat[None], (n_row,) + flat.shape), notes], axis=1)
    got = exchange(sent, "row")
    leading = got[:, : LEAD_TILES * thin].reshape(n_row, LEAD_TILES, thin, size)
    arrived = got[:, LEAD_TILES * thin, : n_front * capacity].astype(jnp.int32)
    arrived = arrived.reshape(n_row, n_front, capacity).transpose(1, 0, 2).reshape(targets.shape)

    lower = jnp.concatenate([leading[i, : i + 1] for i in range(LEAD_TILES)], axis=0)
    lead = pair_gather(lower, "col")
    steps = LEAD_TILES * size // BLOCK
    begun, inverses = factorize_first(ids, lead, size, range(FIRST_STEPS))
    arrived, begun = lax.optimization_barrier((arrived, begun))

    extended, panel = assemble(received, arrived, front, n_col)
    mine = exchange(panel, "col")
    *factors, own = factorize_last(begun, inverses, ids, size, range(FIRST_STEPS, steps))
    solved = solve(mine, factors)
    turned = lax.ppermute(
        solved, ("row", "col"), [(r * n_col + c, c * n_col + r) for r in range(n_row) for c in range(n_col)]
    )
    rows = pair_gather(solved, "col")
    cols = pair_gather(turned, "row")
    factor = finish(ids, rows, cols, own, extended, front)
    return factor.reshape(1, tile_rows, 1, size, tile_cols, 1, size)


def solution(mesh):
    in_specs = (
        P("front", None, "row", None, None, "col", None),
        P("front", "row", "col", None, None, None),
        P("front", "row", "col", None),
        P("front", "row", "col", None),
        P("front", "row", "col", None),
        P("front", "row", "col"),
    )
    out_specs = P("front", None, "row", None, None, "col", None)
    return jax.shard_map(per_device, mesh=mesh, in_specs=in_specs, out_specs=out_specs, check_vma=False)
```

```python
import jax
import jax.numpy as jnp
from jax import lax
from jax.experimental import pallas as pl
from jax.experimental.pallas import tpu as pltpu
from jax.sharding import PartitionSpec as P


LEAD_TILES = 4
BLOCK = 128
HALF = 64
RUN = 32
STRIP = 8
FIRST_STEPS = 7
VMEM_BYTES = 56 * 1024 * 1024


def vmem():
    return pl.BlockSpec(memory_space=pltpu.VMEM)


def smem():
    return pl.BlockSpec(memory_space=pltpu.SMEM)


def hbm():
    return pl.BlockSpec(memory_space=pl.ANY)


def nt(left, right, precision=None):
    return lax.dot_general(
        left, right, (((1,), (1,)), ((), ())), precision=precision, preferred_element_type=jnp.float32
    )


def split(value):
    high = value.astype(jnp.bfloat16)
    return high, (value - high.astype(jnp.float32)).astype(jnp.bfloat16)


def nt3(left, right):
    return nt(left[0], right[0]) + (nt(left[0], right[1]) + nt(left[1], right[0]))


def plan(target_front, target_row, target_col, live_count, n_front, n_row, n_col, tile_cols):
    slots = target_front.shape[0]
    capacity = max(2, -(-slots // (n_front * n_row)))
    buckets = n_front * n_row * capacity

    def kernel(front_ref, row_ref, col_ref, live_ref, targets_ref, bucket_ref, counts):
        def clear(i, carry):
            targets_ref[i] = -1
            return carry

        lax.fori_loop(0, buckets, clear, 0)

        def clear_slots(i, carry):
            bucket_ref[i] = -1
            return carry

        lax.fori_loop(0, slots, clear_slots, 0)

        def clear_counts(i, carry):
            counts[i] = 0
            return carry

        lax.fori_loop(0, n_front * n_row, clear_counts, 0)

        def assign(slot, carry):
            row, col = row_ref[slot], col_ref[slot]
            destination = front_ref[slot] * n_row + lax.rem(row, n_row)
            position = counts[destination]
            counts[destination] = position + 1
            bucket = destination * capacity + position
            targets_ref[bucket] = lax.div(row, n_row) * tile_cols + lax.div(col, n_col)
            bucket_ref[slot] = bucket
            return carry

        lax.fori_loop(0, live_ref[0], assign, 0)

    return pl.pallas_call(
        kernel,
        name="plan",
        out_shape=(jax.ShapeDtypeStruct((buckets,), jnp.int32), jax.ShapeDtypeStruct((slots,), jnp.int32)),
        in_specs=[smem()] * 4,
        out_specs=(smem(), smem()),
        scratch_shapes=[pltpu.SMEM((n_front * n_row,), jnp.int32)],
    )(target_front, target_row, target_col, live_count)


def move(contributions, bucket_of, buckets):
    slots, size, _ = contributions.shape

    def kernel(bucket_ref, tiles_ref, packed_ref, stage, sems_in, sems_out):
        def fetch(slot):
            return pltpu.make_async_copy(tiles_ref.at[slot], stage.at[slot], sems_in.at[slot])

        def store(slot, bucket):
            return pltpu.make_async_copy(stage.at[slot], packed_ref.at[bucket], sems_out.at[slot])

        for slot in range(slots):
            fetch(slot).start()

        def forward(slot, carry):
            fetch(slot).wait()
            bucket = bucket_ref[slot]

            @pl.when(bucket >= 0)
            def _():
                store(slot, bucket).start()

            return carry

        lax.fori_loop(0, slots, forward, 0)

        def drain(slot, carry):
            bucket = bucket_ref[slot]

            @pl.when(bucket >= 0)
            def _():
                store(slot, bucket).wait()

            return carry

        lax.fori_loop(0, slots, drain, 0)

    return pl.pallas_call(
        kernel,
        name="move",
        out_shape=jax.ShapeDtypeStruct((buckets, size, size), contributions.dtype),
        in_specs=[smem(), hbm()],
        out_specs=hbm(),
        scratch_shapes=[
            pltpu.VMEM((slots, size, size), contributions.dtype),
            pltpu.SemaphoreType.DMA((slots,)),
            pltpu.SemaphoreType.DMA((slots,)),
        ],
        compiler_params=pltpu.CompilerParams(vmem_limit_bytes=VMEM_BYTES),
    )(bucket_of, contributions)


SCALE_ROWS = 8
SCALE_STEPS = 64


def encode(values):
    n, m = values.shape
    top = jnp.max(jnp.abs(values), axis=1, keepdims=True)
    code = jnp.floor(jnp.log2(jnp.maximum(top, 2.0**-110)) * SCALE_STEPS) + 1.0
    coded = jnp.round(values * jnp.exp2(15.0 - 1e-3 - code / SCALE_STEPS))
    picked = lax.broadcasted_iota(jnp.int32, (n, m), 0) == lax.broadcasted_iota(jnp.int32, (n, m), 1)
    line = jnp.sum(jnp.where(picked, code, 0.0), axis=0, keepdims=True)
    lines = jnp.broadcast_to(line, (SCALE_ROWS, m))
    return jnp.concatenate([coded, lines], axis=0).astype(jnp.int32).astype(jnp.int16)


def decode(coded):
    wide = coded.astype(jnp.int32).astype(jnp.float32)
    n, m = wide.shape[0] - SCALE_ROWS, wide.shape[1]
    values, line = wide[:n], wide[n : n + 1]
    picked = lax.broadcasted_iota(jnp.int32, (n, m), 0) == lax.broadcasted_iota(jnp.int32, (n, m), 1)
    code = jnp.sum(jnp.where(picked, jnp.broadcast_to(line, (n, m)), 0.0), axis=1, keepdims=True)
    return values * jnp.exp2(code / SCALE_STEPS - 15.0 + 1e-3)


EXTENDED = ((1, 0), (1, 1), (2, 0), (2, 1), (2, 2))


def assemble(received, arrived, front, chunks):
    total, size, _ = received.shape
    thin = front.shape[0] * size // chunks

    def kernel(arrived_ref, received_ref, front_ref, ext_ref, panel_ref, landed, column, sems):
        def copy(i):
            return pltpu.make_async_copy(received_ref.at[i], landed.at[i], sems.at[i])

        def fetch(i, carry):
            @pl.when(arrived_ref[i] >= 0)
            def _():
                copy(i).start()

            return carry

        lax.fori_loop(0, total, fetch, 0)
        for slot, (a, b) in enumerate(EXTENDED):
            ext_ref[slot] = front_ref[a, b].astype(jnp.float32)

        def add(i, carry):
            target = arrived_ref[i]

            @pl.when(target >= 0)
            def _():
                copy(i).wait()
                slot = jnp.where(target >= 6, target - 4, target - 3)
                ext_ref[slot] = ext_ref[slot] + landed[i].astype(jnp.float32)

            return carry

        lax.fori_loop(0, total, add, 0)
        column[0:size] = front_ref[0, 0].astype(jnp.float32)
        column[size : 2 * size] = ext_ref[0]
        column[2 * size : 3 * size] = ext_ref[2]
        for chunk in range(chunks):
            panel_ref[chunk] = encode(column[chunk * thin : (chunk + 1) * thin, :])

    return pl.pallas_call(
        kernel,
        name="assemble",
        out_shape=(
            jax.ShapeDtypeStruct((len(EXTENDED), size, size), jnp.float32),
            jax.ShapeDtypeStruct((chunks, thin + SCALE_ROWS, size), jnp.int16),
        ),
        in_specs=[smem(), hbm(), vmem()],
        out_specs=(vmem(), vmem()),
        scratch_shapes=[
            pltpu.VMEM((total, size, size), jnp.bfloat16),
            pltpu.VMEM((3 * size, size), jnp.float32),
            pltpu.SemaphoreType.DMA((total,)),
        ],
        compiler_params=pltpu.CompilerParams(vmem_limit_bytes=VMEM_BYTES),
    )(arrived, received, front)


def pick_lane(value, lane):
    index = jnp.full(value.shape, lane, jnp.int32)
    return jnp.take_along_axis(value, index, axis=1, mode="promise_in_bounds")


def factor_block(work):
    lanes = lax.broadcasted_iota(jnp.int32, (STRIP, BLOCK), 1)
    strip_rows = lax.broadcasted_iota(jnp.int32, (STRIP, BLOCK), 0)

    def spread(value, i):
        return jnp.broadcast_to(value[i : i + 1, :], value.shape)

    def step(number, top, bottom):
        base = pl.multiple_of(number * STRIP, STRIP)
        strip = work[pl.ds(base, STRIP), :]
        own = [pick_lane(strip, base + i) for i in range(STRIP)]
        whole = work[top:bottom, :]
        below = lax.broadcasted_iota(jnp.int32, whole.shape, 0) + top >= base + STRIP
        columns = [jnp.where(below, pick_lane(whole, base + i), 0.0) for i in range(STRIP)]
        for i in range(STRIP):
            pivot = spread(own[i], i)
            inverse = 1.0 / pivot
            factors = jnp.where(strip_rows > i, own[i] * inverse, 0.0)
            line = jnp.where(lanes == base + i, pivot + pivot, spread(strip, i))
            strip = strip - factors * line
            lower = columns[i] * jnp.broadcast_to(inverse[0:1], whole.shape)
            for j in range(i + 1, STRIP):
                entry = spread(own[j], i)
                own[j] = own[j] - factors * entry
                columns[j] = columns[j] - lower * jnp.broadcast_to(entry[0:1], whole.shape)
            whole = whole - lower * jnp.broadcast_to(line[0:1], whole.shape)
        work[top:bottom, :] = whole
        work[pl.ds(base, STRIP), :] = strip

    for first in range(0, BLOCK, HALF):
        last = first + HALF
        for top in range(first, last, RUN):

            def run(number, carry, top=top):
                step(number, top, last)
                return carry

            lax.fori_loop(top // STRIP, (top + RUN) // STRIP, run, 0)
        if last < BLOCK:
            done = work[first:last, :]
            at_pivot = lax.broadcasted_iota(jnp.int32, done.shape, 0) + first == lax.broadcasted_iota(
                jnp.int32, done.shape, 1
            )
            pivots = jnp.where(at_pivot, done, 0.0)
            scaled = done / jnp.sum(pivots, axis=1, keepdims=True)
            change = lax.dot_general(
                scaled, done + pivots, (((0,), (0,)), ((), ())),
                precision=lax.Precision.HIGHEST, preferred_element_type=jnp.float32,
            )
            work[last:BLOCK, :] = work[last:BLOCK, :] - change[last:BLOCK, :]


HIGHEST = lax.Precision.HIGHEST


def eliminate(full, inverses, work, blocks):
    order = full.shape[0]
    r = lax.broadcasted_iota(jnp.int32, (BLOCK, BLOCK), 0)
    c = lax.broadcasted_iota(jnp.int32, (BLOCK, BLOCK), 1)
    for k in blocks:
        s, e = k * BLOCK, (k + 1) * BLOCK
        work[...] = full[s:e, s:e]
        factor_block(work)
        done = work[...]
        diagonal = jnp.where(r == c, done, 0.0)
        root = lax.rsqrt(jnp.sum(diagonal, axis=1, keepdims=True))
        inverse = jnp.where(r >= c, done, 0.0) * root * (1.0 / jnp.sum(diagonal, axis=0, keepdims=True))
        inverses[k] = inverse
        full[s:e, s:e] = (jnp.where(r <= c, done, 0.0) * root).T
        if e < order:
            panel = nt(full[e:order, s:e], inverse, HIGHEST)
            full[e:order, s:e] = panel
            for o in range(e, order, BLOCK):
                full[o:order, o : o + BLOCK] = full[o:order, o : o + BLOCK] - nt(
                    panel[o - e :], panel[o - e : o - e + BLOCK], HIGHEST
                )


PAIRS = tuple((i, j) for i in range(LEAD_TILES) for j in range(i + 1))


def factorize_first(ids, lead, size, blocks):
    order = LEAD_TILES * size

    def kernel(place_ref, *refs):
        *pieces, full, inverses, work = refs
        for ref, inner, chunk in pair_pieces(pieces, place_ref[1]):
            for number, (i, j) in enumerate(PAIRS):
                tile = ref[inner, number].astype(jnp.float32)
                thin = tile.shape[0]
                start = pl.multiple_of(i * size + chunk * thin, thin)
                full[pl.ds(start, thin), j * size : (j + 1) * size] = tile
        eliminate(full, inverses, work, blocks)

    return pl.pallas_call(
        kernel,
        name="factorize_first",
        out_shape=(
            jax.ShapeDtypeStruct((order, order), jnp.float32),
            jax.ShapeDtypeStruct((order // BLOCK, BLOCK, BLOCK), jnp.float32),
        ),
        in_specs=[smem()] + [vmem()] * len(lead),
        out_specs=(vmem(),) * 2,
        scratch_shapes=[pltpu.VMEM((BLOCK, BLOCK), jnp.float32)],
        compiler_params=pltpu.CompilerParams(vmem_limit_bytes=VMEM_BYTES),
    )(ids, *lead)


def factorize_last(begun, begun_inverses, ids, size, blocks):
    order = LEAD_TILES * size

    def kernel(ids_ref, begun_ref, begun_inv_ref, high_ref, low_ref, inv_high_ref, inv_low_ref, own_ref, full, inverses, work):
        full[...] = begun_ref[...]
        inverses[...] = begun_inv_ref[...]
        eliminate(full, inverses, work, blocks)
        half = size // BLOCK
        for q in range(LEAD_TILES):
            s = q * size
            full[s : s + BLOCK, s + BLOCK : s + size] = jnp.zeros((BLOCK, size - BLOCK), jnp.float32)
            first, second = inverses[q * half], inverses[q * half + 1]
            corner = -jnp.dot(
                second,
                jnp.dot(
                    full[s + BLOCK : s + size, s : s + BLOCK], first,
                    precision=HIGHEST, preferred_element_type=jnp.float32,
                ),
                precision=HIGHEST, preferred_element_type=jnp.float32,
            )
            for (y, x, part) in ((0, 0, first), (0, 1, jnp.zeros_like(first)), (1, 0, corner), (1, 1, second)):
                high, low = split(part)
                inv_high_ref[q, y * BLOCK : (y + 1) * BLOCK, x * BLOCK : (x + 1) * BLOCK] = high
                inv_low_ref[q, y * BLOCK : (y + 1) * BLOCK, x * BLOCK : (x + 1) * BLOCK] = low
        for i, j in PAIRS:
            tile = full[i * size : (i + 1) * size, j * size : (j + 1) * size]
            high, low = split(tile)
            high_ref[i * size : (i + 1) * size, j * size : (j + 1) * size] = high
            low_ref[i * size : (i + 1) * size, j * size : (j + 1) * size] = low

            @pl.when((ids_ref[0] == i) & (ids_ref[1] == j))
            def _():
                own_ref[...] = tile

    wide = jax.ShapeDtypeStruct((order, order), jnp.bfloat16)
    inv = jax.ShapeDtypeStruct((LEAD_TILES, size, size), jnp.bfloat16)
    return pl.pallas_call(
        kernel,
        name="factorize_last",
        out_shape=(wide, wide, inv, inv, jax.ShapeDtypeStruct((size, size), jnp.float32)),
        in_specs=[smem(), vmem(), vmem()],
        out_specs=(vmem(),) * 5,
        scratch_shapes=[
            pltpu.VMEM((order, order), jnp.float32),
            pltpu.VMEM((order // BLOCK, BLOCK, BLOCK), jnp.float32),
            pltpu.VMEM((BLOCK, BLOCK), jnp.float32),
        ],
        compiler_params=pltpu.CompilerParams(vmem_limit_bytes=VMEM_BYTES),
    )(ids, begun, begun_inverses)


def solve(panels, factors):
    _, coded_rows, size = panels[0].shape
    thin, order = coded_rows - SCALE_ROWS, LEAD_TILES * size
    count = len(panels)

    def kernel(*refs):
        panel_refs, (high_ref, low_ref, ih_ref, il_ref) = refs[:count], refs[count : count + 4]
        *out_refs, xh, xl = refs[count + 4 :]
        for q in range(LEAD_TILES):
            s, e = q * size, (q + 1) * size
            acc = jnp.concatenate([decode(ref[q]) for ref in panel_refs], axis=0)
            if q:
                acc = acc - nt3((xh[:, 0:s], xl[:, 0:s]), (high_ref[s:e, 0:s], low_ref[s:e, 0:s]))
            x = nt3(split(acc), (ih_ref[q], il_ref[q]))
            xh[:, s:e], xl[:, s:e] = split(x)
            for number, ref in enumerate(out_refs):
                ref[q] = encode(x[number * thin : (number + 1) * thin])

    return pl.pallas_call(
        kernel,
        name="solve",
        out_shape=(jax.ShapeDtypeStruct((LEAD_TILES, coded_rows, size), jnp.int16),) * count,
        in_specs=[vmem()] * (count + 4),
        out_specs=(vmem(),) * count,
        scratch_shapes=[pltpu.VMEM((count * thin, order), jnp.bfloat16)] * 2,
        compiler_params=pltpu.CompilerParams(vmem_limit_bytes=VMEM_BYTES),
    )(*panels, *factors)


def finish(ids, rows, cols, own, extended, front):
    size = own.shape[0]
    order = LEAD_TILES * size
    tile_rows, tile_cols = front.shape[:2]
    lanes = 128
    parts = size // lanes
    half = len(rows)

    def kernel(ids_ref, *refs):
        row_pieces, col_pieces = refs[:half], refs[half : 2 * half]
        own_ref, ext_ref, front_ref, out_ref, xh, xl = refs[2 * half :]
        row, col = ids_ref[0], ids_ref[1]

        def put(a, b, tile):
            for part in range(parts):
                start = (a * size * tile_cols + b) * parts + part
                out_ref[pl.ds(start, size, stride=tile_cols * parts), :] = tile[:, part * lanes : (part + 1) * lanes]

        for pieces, place, first in ((row_pieces, col, 0), (col_pieces, row, tile_rows * size)):
            for ref, inner, chunk in pair_pieces(pieces, place):
                for q in range(LEAD_TILES):
                    value = decode(ref[inner, q])
                    thin = value.shape[0]
                    start = pl.multiple_of(first + chunk * thin, 32)
                    high, low = split(value)
                    xh[pl.ds(start, thin), q * size : (q + 1) * size] = high
                    xl[pl.ds(start, thin), q * size : (q + 1) * size] = low

        def take(ref, n):
            return ref[n * size : (n + 1) * size, :]

        def update(a, b, base):
            x, y = a, tile_rows + b
            put(a, b, base - nt3((take(xh, x), take(xl, x)), (take(xh, y), take(xl, y))))

        def put_panel(a):
            for q in range(LEAD_TILES):

                @pl.when(col == q)
                def _():
                    high = xh[a * size : (a + 1) * size, q * size : (q + 1) * size].astype(jnp.float32)
                    low = xl[a * size : (a + 1) * size, q * size : (q + 1) * size].astype(jnp.float32)
                    put(a, 0, high + low)

        zero = jnp.zeros((size, size), jnp.float32)
        for a, b in ((0, 1), (0, 2), (1, 2)):
            put(a, b, zero)
        in_panel = col < LEAD_TILES
        lead_row = row < LEAD_TILES
        put_panel(1)
        put_panel(2)

        @pl.when(jnp.logical_not(in_panel))
        def _():
            update(1, 0, ext_ref[0])
            update(2, 0, ext_ref[2])

        @pl.when(row < col)
        def _():
            put(0, 0, zero)
            put(1, 1, zero)
            put(2, 2, zero)

        @pl.when(row >= col)
        def _():
            @pl.when(lead_row)
            def _():
                put(0, 0, own_ref[...])

            @pl.when(jnp.logical_not(lead_row))
            def _():
                put_panel(0)

            @pl.when(jnp.logical_not(in_panel))
            def _():
                update(0, 0, front_ref[0, 0].astype(jnp.float32))

            update(1, 1, ext_ref[1])
            update(2, 2, ext_ref[4])

        update(2, 1, ext_ref[3])

    return pl.pallas_call(
        kernel,
        name="finish",
        out_shape=jax.ShapeDtypeStruct((tile_rows * size * tile_cols * parts, lanes), jnp.float32),
        in_specs=[smem()] + [vmem()] * (2 * half + 3),
        out_specs=vmem(),
        scratch_shapes=[pltpu.VMEM((2 * tile_rows * size, order), jnp.bfloat16)] * 2,
        compiler_params=pltpu.CompilerParams(vmem_limit_bytes=VMEM_BYTES),
    )(ids, *rows, *cols, own, extended, front)


SHIFTS = (1, 3, 2)


def exchange(value, axis):
    return lax.all_to_all(value, axis, split_axis=0, concat_axis=0, tiled=True)


def permute(value, axis, target):
    return lax.ppermute(value, axis, [(i, target(i)) for i in range(lax.axis_size(axis))])


def pair_gather(value, axis):
    ring = lax.axis_size(axis) // 2
    partner = permute(value, axis, lambda i: i ^ 1)
    pair = jnp.stack([value, partner])
    shifted = [permute(pair, axis, lambda i: (i // 2 + shift) % ring * 2 + i % 2) for shift in SHIFTS]
    return (pair, *shifted)


def pair_pieces(pieces, place):
    ring = len(SHIFTS) + 1
    for ref, shift in zip(pieces, (0,) + SHIFTS, strict=True):
        source = lax.rem(lax.div(place, 2) + (ring - shift), ring) * 2
        side = lax.rem(place, 2)
        yield ref, 0, source + side
        yield ref, 1, source + 1 - side


def per_device(front_matrix, contributions, target_front, target_row, target_col, live_count):
    _, tile_rows, _, size, tile_cols, _, _ = front_matrix.shape
    n_front, n_row, n_col = (lax.axis_size(name) for name in ("front", "row", "col"))
    slots = contributions.shape[3]
    front = front_matrix.reshape(tile_rows, size, tile_cols, size).transpose(0, 2, 1, 3)
    ids = jnp.stack([lax.axis_index("row"), lax.axis_index("col")]).astype(jnp.int32)

    thin = size // n_col
    chunk = exchange(front[0, 0].reshape(n_col, thin, size), "col")[:LEAD_TILES]

    targets, bucket_of = plan(
        target_front.reshape(slots), target_row.reshape(slots), target_col.reshape(slots),
        live_count.reshape(1), n_front, n_row, n_col, tile_cols,
    )
    packed = move(contributions.reshape(slots, size, size), bucket_of, targets.shape[0])
    received = exchange(packed, ("front", "row"))

    capacity = targets.shape[0] // (n_front * n_row)
    other = permute(targets, "front", lambda i: 1 - i)
    front_index = lax.axis_index("front")
    by_source = [jnp.where(front_index == source, targets, other) for source in range(n_front)]
    aimed = lax.dynamic_index_in_dim(
        jnp.stack(by_source).reshape(n_front, n_front, n_row, capacity), front_index, axis=1, keepdims=False
    )
    notes = aimed.transpose(1, 0, 2).reshape(n_row, 1, n_front * capacity).astype(jnp.bfloat16)
    notes = jnp.pad(notes, ((0, 0), (0, 7), (0, size - n_front * capacity)))
    flat = chunk.reshape(LEAD_TILES * thin, size)
    sent = jnp.concatenate([jnp.broadcast_to(flat[None], (n_row,) + flat.shape), notes], axis=1)
    got = exchange(sent, "row")
    leading = got[:, : LEAD_TILES * thin].reshape(n_row, LEAD_TILES, thin, size)
    arrived = got[:, LEAD_TILES * thin, : n_front * capacity].astype(jnp.int32)
    arrived = arrived.reshape(n_row, n_front, capacity).transpose(1, 0, 2).reshape(targets.shape)

    lower = jnp.concatenate([leading[i, : i + 1] for i in range(LEAD_TILES)], axis=0)
    lead = pair_gather(lower, "col")
    steps = LEAD_TILES * size // BLOCK
    begun, inverses = factorize_first(ids, lead, size, range(FIRST_STEPS))
    arrived, begun = lax.optimization_barrier((arrived, begun))

    extended, panel = assemble(received, arrived, front, n_col)
    mine = exchange(panel, "col")[:LEAD_TILES]
    *factors, own = factorize_last(begun, inverses, ids, size, range(FIRST_STEPS, steps))
    turned = lax.ppermute(
        mine, ("row", "col"), [(r * n_col + c, c * n_col + r) for r in range(n_row) for c in range(n_col)]
    )
    solved, turned = solve((mine, turned), factors)
    rows = pair_gather(solved, "col")
    cols = pair_gather(turned, "row")
    factor = finish(ids, rows, cols, own, extended, front)
    return factor.reshape(1, tile_rows, 1, size, tile_cols, 1, size)


def solution(mesh):
    in_specs = (
        P("front", None, "row", None, None, "col", None),
        P("front", "row", "col", None, None, None),
        P("front", "row", "col", None),
        P("front", "row", "col", None),
        P("front", "row", "col", None),
        P("front", "row", "col"),
    )
    out_specs = P("front", None, "row", None, None, "col", None)
    return jax.shard_map(per_device, mesh=mesh, in_specs=in_specs, out_specs=out_specs, check_vma=False)
```

```python
import jax
import jax.numpy as jnp
from jax import lax
from jax.experimental import pallas as pl
from jax.experimental.pallas import tpu as pltpu
from jax.sharding import PartitionSpec as P


LEAD_TILES = 4
BLOCK = 128
HALF = 64
RUN = 32
STRIP = 8
VMEM_BYTES = 56 * 1024 * 1024


def vmem():
    return pl.BlockSpec(memory_space=pltpu.VMEM)


def smem():
    return pl.BlockSpec(memory_space=pltpu.SMEM)


def hbm():
    return pl.BlockSpec(memory_space=pl.ANY)


def nt(left, right, precision=None):
    return lax.dot_general(
        left, right, (((1,), (1,)), ((), ())), precision=precision, preferred_element_type=jnp.float32
    )


def split(value):
    high = value.astype(jnp.bfloat16)
    return high, (value - high.astype(jnp.float32)).astype(jnp.bfloat16)


def nt3(left, right):
    return nt(left[0], right[0]) + (nt(left[0], right[1]) + nt(left[1], right[0]))


NOTE_ROWS = 8


def pack(contributions, target_front, target_row, target_col, live_count, n_front, n_row, n_col, tile_cols):
    slots, size, _ = contributions.shape
    capacity = max(2, -(-slots // (n_front * n_row)))
    buckets = n_front * n_row * capacity
    kind = contributions.dtype

    def kernel(
        front_ref, row_ref, col_ref, live_ref, tiles_ref, packed_ref,
        counts, bucket_of, stage, notes, sems_in, sems_out, note_sem,
    ):
        live = live_ref[0]

        def fetch(slot):
            return pltpu.make_async_copy(tiles_ref.at[slot], stage.at[slot], sems_in.at[slot])

        def store(slot, bucket):
            return pltpu.make_async_copy(stage.at[slot], packed_ref.at[bucket, pl.ds(0, size)], sems_out.at[slot])

        def start(slot, carry):
            fetch(slot).start()
            return carry

        lax.fori_loop(0, live, start, 0)
        notes[...] = jnp.full(notes.shape, -1.0, kind)

        def clear(i, carry):
            counts[i] = 0
            return carry

        lax.fori_loop(0, n_front * n_row, clear, 0)

        def assign(slot, carry):
            row, col = row_ref[slot], col_ref[slot]
            destination = front_ref[slot] * n_row + lax.rem(row, n_row)
            position = counts[destination]
            counts[destination] = position + 1
            bucket = destination * capacity + position
            bucket_of[slot] = bucket
            target = lax.div(row, n_row) * tile_cols + lax.div(col, n_col)
            notes[bucket] = jnp.full(notes.shape[1:], target, jnp.int32).astype(jnp.float32).astype(kind)
            return carry

        lax.fori_loop(0, live, assign, 0)
        note_copy = pltpu.make_async_copy(notes, packed_ref.at[:, pl.ds(size, NOTE_ROWS)], note_sem)
        note_copy.start()

        def forward(slot, carry):
            fetch(slot).wait()
            store(slot, bucket_of[slot]).start()
            return carry

        lax.fori_loop(0, live, forward, 0)

        def drain(slot, carry):
            store(slot, bucket_of[slot]).wait()
            return carry

        lax.fori_loop(0, live, drain, 0)
        note_copy.wait()

    return pl.pallas_call(
        kernel,
        name="pack",
        out_shape=jax.ShapeDtypeStruct((buckets, size + NOTE_ROWS, size), kind),
        in_specs=[smem()] * 4 + [hbm()],
        out_specs=hbm(),
        scratch_shapes=[
            pltpu.SMEM((n_front * n_row,), jnp.int32),
            pltpu.SMEM((slots,), jnp.int32),
            pltpu.VMEM((slots, size, size), kind),
            pltpu.VMEM((buckets, NOTE_ROWS, size), kind),
            pltpu.SemaphoreType.DMA((slots,)),
            pltpu.SemaphoreType.DMA((slots,)),
            pltpu.SemaphoreType.DMA,
        ],
        compiler_params=pltpu.CompilerParams(vmem_limit_bytes=VMEM_BYTES),
    )(target_front, target_row, target_col, live_count, contributions)


SCALE_ROWS = 8
SCALE_STEPS = 64


def encode(values):
    n, m = values.shape
    top = jnp.max(jnp.abs(values), axis=1, keepdims=True)
    code = jnp.floor(jnp.log2(jnp.maximum(top, 2.0**-110)) * SCALE_STEPS) + 1.0
    coded = jnp.round(values * jnp.exp2(15.0 - 1e-3 - code / SCALE_STEPS))
    picked = lax.broadcasted_iota(jnp.int32, (n, m), 0) == lax.broadcasted_iota(jnp.int32, (n, m), 1)
    line = jnp.sum(jnp.where(picked, code, 0.0), axis=0, keepdims=True)
    lines = jnp.broadcast_to(line, (SCALE_ROWS, m))
    return jnp.concatenate([coded, lines], axis=0).astype(jnp.int32).astype(jnp.int16)


def decode(coded):
    wide = coded.astype(jnp.int32).astype(jnp.float32)
    n, m = wide.shape[0] - SCALE_ROWS, wide.shape[1]
    values, line = wide[:n], wide[n : n + 1]
    picked = lax.broadcasted_iota(jnp.int32, (n, m), 0) == lax.broadcasted_iota(jnp.int32, (n, m), 1)
    code = jnp.sum(jnp.where(picked, jnp.broadcast_to(line, (n, m)), 0.0), axis=1, keepdims=True)
    return values * jnp.exp2(code / SCALE_STEPS - 15.0 + 1e-3)


EXTENDED = ((1, 0), (1, 1), (2, 0), (2, 1), (2, 2))


def assemble(received, arrived, front, chunks):
    total, _, size = received.shape
    thin = front.shape[0] * size // chunks

    def kernel(arrived_ref, received_ref, front_ref, ext_ref, panel_ref, landed, column, sems):
        def copy(i):
            return pltpu.make_async_copy(received_ref.at[i, pl.ds(0, size)], landed.at[i], sems.at[i])

        def fetch(i, carry):
            @pl.when(arrived_ref[i] >= 0)
            def _():
                copy(i).start()

            return carry

        lax.fori_loop(0, total, fetch, 0)
        for slot, (a, b) in enumerate(EXTENDED):
            ext_ref[slot] = front_ref[a, b].astype(jnp.float32)

        def add(i, carry):
            target = arrived_ref[i]

            @pl.when(target >= 0)
            def _():
                copy(i).wait()
                slot = jnp.where(target >= 6, target - 4, target - 3)
                ext_ref[slot] = ext_ref[slot] + landed[i].astype(jnp.float32)

            return carry

        lax.fori_loop(0, total, add, 0)
        column[0:size] = front_ref[0, 0].astype(jnp.float32)
        column[size : 2 * size] = ext_ref[0]
        column[2 * size : 3 * size] = ext_ref[2]
        for chunk in range(chunks):
            panel_ref[chunk] = encode(column[chunk * thin : (chunk + 1) * thin, :])

    return pl.pallas_call(
        kernel,
        name="assemble",
        out_shape=(
            jax.ShapeDtypeStruct((len(EXTENDED), size, size), jnp.float32),
            jax.ShapeDtypeStruct((chunks, thin + SCALE_ROWS, size), jnp.int16),
        ),
        in_specs=[smem(), hbm(), vmem()],
        out_specs=(vmem(), vmem()),
        scratch_shapes=[
            pltpu.VMEM((total, size, size), jnp.bfloat16),
            pltpu.VMEM((3 * size, size), jnp.float32),
            pltpu.SemaphoreType.DMA((total,)),
        ],
        compiler_params=pltpu.CompilerParams(vmem_limit_bytes=VMEM_BYTES),
    )(arrived, received, front)


def pick_lane(value, lane):
    index = jnp.full(value.shape, lane, jnp.int32)
    return jnp.take_along_axis(value, index, axis=1, mode="promise_in_bounds")


def factor_block(work):
    lanes = lax.broadcasted_iota(jnp.int32, (STRIP, BLOCK), 1)
    strip_rows = lax.broadcasted_iota(jnp.int32, (STRIP, BLOCK), 0)

    def spread(value, i):
        return jnp.broadcast_to(value[i : i + 1, :], value.shape)

    def step(number, top, bottom):
        base = pl.multiple_of(number * STRIP, STRIP)
        strip = work[pl.ds(base, STRIP), :]
        own = [pick_lane(strip, base + i) for i in range(STRIP)]
        whole = work[top:bottom, :]
        below = lax.broadcasted_iota(jnp.int32, whole.shape, 0) + top >= base + STRIP
        columns = [jnp.where(below, pick_lane(whole, base + i), 0.0) for i in range(STRIP)]
        for i in range(STRIP):
            pivot = spread(own[i], i)
            inverse = 1.0 / pivot
            factors = jnp.where(strip_rows > i, own[i] * inverse, 0.0)
            line = jnp.where(lanes == base + i, pivot + pivot, spread(strip, i))
            strip = strip - factors * line
            lower = columns[i] * jnp.broadcast_to(inverse[0:1], whole.shape)
            for j in range(i + 1, STRIP):
                entry = spread(own[j], i)
                own[j] = own[j] - factors * entry
                columns[j] = columns[j] - lower * jnp.broadcast_to(entry[0:1], whole.shape)
            whole = whole - lower * jnp.broadcast_to(line[0:1], whole.shape)
        work[top:bottom, :] = whole
        work[pl.ds(base, STRIP), :] = strip

    for first in range(0, BLOCK, HALF):
        last = first + HALF
        for top in range(first, last, RUN):

            def run(number, carry, top=top):
                step(number, top, last)
                return carry

            lax.fori_loop(top // STRIP, (top + RUN) // STRIP, run, 0)
        if last < BLOCK:
            done = work[first:last, :]
            at_pivot = lax.broadcasted_iota(jnp.int32, done.shape, 0) + first == lax.broadcasted_iota(
                jnp.int32, done.shape, 1
            )
            pivots = jnp.where(at_pivot, done, 0.0)
            scaled = done / jnp.sum(pivots, axis=1, keepdims=True)
            change = lax.dot_general(
                scaled, done + pivots, (((0,), (0,)), ((), ())),
                precision=lax.Precision.HIGHEST, preferred_element_type=jnp.float32,
            )
            work[last:BLOCK, :] = work[last:BLOCK, :] - change[last:BLOCK, :]


def eliminate(full, inverses, work, blocks):
    order = full.shape[0]
    r = lax.broadcasted_iota(jnp.int32, (BLOCK, BLOCK), 0)
    c = lax.broadcasted_iota(jnp.int32, (BLOCK, BLOCK), 1)
    for k in blocks:
        s, e = k * BLOCK, (k + 1) * BLOCK
        work[...] = full[s:e, s:e]
        factor_block(work)
        done = work[...]
        diagonal = jnp.where(r == c, done, 0.0)
        root = lax.rsqrt(jnp.sum(diagonal, axis=1, keepdims=True))
        inverse = jnp.where(r >= c, done, 0.0) * root * (1.0 / jnp.sum(diagonal, axis=0, keepdims=True))
        inverses[k] = inverse
        full[s:e, s:e] = (jnp.where(r <= c, done, 0.0) * root).T
        if e < order:
            panel = nt3(split(full[e:order, s:e]), split(inverse))
            full[e:order, s:e] = panel
            high, low = split(panel)
            for o in range(e, order, BLOCK):
                y = slice(o - e, o - e + BLOCK)
                full[o:order, o : o + BLOCK] = full[o:order, o : o + BLOCK] - nt3(
                    (high[o - e :], low[o - e :]), (high[y], low[y])
                )


def tile_inverse(first, second, between):
    def product(left, right):
        return jnp.dot(left, right, precision=lax.Precision.HIGHEST, preferred_element_type=jnp.float32)

    corner = -product(second, product(between, first))
    above = jnp.concatenate([first, jnp.zeros_like(first)], axis=1)
    return split(jnp.concatenate([above, jnp.concatenate([corner, second], axis=1)], axis=0))


PAIRS = tuple((i, j) for i in range(LEAD_TILES) for j in range(i + 1))


def collect(ids, chunks):
    _, thin, size = chunks[0].shape
    count = len(chunks)

    def kernel(ids_ref, *refs):
        *chunk_refs, out_ref, sems = refs
        for i in range(LEAD_TILES):
            first = PAIRS.index((i, 0))
            steps = lax.rem(ids_ref[0] - i + count, count)

            def copy(ref, i=i, first=first):
                return pltpu.make_async_copy(ref.at[pl.ds(0, i + 1)], out_ref.at[pl.ds(first, i + 1)], sems.at[i])

            for s in range(count):

                @pl.when(steps == s)
                def _():
                    copy(chunk_refs[s]).start()

        for i in range(LEAD_TILES):
            first = PAIRS.index((i, 0))
            pltpu.make_async_copy(
                chunk_refs[0].at[pl.ds(0, i + 1)], out_ref.at[pl.ds(first, i + 1)], sems.at[i]
            ).wait()

    return pl.pallas_call(
        kernel,
        name="collect",
        out_shape=jax.ShapeDtypeStruct((len(PAIRS), thin, size), chunks[0].dtype),
        in_specs=[smem()] + [hbm()] * count,
        out_specs=vmem(),
        scratch_shapes=[pltpu.SemaphoreType.DMA((LEAD_TILES,))],
    )(ids, *chunks)


def factorize_first(ids, lead, size):
    order = LEAD_TILES * size
    done = order - size
    half = size // BLOCK

    def kernel(ids_ref, *refs):
        *pieces, high_ref, low_ref, ih_ref, il_ref, own_ref, rest_ref, full, inverses, work = refs
        for ref, source in ring_pieces(pieces, lax.div(ids_ref[1], 2)):
            for number, (i, j) in enumerate(PAIRS):
                tile = ref[number].astype(jnp.float32)
                thin = tile.shape[0]
                start = pl.multiple_of(i * size + source * thin, thin)
                full[pl.ds(start, thin), j * size : (j + 1) * size] = tile
        eliminate(full, inverses, work, range(done // BLOCK))
        for q in range(LEAD_TILES - 1):
            s = q * size
            full[s : s + BLOCK, s + BLOCK : s + size] = jnp.zeros((BLOCK, size - BLOCK), jnp.float32)
            ih_ref[q], il_ref[q] = tile_inverse(
                inverses[q * half], inverses[q * half + 1], full[s + BLOCK : s + size, s : s + BLOCK]
            )
        for i, j in PAIRS[:-1]:
            tile = full[i * size : (i + 1) * size, j * size : (j + 1) * size]
            high, low = split(tile)
            high_ref[i * size : (i + 1) * size, j * size : (j + 1) * size] = high
            low_ref[i * size : (i + 1) * size, j * size : (j + 1) * size] = low

            @pl.when((ids_ref[0] == i) & (ids_ref[1] == j))
            def _():
                own_ref[...] = tile

        rest_ref[...] = full[done:order, done:order]

    wide = jax.ShapeDtypeStruct((order, done), jnp.bfloat16)
    inv = jax.ShapeDtypeStruct((LEAD_TILES - 1, size, size), jnp.bfloat16)
    tile = jax.ShapeDtypeStruct((size, size), jnp.float32)
    return pl.pallas_call(
        kernel,
        name="factorize_first",
        out_shape=(wide, wide, inv, inv, tile, tile),
        in_specs=[smem()] + [vmem()] * len(lead),
        out_specs=(vmem(),) * 6,
        scratch_shapes=[
            pltpu.VMEM((order, order), jnp.float32),
            pltpu.VMEM((done // BLOCK, BLOCK, BLOCK), jnp.float32),
            pltpu.VMEM((BLOCK, BLOCK), jnp.float32),
        ],
        compiler_params=pltpu.CompilerParams(vmem_limit_bytes=VMEM_BYTES),
    )(ids, *lead)


def factorize_last(rest):
    size = rest.shape[0]

    def kernel(rest_ref, own_ref, ih_ref, il_ref, inverses, work):
        own_ref[...] = rest_ref[...]
        eliminate(own_ref, inverses, work, range(size // BLOCK))
        own_ref[0:BLOCK, BLOCK:size] = jnp.zeros((BLOCK, size - BLOCK), jnp.float32)
        ih_ref[...], il_ref[...] = tile_inverse(inverses[0], inverses[1], own_ref[BLOCK:size, 0:BLOCK])

    inv = jax.ShapeDtypeStruct((size, size), jnp.bfloat16)
    return pl.pallas_call(
        kernel,
        name="factorize_last",
        out_shape=(jax.ShapeDtypeStruct((size, size), jnp.float32), inv, inv),
        in_specs=[vmem()],
        out_specs=(vmem(),) * 3,
        scratch_shapes=[
            pltpu.VMEM((size // BLOCK, BLOCK, BLOCK), jnp.float32),
            pltpu.VMEM((BLOCK, BLOCK), jnp.float32),
        ],
        compiler_params=pltpu.CompilerParams(vmem_limit_bytes=VMEM_BYTES),
    )(rest)


def solve(panels, factors):
    _, coded_rows, size = panels[0].shape
    thin, order = coded_rows - SCALE_ROWS, LEAD_TILES * size
    count = len(panels)

    def kernel(*refs):
        panel_refs = refs[:count]
        high_ref, low_ref, ih_ref, il_ref, last_ih_ref, last_il_ref = refs[count : count + 6]
        *out_refs, xh, xl = refs[count + 6 :]
        for q in range(LEAD_TILES):
            s, e = q * size, (q + 1) * size
            acc = jnp.concatenate([decode(ref[q]) for ref in panel_refs], axis=0)
            if q:
                acc = acc - nt3((xh[:, 0:s], xl[:, 0:s]), (high_ref[s:e, 0:s], low_ref[s:e, 0:s]))
            last = q == LEAD_TILES - 1
            inverse = (last_ih_ref[...], last_il_ref[...]) if last else (ih_ref[q], il_ref[q])
            x = nt3(split(acc), inverse)
            xh[:, s:e], xl[:, s:e] = split(x)
            for number, ref in enumerate(out_refs):
                ref[q] = encode(x[number * thin : (number + 1) * thin])

    return pl.pallas_call(
        kernel,
        name="solve",
        out_shape=(jax.ShapeDtypeStruct((LEAD_TILES, coded_rows, size), jnp.int16),) * count,
        in_specs=[vmem()] * (count + 6),
        out_specs=(vmem(),) * count,
        scratch_shapes=[pltpu.VMEM((count * thin, order), jnp.bfloat16)] * 2,
        compiler_params=pltpu.CompilerParams(vmem_limit_bytes=VMEM_BYTES),
    )(*panels, *factors)


def finish(ids, rows, cols, own, last_own, extended, front):
    size = own.shape[0]
    order = LEAD_TILES * size
    tile_rows, tile_cols = front.shape[:2]
    lanes = 128
    parts = size // lanes
    half = len(rows)

    def kernel(ids_ref, *refs):
        row_pieces, col_pieces = refs[:half], refs[half : 2 * half]
        own_ref, last_own_ref, ext_ref, front_ref, out_ref, xh, xl = refs[2 * half :]
        row, col = ids_ref[0], ids_ref[1]

        def put(a, b, tile):
            for part in range(parts):
                start = (a * size * tile_cols + b) * parts + part
                out_ref[pl.ds(start, size, stride=tile_cols * parts), :] = tile[:, part * lanes : (part + 1) * lanes]

        for pieces, place, first in ((row_pieces, col, 0), (col_pieces, row, tile_rows * size)):
            for ref, inner, chunk in pair_pieces(pieces, place):
                for q in range(LEAD_TILES):
                    value = decode(ref[inner, q])
                    thin = value.shape[0]
                    start = pl.multiple_of(first + chunk * thin, 32)
                    high, low = split(value)
                    xh[pl.ds(start, thin), q * size : (q + 1) * size] = high
                    xl[pl.ds(start, thin), q * size : (q + 1) * size] = low

        def take(ref, n):
            return ref[n * size : (n + 1) * size, :]

        def update(a, b, base):
            x, y = a, tile_rows + b
            put(a, b, base - nt3((take(xh, x), take(xl, x)), (take(xh, y), take(xl, y))))

        def put_panel(a):
            for q in range(LEAD_TILES):

                @pl.when(col == q)
                def _():
                    high = xh[a * size : (a + 1) * size, q * size : (q + 1) * size].astype(jnp.float32)
                    low = xl[a * size : (a + 1) * size, q * size : (q + 1) * size].astype(jnp.float32)
                    put(a, 0, high + low)

        zero = jnp.zeros((size, size), jnp.float32)
        for a, b in ((0, 1), (0, 2), (1, 2)):
            put(a, b, zero)
        in_panel = col < LEAD_TILES
        lead_row = row < LEAD_TILES
        last_tile = LEAD_TILES - 1
        put_panel(1)
        put_panel(2)

        @pl.when(jnp.logical_not(in_panel))
        def _():
            update(1, 0, ext_ref[0])
            update(2, 0, ext_ref[2])

        @pl.when(row < col)
        def _():
            put(0, 0, zero)
            put(1, 1, zero)
            put(2, 2, zero)

        @pl.when(row >= col)
        def _():
            @pl.when(lead_row)
            def _():
                put(0, 0, jnp.where((row == last_tile) & (col == last_tile), last_own_ref[...], own_ref[...]))

            @pl.when(jnp.logical_not(lead_row))
            def _():
                put_panel(0)

            @pl.when(jnp.logical_not(in_panel))
            def _():
                update(0, 0, front_ref[0, 0].astype(jnp.float32))

            update(1, 1, ext_ref[1])
            update(2, 2, ext_ref[4])

        update(2, 1, ext_ref[3])

    return pl.pallas_call(
        kernel,
        name="finish",
        out_shape=jax.ShapeDtypeStruct((tile_rows * size * tile_cols * parts, lanes), jnp.float32),
        in_specs=[smem()] + [vmem()] * (2 * half + 4),
        out_specs=vmem(),
        scratch_shapes=[pltpu.VMEM((2 * tile_rows * size, order), jnp.bfloat16)] * 2,
        compiler_params=pltpu.CompilerParams(vmem_limit_bytes=VMEM_BYTES),
    )(ids, *rows, *cols, own, last_own, extended, front)


SHIFTS = (1, 3, 2)


def exchange(value, axis):
    return lax.all_to_all(value, axis, split_axis=0, concat_axis=0, tiled=True)


def permute(value, axis, target):
    return lax.ppermute(value, axis, [(i, target(i)) for i in range(lax.axis_size(axis))])


def ring_gather(value, axis):
    ring = lax.axis_size(axis) // 2
    shifted = [permute(value, axis, lambda i: (i // 2 + shift) % ring * 2 + i % 2) for shift in SHIFTS]
    return (value, *shifted)


def ring_pieces(pieces, place):
    ring = len(SHIFTS) + 1
    for ref, shift in zip(pieces, (0,) + SHIFTS, strict=True):
        yield ref, lax.rem(place + (ring - shift), ring)


def pair_gather(value, axis):
    partner = permute(value, axis, lambda i: i ^ 1)
    return ring_gather(jnp.stack([value, partner]), axis)


def pair_pieces(pieces, place):
    side = lax.rem(place, 2)
    for ref, source in ring_pieces(pieces, lax.div(place, 2)):
        yield ref, 0, 2 * source + side
        yield ref, 1, 2 * source + 1 - side


def per_device(front_matrix, contributions, target_front, target_row, target_col, live_count):
    _, tile_rows, _, size, tile_cols, _, _ = front_matrix.shape
    n_front, n_row, n_col = (lax.axis_size(name) for name in ("front", "row", "col"))
    slots = contributions.shape[3]
    front = front_matrix.reshape(tile_rows, size, tile_cols, size).transpose(0, 2, 1, 3)
    ids = jnp.stack([lax.axis_index("row"), lax.axis_index("col")]).astype(jnp.int32)

    ring = n_col // 2
    thin = size // ring
    chunks = jnp.repeat(front[0, 0].reshape(ring, thin, size), 2, axis=0)
    chunk = exchange(chunks, "col")[:LEAD_TILES]
    leading = [chunk]
    for step in range(1, n_row):
        leading.append(lax.ppermute(chunk, "row", [(i, (i + step) % n_row) for i in range(LEAD_TILES)]))

    packed = pack(
        contributions.reshape(slots, size, size),
        target_front.reshape(slots), target_row.reshape(slots), target_col.reshape(slots),
        live_count.reshape(1), n_front, n_row, n_col, tile_cols,
    )
    received = exchange(packed, ("front", "row"))

    lead = ring_gather(collect(ids, leading), "col")
    *factors, own, rest = factorize_first(ids, lead, size)
    received, rest = lax.optimization_barrier((received, rest))

    arrived = received[:, size, 0].astype(jnp.int32)
    extended, panel = assemble(received, arrived, front, n_col)
    mine = exchange(panel, "col")[:LEAD_TILES]
    last_own, *last_inverse = factorize_last(rest)
    turned = lax.ppermute(
        mine, ("row", "col"), [(r * n_col + c, c * n_col + r) for r in range(n_row) for c in range(n_col)]
    )
    solved, turned = solve((mine, turned), (*factors, *last_inverse))
    rows = pair_gather(solved, "col")
    cols = pair_gather(turned, "row")
    factor = finish(ids, rows, cols, own, last_own, extended, front)
    return factor.reshape(1, tile_rows, 1, size, tile_cols, 1, size)


def solution(mesh):
    in_specs = (
        P("front", None, "row", None, None, "col", None),
        P("front", "row", "col", None, None, None),
        P("front", "row", "col", None),
        P("front", "row", "col", None),
        P("front", "row", "col", None),
        P("front", "row", "col"),
    )
    out_specs = P("front", None, "row", None, None, "col", None)
    return jax.shard_map(per_device, mesh=mesh, in_specs=in_specs, out_specs=out_specs, check_vma=False)
```

```python
import jax
import jax.numpy as jnp
from jax import lax
from jax.experimental import pallas as pl
from jax.experimental.pallas import tpu as pltpu
from jax.sharding import PartitionSpec as P


LEAD_TILES = 4
BLOCK = 128
HALF = 64
RUN = 32
STRIP = 8
VMEM_BYTES = 56 * 1024 * 1024


def vmem():
    return pl.BlockSpec(memory_space=pltpu.VMEM)


def smem():
    return pl.BlockSpec(memory_space=pltpu.SMEM)


def hbm():
    return pl.BlockSpec(memory_space=pl.ANY)


def nt(left, right, precision=None):
    return lax.dot_general(
        left, right, (((1,), (1,)), ((), ())), precision=precision, preferred_element_type=jnp.float32
    )


def split(value):
    high = value.astype(jnp.bfloat16)
    return high, (value - high.astype(jnp.float32)).astype(jnp.bfloat16)


def nt3(left, right):
    return nt(left[0], right[0]) + (nt(left[0], right[1]) + nt(left[1], right[0]))


NOTE_ROWS = 8


def pack(contributions, target_front, target_row, target_col, live_count, n_front, n_row, n_col, tile_cols):
    slots, size, _ = contributions.shape
    capacity = max(2, -(-slots // (n_front * n_row)))
    buckets = n_front * n_row * capacity
    kind = contributions.dtype

    def kernel(
        front_ref, row_ref, col_ref, live_ref, tiles_ref, packed_ref,
        counts, bucket_of, stage, notes, sems_in, sems_out, note_sem,
    ):
        live = live_ref[0]

        def fetch(slot):
            return pltpu.make_async_copy(tiles_ref.at[slot], stage.at[slot], sems_in.at[slot])

        def store(slot, bucket):
            return pltpu.make_async_copy(stage.at[slot], packed_ref.at[bucket, pl.ds(0, size)], sems_out.at[slot])

        def start(slot, carry):
            fetch(slot).start()
            return carry

        lax.fori_loop(0, live, start, 0)
        notes[...] = jnp.full(notes.shape, -1.0, kind)

        def clear(i, carry):
            counts[i] = 0
            return carry

        lax.fori_loop(0, n_front * n_row, clear, 0)

        def assign(slot, carry):
            row, col = row_ref[slot], col_ref[slot]
            destination = front_ref[slot] * n_row + lax.rem(row, n_row)
            position = counts[destination]
            counts[destination] = position + 1
            bucket = destination * capacity + position
            bucket_of[slot] = bucket
            target = lax.div(row, n_row) * tile_cols + lax.div(col, n_col)
            notes[bucket] = jnp.full(notes.shape[1:], target, jnp.int32).astype(jnp.float32).astype(kind)
            return carry

        lax.fori_loop(0, live, assign, 0)
        note_copy = pltpu.make_async_copy(notes, packed_ref.at[:, pl.ds(size, NOTE_ROWS)], note_sem)
        note_copy.start()

        def forward(slot, carry):
            fetch(slot).wait()
            store(slot, bucket_of[slot]).start()
            return carry

        lax.fori_loop(0, live, forward, 0)

        def drain(slot, carry):
            store(slot, bucket_of[slot]).wait()
            return carry

        lax.fori_loop(0, live, drain, 0)
        note_copy.wait()

    return pl.pallas_call(
        kernel,
        name="pack",
        out_shape=jax.ShapeDtypeStruct((buckets, size + NOTE_ROWS, size), kind),
        in_specs=[smem()] * 4 + [hbm()],
        out_specs=hbm(),
        scratch_shapes=[
            pltpu.SMEM((n_front * n_row,), jnp.int32),
            pltpu.SMEM((slots,), jnp.int32),
            pltpu.VMEM((slots, size, size), kind),
            pltpu.VMEM((buckets, NOTE_ROWS, size), kind),
            pltpu.SemaphoreType.DMA((slots,)),
            pltpu.SemaphoreType.DMA((slots,)),
            pltpu.SemaphoreType.DMA,
        ],
        compiler_params=pltpu.CompilerParams(vmem_limit_bytes=VMEM_BYTES),
    )(target_front, target_row, target_col, live_count, contributions)


SCALE_ROWS = 8
SCALE_STEPS = 64


def encode(values):
    n, m = values.shape
    top = jnp.max(jnp.abs(values), axis=1, keepdims=True)
    code = jnp.floor(jnp.log2(jnp.maximum(top, 2.0**-110)) * SCALE_STEPS) + 1.0
    coded = jnp.round(values * jnp.exp2(15.0 - 1e-3 - code / SCALE_STEPS))
    picked = lax.broadcasted_iota(jnp.int32, (n, m), 0) == lax.broadcasted_iota(jnp.int32, (n, m), 1)
    line = jnp.sum(jnp.where(picked, code, 0.0), axis=0, keepdims=True)
    lines = jnp.broadcast_to(line, (SCALE_ROWS, m))
    return jnp.concatenate([coded, lines], axis=0).astype(jnp.int32).astype(jnp.int16)


def decode(coded):
    wide = coded.astype(jnp.int32).astype(jnp.float32)
    n, m = wide.shape[0] - SCALE_ROWS, wide.shape[1]
    values, line = wide[:n], wide[n : n + 1]
    picked = lax.broadcasted_iota(jnp.int32, (n, m), 0) == lax.broadcasted_iota(jnp.int32, (n, m), 1)
    code = jnp.sum(jnp.where(picked, jnp.broadcast_to(line, (n, m)), 0.0), axis=1, keepdims=True)
    return values * jnp.exp2(code / SCALE_STEPS - 15.0 + 1e-3)


EXTENDED = ((1, 0), (1, 1), (2, 0), (2, 1), (2, 2))


def assemble(received, front, chunks):
    total, _, size = received.shape
    thin = front.shape[0] * size // chunks

    def kernel(
        received_ref, front_ref, ext_ref, panel_ref, landed, column, notes, numbers, arrived_ref, sems, note_sem
    ):
        note_copy = pltpu.make_async_copy(received_ref.at[:, pl.ds(size, NOTE_ROWS)], notes, note_sem)
        note_copy.start()

        def copy(i):
            return pltpu.make_async_copy(received_ref.at[i, pl.ds(0, size)], landed.at[i], sems.at[i])

        def fetch(i, carry):
            @pl.when(arrived_ref[i, 0] >= 0)
            def _():
                copy(i).start()

            return carry

        note_copy.wait()
        for i in range(total):
            numbers[i : i + 1, :] = notes[i, 0:1, 0 : numbers.shape[1]].astype(jnp.float32).astype(jnp.int32)
        number_copy = pltpu.make_async_copy(numbers, arrived_ref, note_sem)
        number_copy.start()
        for slot, (a, b) in enumerate(EXTENDED):
            ext_ref[slot] = front_ref[a, b].astype(jnp.float32)
        number_copy.wait()
        lax.fori_loop(0, total, fetch, 0)

        def add(i, carry):
            target = arrived_ref[i, 0]

            @pl.when(target >= 0)
            def _():
                copy(i).wait()
                slot = jnp.where(target >= 6, target - 4, target - 3)
                ext_ref[slot] = ext_ref[slot] + landed[i].astype(jnp.float32)

            return carry

        lax.fori_loop(0, total, add, 0)
        column[0:size] = front_ref[0, 0].astype(jnp.float32)
        column[size : 2 * size] = ext_ref[0]
        column[2 * size : 3 * size] = ext_ref[2]
        for chunk in range(chunks):
            panel_ref[chunk] = encode(column[chunk * thin : (chunk + 1) * thin, :])

    return pl.pallas_call(
        kernel,
        name="assemble",
        out_shape=(
            jax.ShapeDtypeStruct((len(EXTENDED), size, size), jnp.float32),
            jax.ShapeDtypeStruct((chunks, thin + SCALE_ROWS, size), jnp.int16),
        ),
        in_specs=[hbm(), vmem()],
        out_specs=(vmem(), vmem()),
        scratch_shapes=[
            pltpu.VMEM((total, size, size), jnp.bfloat16),
            pltpu.VMEM((3 * size, size), jnp.float32),
            pltpu.VMEM((total, NOTE_ROWS, size), jnp.bfloat16),
            pltpu.VMEM((total, 128), jnp.int32),
            pltpu.SMEM((total, 128), jnp.int32),
            pltpu.SemaphoreType.DMA((total,)),
            pltpu.SemaphoreType.DMA,
        ],
        compiler_params=pltpu.CompilerParams(vmem_limit_bytes=VMEM_BYTES),
    )(received, front)


def pick_lane(value, lane):
    index = jnp.full(value.shape, lane, jnp.int32)
    return jnp.take_along_axis(value, index, axis=1, mode="promise_in_bounds")


def factor_block(work):
    lanes = lax.broadcasted_iota(jnp.int32, (STRIP, BLOCK), 1)
    strip_rows = lax.broadcasted_iota(jnp.int32, (STRIP, BLOCK), 0)

    def spread(value, i):
        return jnp.broadcast_to(value[i : i + 1, :], value.shape)

    def step(number, top, bottom):
        base = pl.multiple_of(number * STRIP, STRIP)
        strip = work[pl.ds(base, STRIP), :]
        own = [pick_lane(strip, base + i) for i in range(STRIP)]
        whole = work[top:bottom, :]
        below = lax.broadcasted_iota(jnp.int32, whole.shape, 0) + top >= base + STRIP
        columns = [jnp.where(below, pick_lane(whole, base + i), 0.0) for i in range(STRIP)]
        for i in range(STRIP):
            pivot = spread(own[i], i)
            inverse = 1.0 / pivot
            factors = jnp.where(strip_rows > i, own[i] * inverse, 0.0)
            line = jnp.where(lanes == base + i, pivot + pivot, spread(strip, i))
            strip = strip - factors * line
            lower = columns[i] * jnp.broadcast_to(inverse[0:1], whole.shape)
            for j in range(i + 1, STRIP):
                entry = spread(own[j], i)
                own[j] = own[j] - factors * entry
                columns[j] = columns[j] - lower * jnp.broadcast_to(entry[0:1], whole.shape)
            whole = whole - lower * jnp.broadcast_to(line[0:1], whole.shape)
        work[top:bottom, :] = whole
        work[pl.ds(base, STRIP), :] = strip

    for first in range(0, BLOCK, HALF):
        last = first + HALF
        for top in range(first, last, RUN):

            def run(number, carry, top=top):
                step(number, top, last)
                return carry

            lax.fori_loop(top // STRIP, (top + RUN) // STRIP, run, 0)
        if last < BLOCK:
            done = work[first:last, :]
            at_pivot = lax.broadcasted_iota(jnp.int32, done.shape, 0) + first == lax.broadcasted_iota(
                jnp.int32, done.shape, 1
            )
            pivots = jnp.where(at_pivot, done, 0.0)
            scaled = done / jnp.sum(pivots, axis=1, keepdims=True)
            change = lax.dot_general(
                scaled, done + pivots, (((0,), (0,)), ((), ())),
                precision=lax.Precision.HIGHEST, preferred_element_type=jnp.float32,
            )
            work[last:BLOCK, :] = work[last:BLOCK, :] - change[last:BLOCK, :]


def eliminate(full, inverses, work, blocks):
    order = full.shape[0]
    r = lax.broadcasted_iota(jnp.int32, (BLOCK, BLOCK), 0)
    c = lax.broadcasted_iota(jnp.int32, (BLOCK, BLOCK), 1)
    for k in blocks:
        s, e = k * BLOCK, (k + 1) * BLOCK
        work[...] = full[s:e, s:e]
        factor_block(work)
        done = work[...]
        diagonal = jnp.where(r == c, done, 0.0)
        root = lax.rsqrt(jnp.sum(diagonal, axis=1, keepdims=True))
        inverse = jnp.where(r >= c, done, 0.0) * root * (1.0 / jnp.sum(diagonal, axis=0, keepdims=True))
        inverses[k] = inverse
        full[s:e, s:e] = (jnp.where(r <= c, done, 0.0) * root).T
        if e < order:
            panel = nt3(split(full[e:order, s:e]), split(inverse))
            full[e:order, s:e] = panel
            high, low = split(panel)
            for o in range(e, order, BLOCK):
                y = slice(o - e, o - e + BLOCK)
                full[o:order, o : o + BLOCK] = full[o:order, o : o + BLOCK] - nt3(
                    (high[o - e :], low[o - e :]), (high[y], low[y])
                )


def tile_inverse(first, second, between):
    def product(left, right):
        return jnp.dot(left, right, precision=lax.Precision.HIGHEST, preferred_element_type=jnp.float32)

    corner = -product(second, product(between, first))
    above = jnp.concatenate([first, jnp.zeros_like(first)], axis=1)
    return split(jnp.concatenate([above, jnp.concatenate([corner, second], axis=1)], axis=0))


PAIRS = tuple((i, j) for i in range(LEAD_TILES) for j in range(i + 1))


def collect(ids, pairs):
    _, _, thin, size = pairs[0].shape
    ring = len(pairs)

    def kernel(ids_ref, *refs):
        *pair_refs, out_ref, sems = refs
        place, side = lax.div(ids_ref[0], 2), lax.rem(ids_ref[0], 2)
        copies = []
        for i in range(LEAD_TILES):
            first = PAIRS.index((i, 0))
            inner = lax.rem(side + i, 2)
            steps = lax.rem(place - i // 2 + ring, ring)

            def copy(ref, i=i, first=first, inner=inner):
                return pltpu.make_async_copy(
                    ref.at[inner, pl.ds(0, i + 1)], out_ref.at[pl.ds(first, i + 1)], sems.at[i]
                )

            for s in range(ring):

                @pl.when(steps == s)
                def _():
                    copy(pair_refs[s]).start()

            copies.append(copy(pair_refs[0]))
        for one in copies:
            one.wait()

    return pl.pallas_call(
        kernel,
        name="collect",
        out_shape=jax.ShapeDtypeStruct((len(PAIRS), thin, size), pairs[0].dtype),
        in_specs=[smem()] + [hbm()] * ring,
        out_specs=vmem(),
        scratch_shapes=[pltpu.SemaphoreType.DMA((LEAD_TILES,))],
    )(ids, *pairs)


def factorize_first(ids, lead, size):
    order = LEAD_TILES * size
    done = order - size
    half = size // BLOCK

    def kernel(ids_ref, *refs):
        *pieces, high_ref, low_ref, ih_ref, il_ref, own_ref, rest_ref, full, inverses, work = refs
        for ref, first, source in ring_pieces(pieces, lax.div(ids_ref[1], 2), len(PAIRS)):
            for number in range(ref.shape[0]):
                i, j = PAIRS[first + number]
                tile = ref[number].astype(jnp.float32)
                thin = tile.shape[0]
                start = pl.multiple_of(i * size + source * thin, thin)
                full[pl.ds(start, thin), j * size : (j + 1) * size] = tile
        eliminate(full, inverses, work, range(done // BLOCK))
        for q in range(LEAD_TILES - 1):
            s = q * size
            full[s : s + BLOCK, s + BLOCK : s + size] = jnp.zeros((BLOCK, size - BLOCK), jnp.float32)
            ih_ref[q], il_ref[q] = tile_inverse(
                inverses[q * half], inverses[q * half + 1], full[s + BLOCK : s + size, s : s + BLOCK]
            )
        for i, j in PAIRS[:-1]:
            tile = full[i * size : (i + 1) * size, j * size : (j + 1) * size]
            high, low = split(tile)
            high_ref[i * size : (i + 1) * size, j * size : (j + 1) * size] = high
            low_ref[i * size : (i + 1) * size, j * size : (j + 1) * size] = low

            @pl.when((ids_ref[0] == i) & (ids_ref[1] == j))
            def _():
                own_ref[...] = tile

        rest_ref[...] = full[done:order, done:order]

    wide = jax.ShapeDtypeStruct((order, done), jnp.bfloat16)
    inv = jax.ShapeDtypeStruct((LEAD_TILES - 1, size, size), jnp.bfloat16)
    tile = jax.ShapeDtypeStruct((size, size), jnp.float32)
    return pl.pallas_call(
        kernel,
        name="factorize_first",
        out_shape=(wide, wide, inv, inv, tile, tile),
        in_specs=[smem()] + [vmem()] * len(lead),
        out_specs=(vmem(),) * 6,
        scratch_shapes=[
            pltpu.VMEM((order, order), jnp.float32),
            pltpu.VMEM((done // BLOCK, BLOCK, BLOCK), jnp.float32),
            pltpu.VMEM((BLOCK, BLOCK), jnp.float32),
        ],
        compiler_params=pltpu.CompilerParams(vmem_limit_bytes=VMEM_BYTES),
    )(ids, *lead)


def factorize_next(rest):
    def kernel(rest_ref, out_ref, inverses, work):
        out_ref[...] = rest_ref[...]
        eliminate(out_ref, inverses, work, range(1))

    return pl.pallas_call(
        kernel,
        name="factorize_next",
        out_shape=(
            jax.ShapeDtypeStruct(rest.shape, jnp.float32),
            jax.ShapeDtypeStruct((1, BLOCK, BLOCK), jnp.float32),
        ),
        in_specs=[vmem()],
        out_specs=(vmem(),) * 2,
        scratch_shapes=[pltpu.VMEM((BLOCK, BLOCK), jnp.float32)],
        compiler_params=pltpu.CompilerParams(vmem_limit_bytes=VMEM_BYTES),
    )(rest)


def factorize_last(rest, first_inverse):
    size = rest.shape[0]

    def kernel(rest_ref, first_ref, own_ref, ih_ref, il_ref, inverses, work):
        own_ref[...] = rest_ref[...]
        eliminate(own_ref, inverses, work, range(1, 2))
        own_ref[0:BLOCK, BLOCK:size] = jnp.zeros((BLOCK, size - BLOCK), jnp.float32)
        ih_ref[...], il_ref[...] = tile_inverse(first_ref[0], inverses[1], own_ref[BLOCK:size, 0:BLOCK])

    inv = jax.ShapeDtypeStruct((size, size), jnp.bfloat16)
    return pl.pallas_call(
        kernel,
        name="factorize_last",
        out_shape=(jax.ShapeDtypeStruct((size, size), jnp.float32), inv, inv),
        in_specs=[vmem()] * 2,
        out_specs=(vmem(),) * 3,
        scratch_shapes=[
            pltpu.VMEM((size // BLOCK, BLOCK, BLOCK), jnp.float32),
            pltpu.VMEM((BLOCK, BLOCK), jnp.float32),
        ],
        compiler_params=pltpu.CompilerParams(vmem_limit_bytes=VMEM_BYTES),
    )(rest, first_inverse)


def solve(panels, factors):
    _, coded_rows, size = panels[0].shape
    thin, order = coded_rows - SCALE_ROWS, LEAD_TILES * size
    count = len(panels)

    def kernel(*refs):
        panel_refs = refs[:count]
        high_ref, low_ref, ih_ref, il_ref, last_ih_ref, last_il_ref = refs[count : count + 6]
        *out_refs, xh, xl = refs[count + 6 :]
        for q in range(LEAD_TILES):
            s, e = q * size, (q + 1) * size
            acc = jnp.concatenate([decode(ref[q]) for ref in panel_refs], axis=0)
            if q:
                acc = acc - nt3((xh[:, 0:s], xl[:, 0:s]), (high_ref[s:e, 0:s], low_ref[s:e, 0:s]))
            last = q == LEAD_TILES - 1
            inverse = (last_ih_ref[...], last_il_ref[...]) if last else (ih_ref[q], il_ref[q])
            x = nt3(split(acc), inverse)
            xh[:, s:e], xl[:, s:e] = split(x)
            for number, ref in enumerate(out_refs):
                ref[q] = encode(x[number * thin : (number + 1) * thin])

    return pl.pallas_call(
        kernel,
        name="solve",
        out_shape=(jax.ShapeDtypeStruct((LEAD_TILES, coded_rows, size), jnp.int16),) * count,
        in_specs=[vmem()] * (count + 6),
        out_specs=(vmem(),) * count,
        scratch_shapes=[pltpu.VMEM((count * thin, order), jnp.bfloat16)] * 2,
        compiler_params=pltpu.CompilerParams(vmem_limit_bytes=VMEM_BYTES),
    )(*panels, *factors)


def finish(ids, rows, cols, own, last_own, extended, front):
    size = own.shape[0]
    order = LEAD_TILES * size
    tile_rows, tile_cols = front.shape[:2]
    lanes = 128
    parts = size // lanes
    half = len(rows)

    def kernel(ids_ref, *refs):
        row_pieces, col_pieces = refs[:half], refs[half : 2 * half]
        own_ref, last_own_ref, ext_ref, front_ref, out_ref, xh, xl = refs[2 * half :]
        row, col = ids_ref[0], ids_ref[1]

        def put(a, b, tile):
            for part in range(parts):
                start = (a * size * tile_cols + b) * parts + part
                out_ref[pl.ds(start, size, stride=tile_cols * parts), :] = tile[:, part * lanes : (part + 1) * lanes]

        for pieces, place, first in ((row_pieces, col, 0), (col_pieces, row, tile_rows * size)):
            for ref, inner, chunk in pair_pieces(pieces, place):
                for q in range(LEAD_TILES):
                    value = decode(ref[inner, q])
                    thin = value.shape[0]
                    start = pl.multiple_of(first + chunk * thin, 32)
                    high, low = split(value)
                    xh[pl.ds(start, thin), q * size : (q + 1) * size] = high
                    xl[pl.ds(start, thin), q * size : (q + 1) * size] = low

        def take(ref, n):
            return ref[n * size : (n + 1) * size, :]

        def update(a, b, base):
            x, y = a, tile_rows + b
            put(a, b, base - nt3((take(xh, x), take(xl, x)), (take(xh, y), take(xl, y))))

        def put_panel(a):
            for q in range(LEAD_TILES):

                @pl.when(col == q)
                def _():
                    high = xh[a * size : (a + 1) * size, q * size : (q + 1) * size].astype(jnp.float32)
                    low = xl[a * size : (a + 1) * size, q * size : (q + 1) * size].astype(jnp.float32)
                    put(a, 0, high + low)

        zero = jnp.zeros((size, size), jnp.float32)
        for a, b in ((0, 1), (0, 2), (1, 2)):
            put(a, b, zero)
        in_panel = col < LEAD_TILES
        lead_row = row < LEAD_TILES
        last_tile = LEAD_TILES - 1
        put_panel(1)
        put_panel(2)

        @pl.when(jnp.logical_not(in_panel))
        def _():
            update(1, 0, ext_ref[0])
            update(2, 0, ext_ref[2])

        @pl.when(row < col)
        def _():
            put(0, 0, zero)
            put(1, 1, zero)
            put(2, 2, zero)

        @pl.when(row >= col)
        def _():
            @pl.when(lead_row)
            def _():
                put(0, 0, jnp.where((row == last_tile) & (col == last_tile), last_own_ref[...], own_ref[...]))

            @pl.when(jnp.logical_not(lead_row))
            def _():
                put_panel(0)

            @pl.when(jnp.logical_not(in_panel))
            def _():
                update(0, 0, front_ref[0, 0].astype(jnp.float32))

            update(1, 1, ext_ref[1])
            update(2, 2, ext_ref[4])

        update(2, 1, ext_ref[3])

    return pl.pallas_call(
        kernel,
        name="finish",
        out_shape=jax.ShapeDtypeStruct((tile_rows * size * tile_cols * parts, lanes), jnp.float32),
        in_specs=[smem()] + [vmem()] * (2 * half + 4),
        out_specs=vmem(),
        scratch_shapes=[pltpu.VMEM((2 * tile_rows * size, order), jnp.bfloat16)] * 2,
        compiler_params=pltpu.CompilerParams(vmem_limit_bytes=VMEM_BYTES),
    )(ids, *rows, *cols, own, last_own, extended, front)


def exchange(value, axis):
    return lax.all_to_all(value, axis, split_axis=0, concat_axis=0, tiled=True)


def permute(value, axis, target):
    return lax.ppermute(value, axis, [(i, target(i)) for i in range(lax.axis_size(axis))])


def ring_gather(value, axis):
    ring = lax.axis_size(axis) // 2
    half = value.shape[0] // 2

    def shift(array, steps):
        return permute(array, axis, lambda i: (i // 2 + steps) % ring * 2 + i % 2)

    before, after = shift(value, 1), shift(value, ring - 1)
    return (value, before, after, shift(before[:half], 1), shift(after[half:], ring - 1))


def ring_pieces(pieces, place, length):
    ring = len(pieces) - 1
    for ref, step, first in zip(pieces, (0, 1, 3, 2, 2), (0, 0, 0, 0, length // 2), strict=True):
        yield ref, first, lax.rem(place + (ring - step), ring)


def pair_gather(value, axis):
    partner = permute(value, axis, lambda i: i ^ 1)
    return ring_gather(jnp.stack([value, partner]), axis)


def pair_pieces(pieces, place):
    side = lax.rem(place, 2)
    for ref, first, source in ring_pieces(pieces, lax.div(place, 2), 2):
        for position in range(ref.shape[0]):
            yield ref, position, 2 * source + (side if first + position == 0 else 1 - side)


def per_device(front_matrix, contributions, target_front, target_row, target_col, live_count):
    _, tile_rows, _, size, tile_cols, _, _ = front_matrix.shape
    n_front, n_row, n_col = (lax.axis_size(name) for name in ("front", "row", "col"))
    slots = contributions.shape[3]
    front = front_matrix.reshape(tile_rows, size, tile_cols, size).transpose(0, 2, 1, 3)
    ids = jnp.stack([lax.axis_index("row"), lax.axis_index("col")]).astype(jnp.int32)

    ring = n_col // 2
    thin = size // ring
    chunks = jnp.repeat(front[0, 0].reshape(ring, thin, size), 2, axis=0)
    chunk = exchange(chunks, "col")[:LEAD_TILES]
    owners = range(LEAD_TILES)
    partner = lax.ppermute(chunk, "row", [(i, i ^ 1) for i in owners])
    pair = jnp.stack([chunk, partner])
    leading = [pair]
    for step in range(1, n_row // 2):
        leading.append(lax.ppermute(pair, "row", [(i, (i + 2 * step) % n_row) for i in owners]))

    packed = pack(
        contributions.reshape(slots, size, size),
        target_front.reshape(slots), target_row.reshape(slots), target_col.reshape(slots),
        live_count.reshape(1), n_front, n_row, n_col, tile_cols,
    )
    received = exchange(packed, ("front", "row"))

    lead = ring_gather(collect(ids, leading), "col")
    *factors, own, rest = factorize_first(ids, lead, size)
    received, rest = lax.optimization_barrier((received, rest))

    extended, panel = assemble(received, front, n_col)
    mine = exchange(panel, "col")[:LEAD_TILES]
    rest, first_inverse = factorize_next(rest)
    last_own, *last_inverse = factorize_last(rest, first_inverse)
    turned = lax.ppermute(
        mine, ("row", "col"), [(r * n_col + c, c * n_col + r) for r in range(n_row) for c in range(n_col)]
    )
    solved, turned = solve((mine, turned), (*factors, *last_inverse))
    rows = pair_gather(solved, "col")
    cols = pair_gather(turned, "row")
    factor = finish(ids, rows, cols, own, last_own, extended, front)
    return factor.reshape(1, tile_rows, 1, size, tile_cols, 1, size)


def solution(mesh):
    in_specs = (
        P("front", None, "row", None, None, "col", None),
        P("front", "row", "col", None, None, None),
        P("front", "row", "col", None),
        P("front", "row", "col", None),
        P("front", "row", "col", None),
        P("front", "row", "col"),
    )
    out_specs = P("front", None, "row", None, None, "col", None)
    return jax.shard_map(per_device, mesh=mesh, in_specs=in_specs, out_specs=out_specs, check_vma=False)
```

```python
import jax
import jax.numpy as jnp
from jax import lax
from jax.experimental import pallas as pl
from jax.experimental.pallas import tpu as pltpu
from jax.sharding import PartitionSpec as P


LEAD_TILES = 4
BLOCK = 128
HALF = 64
RUN = 32
STRIP = 8
VMEM_BYTES = 56 * 1024 * 1024


def vmem():
    return pl.BlockSpec(memory_space=pltpu.VMEM)


def smem():
    return pl.BlockSpec(memory_space=pltpu.SMEM)


def hbm():
    return pl.BlockSpec(memory_space=pl.ANY)


def nt(left, right, precision=None):
    return lax.dot_general(
        left, right, (((1,), (1,)), ((), ())), precision=precision, preferred_element_type=jnp.float32
    )


def split(value):
    high = value.astype(jnp.bfloat16)
    return high, (value - high.astype(jnp.float32)).astype(jnp.bfloat16)


def nt3(left, right):
    return nt(left[0], right[0]) + (nt(left[0], right[1]) + nt(left[1], right[0]))


NOTE_ROWS = 8


def pack(contributions, target_front, target_row, target_col, live_count, n_front, n_row, n_col, tile_cols):
    slots, size, _ = contributions.shape
    capacity = max(2, -(-slots // (n_front * n_row)))
    buckets = n_front * n_row * capacity
    kind = contributions.dtype

    def kernel(
        front_ref, row_ref, col_ref, live_ref, tiles_ref, packed_ref,
        counts, bucket_of, stage, notes, sems_in, sems_out, note_sem,
    ):
        live = live_ref[0]

        def fetch(slot):
            return pltpu.make_async_copy(tiles_ref.at[slot], stage.at[slot], sems_in.at[slot])

        def store(slot, bucket):
            return pltpu.make_async_copy(stage.at[slot], packed_ref.at[bucket, pl.ds(0, size)], sems_out.at[slot])

        def start(slot, carry):
            fetch(slot).start()
            return carry

        lax.fori_loop(0, live, start, 0)
        notes[...] = jnp.full(notes.shape, -1.0, kind)

        def clear(i, carry):
            counts[i] = 0
            return carry

        lax.fori_loop(0, n_front * n_row, clear, 0)

        def assign(slot, carry):
            row, col = row_ref[slot], col_ref[slot]
            destination = front_ref[slot] * n_row + lax.rem(row, n_row)
            position = counts[destination]
            counts[destination] = position + 1
            bucket = destination * capacity + position
            bucket_of[slot] = bucket
            target = lax.div(row, n_row) * tile_cols + lax.div(col, n_col)
            notes[bucket] = jnp.full(notes.shape[1:], target, jnp.int32).astype(jnp.float32).astype(kind)
            return carry

        lax.fori_loop(0, live, assign, 0)
        note_copy = pltpu.make_async_copy(notes, packed_ref.at[:, pl.ds(size, NOTE_ROWS)], note_sem)
        note_copy.start()

        def forward(slot, carry):
            fetch(slot).wait()
            store(slot, bucket_of[slot]).start()
            return carry

        lax.fori_loop(0, live, forward, 0)

        def drain(slot, carry):
            store(slot, bucket_of[slot]).wait()
            return carry

        lax.fori_loop(0, live, drain, 0)
        note_copy.wait()

    return pl.pallas_call(
        kernel,
        name="pack",
        out_shape=jax.ShapeDtypeStruct((buckets, size + NOTE_ROWS, size), kind),
        in_specs=[smem()] * 4 + [hbm()],
        out_specs=hbm(),
        scratch_shapes=[
            pltpu.SMEM((n_front * n_row,), jnp.int32),
            pltpu.SMEM((slots,), jnp.int32),
            pltpu.VMEM((slots, size, size), kind),
            pltpu.VMEM((buckets, NOTE_ROWS, size), kind),
            pltpu.SemaphoreType.DMA((slots,)),
            pltpu.SemaphoreType.DMA((slots,)),
            pltpu.SemaphoreType.DMA,
        ],
        compiler_params=pltpu.CompilerParams(vmem_limit_bytes=VMEM_BYTES),
    )(target_front, target_row, target_col, live_count, contributions)


SCALE_ROWS = 8
SCALE_STEPS = 64


def encode(values):
    n, m = values.shape
    top = jnp.max(jnp.abs(values), axis=1, keepdims=True)
    code = jnp.floor(jnp.log2(jnp.maximum(top, 2.0**-110)) * SCALE_STEPS) + 1.0
    coded = jnp.round(values * jnp.exp2(15.0 - 1e-3 - code / SCALE_STEPS))
    picked = lax.broadcasted_iota(jnp.int32, (n, m), 0) == lax.broadcasted_iota(jnp.int32, (n, m), 1)
    line = jnp.sum(jnp.where(picked, code, 0.0), axis=0, keepdims=True)
    lines = jnp.broadcast_to(line, (SCALE_ROWS, m))
    return jnp.concatenate([coded, lines], axis=0).astype(jnp.int32).astype(jnp.int16)


def decode(coded):
    wide = coded.astype(jnp.int32).astype(jnp.float32)
    n, m = wide.shape[0] - SCALE_ROWS, wide.shape[1]
    values, line = wide[:n], wide[n : n + 1]
    picked = lax.broadcasted_iota(jnp.int32, (n, m), 0) == lax.broadcasted_iota(jnp.int32, (n, m), 1)
    code = jnp.sum(jnp.where(picked, jnp.broadcast_to(line, (n, m)), 0.0), axis=1, keepdims=True)
    return values * jnp.exp2(code / SCALE_STEPS - 15.0 + 1e-3)


EXTENDED = ((1, 0), (1, 1), (2, 0), (2, 1), (2, 2))


def assemble(received, front, chunks):
    total, _, size = received.shape
    thin = front.shape[0] * size // chunks

    def kernel(
        received_ref, front_ref, ext_ref, panel_ref, landed, column, notes, numbers, arrived_ref, sems, note_sem
    ):
        note_copy = pltpu.make_async_copy(received_ref.at[:, pl.ds(size, NOTE_ROWS)], notes, note_sem)
        note_copy.start()

        def copy(i):
            return pltpu.make_async_copy(received_ref.at[i, pl.ds(0, size)], landed.at[i], sems.at[i])

        def fetch(i, carry):
            @pl.when(arrived_ref[i, 0] >= 0)
            def _():
                copy(i).start()

            return carry

        note_copy.wait()
        for i in range(total):
            numbers[i : i + 1, :] = notes[i, 0:1, 0 : numbers.shape[1]].astype(jnp.float32).astype(jnp.int32)
        number_copy = pltpu.make_async_copy(numbers, arrived_ref, note_sem)
        number_copy.start()
        for slot, (a, b) in enumerate(EXTENDED):
            ext_ref[slot] = front_ref[a, b].astype(jnp.float32)
        number_copy.wait()
        lax.fori_loop(0, total, fetch, 0)

        def add(i, carry):
            target = arrived_ref[i, 0]

            @pl.when(target >= 0)
            def _():
                copy(i).wait()
                slot = jnp.where(target >= 6, target - 4, target - 3)
                ext_ref[slot] = ext_ref[slot] + landed[i].astype(jnp.float32)

            return carry

        lax.fori_loop(0, total, add, 0)
        column[0:size] = front_ref[0, 0].astype(jnp.float32)
        column[size : 2 * size] = ext_ref[0]
        column[2 * size : 3 * size] = ext_ref[2]
        for chunk in range(chunks):
            panel_ref[chunk] = encode(column[chunk * thin : (chunk + 1) * thin, :])

    return pl.pallas_call(
        kernel,
        name="assemble",
        out_shape=(
            jax.ShapeDtypeStruct((len(EXTENDED), size, size), jnp.float32),
            jax.ShapeDtypeStruct((chunks, thin + SCALE_ROWS, size), jnp.int16),
        ),
        in_specs=[hbm(), vmem()],
        out_specs=(vmem(), vmem()),
        scratch_shapes=[
            pltpu.VMEM((total, size, size), jnp.bfloat16),
            pltpu.VMEM((3 * size, size), jnp.float32),
            pltpu.VMEM((total, NOTE_ROWS, size), jnp.bfloat16),
            pltpu.VMEM((total, 128), jnp.int32),
            pltpu.SMEM((total, 128), jnp.int32),
            pltpu.SemaphoreType.DMA((total,)),
            pltpu.SemaphoreType.DMA,
        ],
        compiler_params=pltpu.CompilerParams(vmem_limit_bytes=VMEM_BYTES),
    )(received, front)


def pick_lane(value, lane):
    index = jnp.full(value.shape, lane, jnp.int32)
    return jnp.take_along_axis(value, index, axis=1, mode="promise_in_bounds")


def factor_block(work):
    lanes = lax.broadcasted_iota(jnp.int32, (STRIP, BLOCK), 1)
    strip_rows = lax.broadcasted_iota(jnp.int32, (STRIP, BLOCK), 0)

    def spread(value, i):
        return jnp.broadcast_to(value[i : i + 1, :], value.shape)

    def step(number, top, bottom):
        base = pl.multiple_of(number * STRIP, STRIP)
        strip = work[pl.ds(base, STRIP), :]
        own = [pick_lane(strip, base + i) for i in range(STRIP)]
        whole = work[top:bottom, :]
        below = lax.broadcasted_iota(jnp.int32, whole.shape, 0) + top >= base + STRIP
        columns = [jnp.where(below, pick_lane(whole, base + i), 0.0) for i in range(STRIP)]
        for i in range(STRIP):
            pivot = spread(own[i], i)
            inverse = 1.0 / pivot
            factors = jnp.where(strip_rows > i, own[i] * inverse, 0.0)
            line = jnp.where(lanes == base + i, pivot + pivot, spread(strip, i))
            strip = strip - factors * line
            lower = columns[i] * jnp.broadcast_to(inverse[0:1], whole.shape)
            for j in range(i + 1, STRIP):
                entry = spread(own[j], i)
                own[j] = own[j] - factors * entry
                columns[j] = columns[j] - lower * jnp.broadcast_to(entry[0:1], whole.shape)
            whole = whole - lower * jnp.broadcast_to(line[0:1], whole.shape)
        work[top:bottom, :] = whole
        work[pl.ds(base, STRIP), :] = strip

    for first in range(0, BLOCK, HALF):
        last = first + HALF
        for top in range(first, last, RUN):

            def run(number, carry, top=top):
                step(number, top, last)
                return carry

            lax.fori_loop(top // STRIP, (top + RUN) // STRIP, run, 0)
        if last < BLOCK:
            done = work[first:last, :]
            at_pivot = lax.broadcasted_iota(jnp.int32, done.shape, 0) + first == lax.broadcasted_iota(
                jnp.int32, done.shape, 1
            )
            pivots = jnp.where(at_pivot, done, 0.0)
            scaled = done / jnp.sum(pivots, axis=1, keepdims=True)
            change = lax.dot_general(
                scaled, done + pivots, (((0,), (0,)), ((), ())),
                precision=lax.Precision.HIGHEST, preferred_element_type=jnp.float32,
            )
            work[last:BLOCK, :] = work[last:BLOCK, :] - change[last:BLOCK, :]


def eliminate(full, inverses, work, blocks):
    order = full.shape[0]
    r = lax.broadcasted_iota(jnp.int32, (BLOCK, BLOCK), 0)
    c = lax.broadcasted_iota(jnp.int32, (BLOCK, BLOCK), 1)
    for k in blocks:
        s, e = k * BLOCK, (k + 1) * BLOCK
        work[...] = full[s:e, s:e]
        factor_block(work)
        done = work[...]
        diagonal = jnp.where(r == c, done, 0.0)
        root = lax.rsqrt(jnp.sum(diagonal, axis=1, keepdims=True))
        inverse = jnp.where(r >= c, done, 0.0) * root * (1.0 / jnp.sum(diagonal, axis=0, keepdims=True))
        inverses[k] = inverse
        full[s:e, s:e] = (jnp.where(r <= c, done, 0.0) * root).T
        if e < order:
            panel = nt3(split(full[e:order, s:e]), split(inverse))
            full[e:order, s:e] = panel
            high, low = split(panel)
            for o in range(e, order, BLOCK):
                y = slice(o - e, o - e + BLOCK)
                full[o:order, o : o + BLOCK] = full[o:order, o : o + BLOCK] - nt3(
                    (high[o - e :], low[o - e :]), (high[y], low[y])
                )


def tile_inverse(first, second, between):
    def product(left, right):
        return jnp.dot(left, right, precision=lax.Precision.HIGHEST, preferred_element_type=jnp.float32)

    corner = -product(second, product(between, first))
    above = jnp.concatenate([first, jnp.zeros_like(first)], axis=1)
    return split(jnp.concatenate([above, jnp.concatenate([corner, second], axis=1)], axis=0))


PAIRS = tuple((i, j) for i in range(LEAD_TILES) for j in range(i + 1))


def collect(ids, pairs):
    _, _, thin, size = pairs[0].shape
    ring = len(pairs)

    def kernel(ids_ref, *refs):
        *pair_refs, out_ref, sems = refs
        place, side = lax.div(ids_ref[0], 2), lax.rem(ids_ref[0], 2)
        copies = []
        for i in range(LEAD_TILES):
            first = PAIRS.index((i, 0))
            inner = lax.rem(side + i, 2)
            steps = lax.rem(place - i // 2 + ring, ring)

            def copy(ref, i=i, first=first, inner=inner):
                return pltpu.make_async_copy(
                    ref.at[inner, pl.ds(0, i + 1)], out_ref.at[pl.ds(first, i + 1)], sems.at[i]
                )

            for s in range(ring):

                @pl.when(steps == s)
                def _():
                    copy(pair_refs[s]).start()

            copies.append(copy(pair_refs[0]))
        for one in copies:
            one.wait()

    return pl.pallas_call(
        kernel,
        name="collect",
        out_shape=jax.ShapeDtypeStruct((len(PAIRS), thin, size), pairs[0].dtype),
        in_specs=[smem()] + [hbm()] * ring,
        out_specs=vmem(),
        scratch_shapes=[pltpu.SemaphoreType.DMA((LEAD_TILES,))],
    )(ids, *pairs)


FIRST_TILES = 2


def columns_out(full, inverses, tiles, high_ref, low_ref, ih_ref, il_ref, rest_ref):
    order = full.shape[0]
    size = ih_ref.shape[1]
    half = size // BLOCK
    for q in range(tiles):
        s, e = q * size, (q + 1) * size
        full[s : s + BLOCK, s + BLOCK : e] = jnp.zeros((BLOCK, size - BLOCK), jnp.float32)
        ih_ref[q], il_ref[q] = tile_inverse(inverses[q * half], inverses[q * half + 1], full[s + BLOCK : e, s : s + BLOCK])
        if e < order:
            high_ref[e:order, s:e], low_ref[e:order, s:e] = split(full[e:order, s:e])
    done = tiles * size
    rest_ref[...] = full[done:order, done:order]


def columns_shapes(order, tiles, size):
    wide = jax.ShapeDtypeStruct((order, tiles * size), jnp.bfloat16)
    inv = jax.ShapeDtypeStruct((tiles, size, size), jnp.bfloat16)
    left = order - tiles * size
    return (wide, wide, inv, inv, jax.ShapeDtypeStruct((left, left), jnp.float32))


def columns_scratch(order, tiles, size):
    return [
        pltpu.VMEM((order, order), jnp.float32),
        pltpu.VMEM((tiles * size // BLOCK, BLOCK, BLOCK), jnp.float32),
        pltpu.VMEM((BLOCK, BLOCK), jnp.float32),
    ]


def factorize_first(ids, lead, size):
    order = LEAD_TILES * size

    def kernel(ids_ref, *refs):
        *pieces, high_ref, low_ref, ih_ref, il_ref, rest_ref, own_ref, full, inverses, work = refs
        for ref, first, source in ring_pieces(pieces, lax.div(ids_ref[1], 2), len(PAIRS)):
            for number in range(ref.shape[0]):
                i, j = PAIRS[first + number]
                tile = ref[number].astype(jnp.float32)
                thin = tile.shape[0]
                start = pl.multiple_of(i * size + source * thin, thin)
                full[pl.ds(start, thin), j * size : (j + 1) * size] = tile
        eliminate(full, inverses, work, range(FIRST_TILES * size // BLOCK))
        columns_out(full, inverses, FIRST_TILES, high_ref, low_ref, ih_ref, il_ref, rest_ref)
        for i, j in PAIRS:
            if j < FIRST_TILES:

                @pl.when((ids_ref[0] == i) & (ids_ref[1] == j))
                def _():
                    own_ref[...] = full[i * size : (i + 1) * size, j * size : (j + 1) * size]

    return pl.pallas_call(
        kernel,
        name="factorize_first",
        out_shape=(*columns_shapes(order, FIRST_TILES, size), jax.ShapeDtypeStruct((size, size), jnp.float32)),
        in_specs=[smem()] + [vmem()] * len(lead),
        out_specs=(vmem(),) * 6,
        scratch_shapes=columns_scratch(order, FIRST_TILES, size),
        compiler_params=pltpu.CompilerParams(vmem_limit_bytes=VMEM_BYTES),
    )(ids, *lead)


def factorize_second(rest, size):
    order = rest.shape[0]

    def kernel(rest_ref, high_ref, low_ref, ih_ref, il_ref, out_ref, column_ref, full, inverses, work):
        full[...] = rest_ref[...]
        eliminate(full, inverses, work, range(size // BLOCK))
        columns_out(full, inverses, 1, high_ref, low_ref, ih_ref, il_ref, out_ref)
        column_ref[...] = full[:, 0:size]

    return pl.pallas_call(
        kernel,
        name="factorize_second",
        out_shape=(*columns_shapes(order, 1, size), jax.ShapeDtypeStruct((order, size), jnp.float32)),
        in_specs=[vmem()],
        out_specs=(vmem(),) * 6,
        scratch_shapes=columns_scratch(order, 1, size),
        compiler_params=pltpu.CompilerParams(vmem_limit_bytes=VMEM_BYTES),
    )(rest)


def factorize_next(rest):
    def kernel(rest_ref, out_ref, inverses, work):
        out_ref[...] = rest_ref[...]
        eliminate(out_ref, inverses, work, range(1))

    return pl.pallas_call(
        kernel,
        name="factorize_next",
        out_shape=(
            jax.ShapeDtypeStruct(rest.shape, jnp.float32),
            jax.ShapeDtypeStruct((1, BLOCK, BLOCK), jnp.float32),
        ),
        in_specs=[vmem()],
        out_specs=(vmem(),) * 2,
        scratch_shapes=[pltpu.VMEM((BLOCK, BLOCK), jnp.float32)],
        compiler_params=pltpu.CompilerParams(vmem_limit_bytes=VMEM_BYTES),
    )(rest)


def factorize_last(rest, first_inverse):
    size = rest.shape[0]

    def kernel(rest_ref, first_ref, own_ref, ih_ref, il_ref, inverses, work):
        own_ref[...] = rest_ref[...]
        eliminate(own_ref, inverses, work, range(1, 2))
        own_ref[0:BLOCK, BLOCK:size] = jnp.zeros((BLOCK, size - BLOCK), jnp.float32)
        ih_ref[...], il_ref[...] = tile_inverse(first_ref[0], inverses[1], own_ref[BLOCK:size, 0:BLOCK])

    inv = jax.ShapeDtypeStruct((size, size), jnp.bfloat16)
    return pl.pallas_call(
        kernel,
        name="factorize_last",
        out_shape=(jax.ShapeDtypeStruct((size, size), jnp.float32), inv, inv),
        in_specs=[vmem()] * 2,
        out_specs=(vmem(),) * 3,
        scratch_shapes=[
            pltpu.VMEM((size // BLOCK, BLOCK, BLOCK), jnp.float32),
            pltpu.VMEM((BLOCK, BLOCK), jnp.float32),
        ],
        compiler_params=pltpu.CompilerParams(vmem_limit_bytes=VMEM_BYTES),
    )(rest, first_inverse)


def solve(panels, first, second, last):
    _, coded_rows, size = panels[0].shape
    thin, order = coded_rows - SCALE_ROWS, LEAD_TILES * size
    count = len(panels)
    inner = FIRST_TILES * size

    def kernel(*refs):
        panel_refs = refs[:count]
        high1, low1, ih1, il1, high2, low2, ih2, il2, ih3, il3 = refs[count : count + 10]
        *out_refs, xh, xl = refs[count + 10 :]
        for q in range(LEAD_TILES):
            s, e = q * size, (q + 1) * size
            acc = jnp.concatenate([decode(ref[q]) for ref in panel_refs], axis=0)
            if q:
                k = min(s, inner)
                acc = acc - nt3((xh[:, 0:k], xl[:, 0:k]), (high1[s:e, 0:k], low1[s:e, 0:k]))
            if s > inner:
                y = slice(s - inner, e - inner)
                acc = acc - nt3((xh[:, inner:s], xl[:, inner:s]), (high2[y, :], low2[y, :]))
            if q < FIRST_TILES:
                inverse = (ih1[q], il1[q])
            elif q == FIRST_TILES:
                inverse = (ih2[0], il2[0])
            else:
                inverse = (ih3[...], il3[...])
            x = nt3(split(acc), inverse)
            if e < order:
                xh[:, s:e], xl[:, s:e] = split(x)
            for number in range(count):
                out_refs[number // 2][number % 2, q] = encode(x[number * thin : (number + 1) * thin])

    return pl.pallas_call(
        kernel,
        name="solve",
        out_shape=(jax.ShapeDtypeStruct((2, LEAD_TILES, coded_rows, size), jnp.int16),) * (count // 2),
        in_specs=[vmem()] * (count + 10),
        out_specs=(vmem(),) * (count // 2),
        scratch_shapes=[pltpu.VMEM((count * thin, order - size), jnp.bfloat16)] * 2,
        compiler_params=pltpu.CompilerParams(vmem_limit_bytes=VMEM_BYTES),
    )(*panels, *first, *second, *last)


def finish(ids, rows, cols, own, column, last_own, extended, front):
    size = own.shape[0]
    order = LEAD_TILES * size
    tile_rows, tile_cols = front.shape[:2]
    lanes = 128
    parts = size // lanes
    half = len(rows)

    def kernel(ids_ref, *refs):
        row_pieces, col_pieces = refs[:half], refs[half : 2 * half]
        own_ref, column_ref, last_own_ref, ext_ref, front_ref, out_ref, xh, xl = refs[2 * half :]
        row, col = ids_ref[0], ids_ref[1]

        def put(a, b, tile):
            for part in range(parts):
                start = (a * size * tile_cols + b) * parts + part
                out_ref[pl.ds(start, size, stride=tile_cols * parts), :] = tile[:, part * lanes : (part + 1) * lanes]

        for pieces, place, first in ((row_pieces, col, 0), (col_pieces, row, tile_rows * size)):
            for ref, inner, chunk in pair_pieces(pieces, place):
                for q in range(LEAD_TILES):
                    value = decode(ref[inner, q])
                    thin = value.shape[0]
                    start = pl.multiple_of(first + chunk * thin, 32)
                    high, low = split(value)
                    xh[pl.ds(start, thin), q * size : (q + 1) * size] = high
                    xl[pl.ds(start, thin), q * size : (q + 1) * size] = low

        def take(ref, n):
            return ref[n * size : (n + 1) * size, :]

        def update(a, b, base):
            x, y = a, tile_rows + b
            put(a, b, base - nt3((take(xh, x), take(xl, x)), (take(xh, y), take(xl, y))))

        def put_panel(a):
            for q in range(LEAD_TILES):

                @pl.when(col == q)
                def _():
                    high = xh[a * size : (a + 1) * size, q * size : (q + 1) * size].astype(jnp.float32)
                    low = xl[a * size : (a + 1) * size, q * size : (q + 1) * size].astype(jnp.float32)
                    put(a, 0, high + low)

        zero = jnp.zeros((size, size), jnp.float32)
        for a, b in ((0, 1), (0, 2), (1, 2)):
            put(a, b, zero)
        in_panel = col < LEAD_TILES
        lead_row = row < LEAD_TILES
        last_tile = LEAD_TILES - 1
        put_panel(1)
        put_panel(2)

        @pl.when(jnp.logical_not(in_panel))
        def _():
            update(1, 0, ext_ref[0])
            update(2, 0, ext_ref[2])

        @pl.when(row < col)
        def _():
            put(0, 0, zero)
            put(1, 1, zero)
            put(2, 2, zero)

        @pl.when(row >= col)
        def _():
            @pl.when(lead_row)
            def _():
                start = pl.multiple_of(jnp.clip(row - FIRST_TILES, 0, 1) * size, size)
                late = jnp.where(col == last_tile, last_own_ref[...], column_ref[pl.ds(start, size), :])
                put(0, 0, jnp.where(col < FIRST_TILES, own_ref[...], late))

            @pl.when(jnp.logical_not(lead_row))
            def _():
                put_panel(0)

            @pl.when(jnp.logical_not(in_panel))
            def _():
                update(0, 0, front_ref[0, 0].astype(jnp.float32))

            update(1, 1, ext_ref[1])
            update(2, 2, ext_ref[4])

        update(2, 1, ext_ref[3])

    return pl.pallas_call(
        kernel,
        name="finish",
        out_shape=jax.ShapeDtypeStruct((tile_rows * size * tile_cols * parts, lanes), jnp.float32),
        in_specs=[smem()] + [vmem()] * (2 * half + 5),
        out_specs=vmem(),
        scratch_shapes=[pltpu.VMEM((2 * tile_rows * size, order), jnp.bfloat16)] * 2,
        compiler_params=pltpu.CompilerParams(vmem_limit_bytes=VMEM_BYTES),
    )(ids, *rows, *cols, own, column, last_own, extended, front)


def exchange(value, axis):
    return lax.all_to_all(value, axis, split_axis=0, concat_axis=0, tiled=True)


def permute(value, axis, target):
    return lax.ppermute(value, axis, [(i, target(i)) for i in range(lax.axis_size(axis))])


def ring_gather(value, axis):
    ring = lax.axis_size(axis) // 2
    half = value.shape[0] // 2

    def shift(array, steps):
        return permute(array, axis, lambda i: (i // 2 + steps) % ring * 2 + i % 2)

    before, after = shift(value, 1), shift(value, ring - 1)
    return (value, before, after, shift(before[:half], 1), shift(after[half:], ring - 1))


def ring_pieces(pieces, place, length):
    ring = len(pieces) - 1
    for ref, step, first in zip(pieces, (0, 1, 3, 2, 2), (0, 0, 0, 0, length // 2), strict=True):
        yield ref, first, lax.rem(place + (ring - step), ring)


def pair_pieces(pieces, place):
    side = lax.rem(place, 2)
    for ref, first, source in ring_pieces(pieces, lax.div(place, 2), 2):
        for position in range(ref.shape[0]):
            yield ref, position, 2 * source + (side if first + position == 0 else 1 - side)


def per_device(front_matrix, contributions, target_front, target_row, target_col, live_count):
    _, tile_rows, _, size, tile_cols, _, _ = front_matrix.shape
    n_front, n_row, n_col = (lax.axis_size(name) for name in ("front", "row", "col"))
    slots = contributions.shape[3]
    front = front_matrix.reshape(tile_rows, size, tile_cols, size).transpose(0, 2, 1, 3)
    ids = jnp.stack([lax.axis_index("row"), lax.axis_index("col")]).astype(jnp.int32)

    ring = n_col // 2
    thin = size // ring
    chunks = jnp.repeat(front[0, 0].reshape(ring, thin, size), 2, axis=0)
    chunk = exchange(chunks, "col")[:LEAD_TILES]
    owners = range(LEAD_TILES)
    partner = lax.ppermute(chunk, "row", [(i, i ^ 1) for i in owners])
    pair = jnp.stack([chunk, partner])
    leading = [pair]
    for step in range(1, n_row // 2):
        leading.append(lax.ppermute(pair, "row", [(i, (i + 2 * step) % n_row) for i in owners]))

    packed = pack(
        contributions.reshape(slots, size, size),
        target_front.reshape(slots), target_row.reshape(slots), target_col.reshape(slots),
        live_count.reshape(1), n_front, n_row, n_col, tile_cols,
    )
    received = exchange(packed, ("front", "row"))

    lead = ring_gather(collect(ids, leading), "col")
    *first, rest, own = factorize_first(ids, lead, size)
    received, rest = lax.optimization_barrier((received, rest))

    extended, panel = assemble(received, front, n_col)
    mine = exchange(panel, "col")[:LEAD_TILES]
    *second, rest, column = factorize_second(rest, size)
    turned = lax.ppermute(
        mine, ("row", "col"), [(r * n_col + c, c * n_col + r) for r in range(n_row) for c in range(n_col)]
    )
    beside = permute(mine, "col", lambda i: i ^ 1)
    rest, first_inverse = factorize_next(rest)
    turned_beside = permute(turned, "row", lambda i: i ^ 1)
    last_own, *last = factorize_last(rest, first_inverse)
    row_pair, col_pair = solve((mine, beside, turned, turned_beside), first, second, last)
    rows = ring_gather(row_pair, "col")
    cols = ring_gather(col_pair, "row")
    factor = finish(ids, rows, cols, own, column, last_own, extended, front)
    return factor.reshape(1, tile_rows, 1, size, tile_cols, 1, size)


def solution(mesh):
    in_specs = (
        P("front", None, "row", None, None, "col", None),
        P("front", "row", "col", None, None, None),
        P("front", "row", "col", None),
        P("front", "row", "col", None),
        P("front", "row", "col", None),
        P("front", "row", "col"),
    )
    out_specs = P("front", None, "row", None, None, "col", None)
    return jax.shard_map(per_device, mesh=mesh, in_specs=in_specs, out_specs=out_specs, check_vma=False)
```

```python
import jax
import jax.numpy as jnp
from jax import lax
from jax.experimental import pallas as pl
from jax.experimental.pallas import tpu as pltpu
from jax.sharding import PartitionSpec as P


LEAD_TILES = 4
BLOCK = 128
HALF = 64
RUN = 32
STRIP = 8
VMEM_BYTES = 56 * 1024 * 1024


def vmem():
    return pl.BlockSpec(memory_space=pltpu.VMEM)


def smem():
    return pl.BlockSpec(memory_space=pltpu.SMEM)


def hbm():
    return pl.BlockSpec(memory_space=pl.ANY)


def nt(left, right, precision=None):
    return lax.dot_general(
        left, right, (((1,), (1,)), ((), ())), precision=precision, preferred_element_type=jnp.float32
    )


def split(value):
    high = value.astype(jnp.bfloat16)
    return high, (value - high.astype(jnp.float32)).astype(jnp.bfloat16)


def nt3(left, right):
    return nt(left[0], right[0]) + (nt(left[0], right[1]) + nt(left[1], right[0]))


NOTE_ROWS = 8


def pack(contributions, target_front, target_row, target_col, live_count, n_front, n_row, n_col, tile_cols):
    slots, size, _ = contributions.shape
    capacity = max(2, -(-slots // (n_front * n_row)))
    buckets = n_front * n_row * capacity
    kind = contributions.dtype

    def kernel(
        front_ref, row_ref, col_ref, live_ref, tiles_ref, packed_ref,
        counts, bucket_of, stage, notes, sems_in, sems_out, note_sem,
    ):
        live = live_ref[0]

        def fetch(slot):
            return pltpu.make_async_copy(tiles_ref.at[slot], stage.at[slot], sems_in.at[slot])

        def store(slot, bucket):
            return pltpu.make_async_copy(stage.at[slot], packed_ref.at[bucket, pl.ds(0, size)], sems_out.at[slot])

        def start(slot, carry):
            fetch(slot).start()
            return carry

        lax.fori_loop(0, live, start, 0)
        notes[...] = jnp.full(notes.shape, -1.0, kind)

        def clear(i, carry):
            counts[i] = 0
            return carry

        lax.fori_loop(0, n_front * n_row, clear, 0)

        def assign(slot, carry):
            row, col = row_ref[slot], col_ref[slot]
            destination = front_ref[slot] * n_row + lax.rem(row, n_row)
            position = counts[destination]
            counts[destination] = position + 1
            bucket = destination * capacity + position
            bucket_of[slot] = bucket
            target = lax.div(row, n_row) * tile_cols + lax.div(col, n_col)
            notes[bucket] = jnp.full(notes.shape[1:], target, jnp.int32).astype(jnp.float32).astype(kind)
            return carry

        lax.fori_loop(0, live, assign, 0)
        note_copy = pltpu.make_async_copy(notes, packed_ref.at[:, pl.ds(size, NOTE_ROWS)], note_sem)
        note_copy.start()

        def forward(slot, carry):
            fetch(slot).wait()
            store(slot, bucket_of[slot]).start()
            return carry

        lax.fori_loop(0, live, forward, 0)

        def drain(slot, carry):
            store(slot, bucket_of[slot]).wait()
            return carry

        lax.fori_loop(0, live, drain, 0)
        note_copy.wait()

    return pl.pallas_call(
        kernel,
        name="pack",
        out_shape=jax.ShapeDtypeStruct((buckets, size + NOTE_ROWS, size), kind),
        in_specs=[smem()] * 4 + [hbm()],
        out_specs=hbm(),
        scratch_shapes=[
            pltpu.SMEM((n_front * n_row,), jnp.int32),
            pltpu.SMEM((slots,), jnp.int32),
            pltpu.VMEM((slots, size, size), kind),
            pltpu.VMEM((buckets, NOTE_ROWS, size), kind),
            pltpu.SemaphoreType.DMA((slots,)),
            pltpu.SemaphoreType.DMA((slots,)),
            pltpu.SemaphoreType.DMA,
        ],
        compiler_params=pltpu.CompilerParams(vmem_limit_bytes=VMEM_BYTES),
    )(target_front, target_row, target_col, live_count, contributions)


SCALE_ROWS = 8
SCALE_STEPS = 64


def encode(values):
    n, m = values.shape
    top = jnp.max(jnp.abs(values), axis=1, keepdims=True)
    code = jnp.floor(jnp.log2(jnp.maximum(top, 2.0**-110)) * SCALE_STEPS) + 1.0
    coded = jnp.round(values * jnp.exp2(15.0 - 1e-3 - code / SCALE_STEPS))
    picked = lax.broadcasted_iota(jnp.int32, (n, m), 0) == lax.broadcasted_iota(jnp.int32, (n, m), 1)
    line = jnp.sum(jnp.where(picked, code, 0.0), axis=0, keepdims=True)
    lines = jnp.broadcast_to(line, (SCALE_ROWS, m))
    return jnp.concatenate([coded, lines], axis=0).astype(jnp.int32).astype(jnp.int16)


def decode(coded):
    wide = coded.astype(jnp.int32).astype(jnp.float32)
    n, m = wide.shape[0] - SCALE_ROWS, wide.shape[1]
    values, line = wide[:n], wide[n : n + 1]
    picked = lax.broadcasted_iota(jnp.int32, (n, m), 0) == lax.broadcasted_iota(jnp.int32, (n, m), 1)
    code = jnp.sum(jnp.where(picked, jnp.broadcast_to(line, (n, m)), 0.0), axis=1, keepdims=True)
    return values * jnp.exp2(code / SCALE_STEPS - 15.0 + 1e-3)


EXTENDED = ((1, 0), (1, 1), (2, 0), (2, 1), (2, 2))


def assemble(received, front, chunks):
    total, _, size = received.shape
    thin = front.shape[0] * size // chunks

    def kernel(
        received_ref, front_ref, ext_ref, panel_ref, landed, column, notes, numbers, arrived_ref, sems, note_sem
    ):
        note_copy = pltpu.make_async_copy(received_ref.at[:, pl.ds(size, NOTE_ROWS)], notes, note_sem)
        note_copy.start()

        def copy(i):
            return pltpu.make_async_copy(received_ref.at[i, pl.ds(0, size)], landed.at[i], sems.at[i])

        for i in range(total):
            copy(i).start()
        note_copy.wait()
        for i in range(total):
            numbers[i : i + 1, :] = notes[i, 0:1, 0 : numbers.shape[1]].astype(jnp.float32).astype(jnp.int32)
        number_copy = pltpu.make_async_copy(numbers, arrived_ref, note_sem)
        number_copy.start()
        for slot, (a, b) in enumerate(EXTENDED):
            ext_ref[slot] = front_ref[a, b].astype(jnp.float32)
        number_copy.wait()

        def add(i, carry):
            target = arrived_ref[i, 0]
            copy(i).wait()

            @pl.when(target >= 0)
            def _():
                slot = jnp.where(target >= 6, target - 4, target - 3)
                ext_ref[slot] = ext_ref[slot] + landed[i].astype(jnp.float32)

            return carry

        lax.fori_loop(0, total, add, 0)
        column[0:size] = front_ref[0, 0].astype(jnp.float32)
        column[size : 2 * size] = ext_ref[0]
        column[2 * size : 3 * size] = ext_ref[2]
        for chunk in range(chunks):
            panel_ref[chunk] = encode(column[chunk * thin : (chunk + 1) * thin, :])

    return pl.pallas_call(
        kernel,
        name="assemble",
        out_shape=(
            jax.ShapeDtypeStruct((len(EXTENDED), size, size), jnp.float32),
            jax.ShapeDtypeStruct((chunks, thin + SCALE_ROWS, size), jnp.int16),
        ),
        in_specs=[hbm(), vmem()],
        out_specs=(vmem(), vmem()),
        scratch_shapes=[
            pltpu.VMEM((total, size, size), jnp.bfloat16),
            pltpu.VMEM((3 * size, size), jnp.float32),
            pltpu.VMEM((total, NOTE_ROWS, size), jnp.bfloat16),
            pltpu.VMEM((total, 128), jnp.int32),
            pltpu.SMEM((total, 128), jnp.int32),
            pltpu.SemaphoreType.DMA((total,)),
            pltpu.SemaphoreType.DMA,
        ],
        compiler_params=pltpu.CompilerParams(vmem_limit_bytes=VMEM_BYTES),
    )(received, front)


def pick_lane(value, lane):
    index = jnp.full(value.shape, lane, jnp.int32)
    return jnp.take_along_axis(value, index, axis=1, mode="promise_in_bounds")


def factor_block(work):
    lanes = lax.broadcasted_iota(jnp.int32, (STRIP, BLOCK), 1)
    strip_rows = lax.broadcasted_iota(jnp.int32, (STRIP, BLOCK), 0)

    def spread(value, i):
        return jnp.broadcast_to(value[i : i + 1, :], value.shape)

    def step(number, top, bottom):
        base = pl.multiple_of(number * STRIP, STRIP)
        strip = work[pl.ds(base, STRIP), :]
        own = [pick_lane(strip, base + i) for i in range(STRIP)]
        whole = work[top:bottom, :]
        below = lax.broadcasted_iota(jnp.int32, whole.shape, 0) + top >= base + STRIP
        columns = [jnp.where(below, pick_lane(whole, base + i), 0.0) for i in range(STRIP)]
        for i in range(STRIP):
            pivot = spread(own[i], i)
            inverse = 1.0 / pivot
            factors = jnp.where(strip_rows > i, own[i] * inverse, 0.0)
            line = jnp.where(lanes == base + i, pivot + pivot, spread(strip, i))
            strip = strip - factors * line
            lower = columns[i] * jnp.broadcast_to(inverse[0:1], whole.shape)
            for j in range(i + 1, STRIP):
                entry = spread(own[j], i)
                own[j] = own[j] - factors * entry
                columns[j] = columns[j] - lower * jnp.broadcast_to(entry[0:1], whole.shape)
            whole = whole - lower * jnp.broadcast_to(line[0:1], whole.shape)
        work[top:bottom, :] = whole
        work[pl.ds(base, STRIP), :] = strip

    for first in range(0, BLOCK, HALF):
        last = first + HALF
        for top in range(first, last, RUN):

            def run(number, carry, top=top):
                step(number, top, last)
                return carry

            lax.fori_loop(top // STRIP, (top + RUN) // STRIP, run, 0)
        if last < BLOCK:
            done = work[first:last, :]
            at_pivot = lax.broadcasted_iota(jnp.int32, done.shape, 0) + first == lax.broadcasted_iota(
                jnp.int32, done.shape, 1
            )
            pivots = jnp.where(at_pivot, done, 0.0)
            scaled = done / jnp.sum(pivots, axis=1, keepdims=True)
            change = lax.dot_general(
                scaled, done + pivots, (((0,), (0,)), ((), ())),
                precision=lax.Precision.HIGHEST, preferred_element_type=jnp.float32,
            )
            work[last:BLOCK, :] = work[last:BLOCK, :] - change[last:BLOCK, :]


def eliminate(full, inverses, work, blocks):
    order = full.shape[0]
    r = lax.broadcasted_iota(jnp.int32, (BLOCK, BLOCK), 0)
    c = lax.broadcasted_iota(jnp.int32, (BLOCK, BLOCK), 1)
    for k in blocks:
        s, e = k * BLOCK, (k + 1) * BLOCK
        work[...] = full[s:e, s:e]
        factor_block(work)
        done = work[...]
        diagonal = jnp.where(r == c, done, 0.0)
        root = lax.rsqrt(jnp.sum(diagonal, axis=1, keepdims=True))
        inverse = jnp.where(r >= c, done, 0.0) * root * (1.0 / jnp.sum(diagonal, axis=0, keepdims=True))
        inverses[k] = inverse
        full[s:e, s:e] = (jnp.where(r <= c, done, 0.0) * root).T
        if e < order:
            panel = nt3(split(full[e:order, s:e]), split(inverse))
            full[e:order, s:e] = panel
            high, low = split(panel)
            for o in range(e, order, BLOCK):
                y = slice(o - e, o - e + BLOCK)
                full[o:order, o : o + BLOCK] = full[o:order, o : o + BLOCK] - nt3(
                    (high[o - e :], low[o - e :]), (high[y], low[y])
                )


def tile_inverse(first, second, between):
    def product(left, right):
        return jnp.dot(left, right, precision=lax.Precision.HIGHEST, preferred_element_type=jnp.float32)

    corner = -product(second, product(between, first))
    above = jnp.concatenate([first, jnp.zeros_like(first)], axis=1)
    return split(jnp.concatenate([above, jnp.concatenate([corner, second], axis=1)], axis=0))


PAIRS = tuple((i, j) for i in range(LEAD_TILES) for j in range(i + 1))


def collect(ids, pairs):
    _, _, thin, size = pairs[0].shape
    ring = len(pairs)

    def kernel(ids_ref, *refs):
        *pair_refs, out_ref, sems = refs
        place, side = lax.div(ids_ref[0], 2), lax.rem(ids_ref[0], 2)
        copies = []
        for i in range(LEAD_TILES):
            first = PAIRS.index((i, 0))
            inner = lax.rem(side + i, 2)
            steps = lax.rem(place - i // 2 + ring, ring)

            def copy(ref, i=i, first=first, inner=inner):
                return pltpu.make_async_copy(
                    ref.at[inner, pl.ds(0, i + 1)], out_ref.at[pl.ds(first, i + 1)], sems.at[i]
                )

            for s in range(ring):

                @pl.when(steps == s)
                def _():
                    copy(pair_refs[s]).start()

            copies.append(copy(pair_refs[0]))
        for one in copies:
            one.wait()

    return pl.pallas_call(
        kernel,
        name="collect",
        out_shape=jax.ShapeDtypeStruct((len(PAIRS), thin, size), pairs[0].dtype),
        in_specs=[smem()] + [hbm()] * ring,
        out_specs=vmem(),
        scratch_shapes=[pltpu.SemaphoreType.DMA((LEAD_TILES,))],
    )(ids, *pairs)


FIRST_TILES = 2


def columns_out(full, inverses, tiles, high_ref, low_ref, ih_ref, il_ref, rest_ref):
    order = full.shape[0]
    size = ih_ref.shape[1]
    half = size // BLOCK
    for q in range(tiles):
        s, e = q * size, (q + 1) * size
        full[s : s + BLOCK, s + BLOCK : e] = jnp.zeros((BLOCK, size - BLOCK), jnp.float32)
        ih_ref[q], il_ref[q] = tile_inverse(inverses[q * half], inverses[q * half + 1], full[s + BLOCK : e, s : s + BLOCK])
        if e < order:
            high_ref[e:order, s:e], low_ref[e:order, s:e] = split(full[e:order, s:e])
    done = tiles * size
    rest_ref[...] = full[done:order, done:order]


def columns_shapes(order, tiles, size):
    wide = jax.ShapeDtypeStruct((order, tiles * size), jnp.bfloat16)
    inv = jax.ShapeDtypeStruct((tiles, size, size), jnp.bfloat16)
    left = order - tiles * size
    return (wide, wide, inv, inv, jax.ShapeDtypeStruct((left, left), jnp.float32))


def columns_scratch(order, tiles, size):
    return [
        pltpu.VMEM((order, order), jnp.float32),
        pltpu.VMEM((tiles * size // BLOCK + 1, BLOCK, BLOCK), jnp.float32),
        pltpu.VMEM((BLOCK, BLOCK), jnp.float32),
    ]


def factorize_first(ids, lead, size):
    order = LEAD_TILES * size

    def kernel(ids_ref, *refs):
        *pieces, high_ref, low_ref, ih_ref, il_ref, rest_ref, own_ref, begun_ref, full, inverses, work = refs
        for ref, first, source in ring_pieces(pieces, lax.div(ids_ref[1], 2), len(PAIRS)):
            for number in range(ref.shape[0]):
                i, j = PAIRS[first + number]
                tile = ref[number].astype(jnp.float32)
                thin = tile.shape[0]
                start = pl.multiple_of(i * size + source * thin, thin)
                full[pl.ds(start, thin), j * size : (j + 1) * size] = tile
        steps = FIRST_TILES * size // BLOCK
        eliminate(full, inverses, work, range(steps + 1))
        begun_ref[...] = inverses[steps]
        columns_out(full, inverses, FIRST_TILES, high_ref, low_ref, ih_ref, il_ref, rest_ref)
        for i, j in PAIRS:
            if j < FIRST_TILES:

                @pl.when((ids_ref[0] == i) & (ids_ref[1] == j))
                def _():
                    own_ref[...] = full[i * size : (i + 1) * size, j * size : (j + 1) * size]

    return pl.pallas_call(
        kernel,
        name="factorize_first",
        out_shape=(
            *columns_shapes(order, FIRST_TILES, size),
            jax.ShapeDtypeStruct((size, size), jnp.float32),
            jax.ShapeDtypeStruct((BLOCK, BLOCK), jnp.float32),
        ),
        in_specs=[smem()] + [vmem()] * len(lead),
        out_specs=(vmem(),) * 7,
        scratch_shapes=columns_scratch(order, FIRST_TILES, size),
        compiler_params=pltpu.CompilerParams(vmem_limit_bytes=VMEM_BYTES),
    )(ids, *lead)


def factorize_second(rest, begun, size):
    order = rest.shape[0]

    def kernel(rest_ref, begun_ref, high_ref, low_ref, ih_ref, il_ref, out_ref, column_ref, full, inverses, work):
        full[...] = rest_ref[...]
        inverses[0] = begun_ref[...]
        eliminate(full, inverses, work, range(1, size // BLOCK))
        columns_out(full, inverses, 1, high_ref, low_ref, ih_ref, il_ref, out_ref)
        column_ref[...] = full[:, 0:size]

    return pl.pallas_call(
        kernel,
        name="factorize_second",
        out_shape=(*columns_shapes(order, 1, size), jax.ShapeDtypeStruct((order, size), jnp.float32)),
        in_specs=[vmem()] * 2,
        out_specs=(vmem(),) * 6,
        scratch_shapes=columns_scratch(order, 1, size),
        compiler_params=pltpu.CompilerParams(vmem_limit_bytes=VMEM_BYTES),
    )(rest, begun)


def factorize_next(rest):
    def kernel(rest_ref, out_ref, inverses, work):
        out_ref[...] = rest_ref[...]
        eliminate(out_ref, inverses, work, range(1))

    return pl.pallas_call(
        kernel,
        name="factorize_next",
        out_shape=(
            jax.ShapeDtypeStruct(rest.shape, jnp.float32),
            jax.ShapeDtypeStruct((1, BLOCK, BLOCK), jnp.float32),
        ),
        in_specs=[vmem()],
        out_specs=(vmem(),) * 2,
        scratch_shapes=[pltpu.VMEM((BLOCK, BLOCK), jnp.float32)],
        compiler_params=pltpu.CompilerParams(vmem_limit_bytes=VMEM_BYTES),
    )(rest)


def factorize_last(rest, first_inverse):
    size = rest.shape[0]

    def kernel(rest_ref, first_ref, own_ref, ih_ref, il_ref, inverses, work):
        own_ref[...] = rest_ref[...]
        eliminate(own_ref, inverses, work, range(1, 2))
        own_ref[0:BLOCK, BLOCK:size] = jnp.zeros((BLOCK, size - BLOCK), jnp.float32)
        ih_ref[...], il_ref[...] = tile_inverse(first_ref[0], inverses[1], own_ref[BLOCK:size, 0:BLOCK])

    inv = jax.ShapeDtypeStruct((size, size), jnp.bfloat16)
    return pl.pallas_call(
        kernel,
        name="factorize_last",
        out_shape=(jax.ShapeDtypeStruct((size, size), jnp.float32), inv, inv),
        in_specs=[vmem()] * 2,
        out_specs=(vmem(),) * 3,
        scratch_shapes=[
            pltpu.VMEM((size // BLOCK, BLOCK, BLOCK), jnp.float32),
            pltpu.VMEM((BLOCK, BLOCK), jnp.float32),
        ],
        compiler_params=pltpu.CompilerParams(vmem_limit_bytes=VMEM_BYTES),
    )(rest, first_inverse)


def solve(panels, first, second, last):
    _, coded_rows, size = panels[0].shape
    thin, order = coded_rows - SCALE_ROWS, LEAD_TILES * size
    count = len(panels)
    inner = FIRST_TILES * size

    def kernel(*refs):
        panel_refs = refs[:count]
        high1, low1, ih1, il1, high2, low2, ih2, il2, ih3, il3 = refs[count : count + 10]
        *out_refs, xh, xl = refs[count + 10 :]
        for q in range(LEAD_TILES):
            s, e = q * size, (q + 1) * size
            acc = jnp.concatenate([decode(ref[q]) for ref in panel_refs], axis=0)
            if q:
                k = min(s, inner)
                acc = acc - nt3((xh[:, 0:k], xl[:, 0:k]), (high1[s:e, 0:k], low1[s:e, 0:k]))
            if s > inner:
                y = slice(s - inner, e - inner)
                acc = acc - nt3((xh[:, inner:s], xl[:, inner:s]), (high2[y, :], low2[y, :]))
            if q < FIRST_TILES:
                inverse = (ih1[q], il1[q])
            elif q == FIRST_TILES:
                inverse = (ih2[0], il2[0])
            else:
                inverse = (ih3[...], il3[...])
            x = nt3(split(acc), inverse)
            if e < order:
                xh[:, s:e], xl[:, s:e] = split(x)
            for number in range(count):
                out_refs[number // 2][number % 2, q] = encode(x[number * thin : (number + 1) * thin])

    return pl.pallas_call(
        kernel,
        name="solve",
        out_shape=(jax.ShapeDtypeStruct((2, LEAD_TILES, coded_rows, size), jnp.int16),) * (count // 2),
        in_specs=[vmem()] * (count + 10),
        out_specs=(vmem(),) * (count // 2),
        scratch_shapes=[pltpu.VMEM((count * thin, order - size), jnp.bfloat16)] * 2,
        compiler_params=pltpu.CompilerParams(vmem_limit_bytes=VMEM_BYTES),
    )(*panels, *first, *second, *last)


def finish(ids, rows, cols, own, column, last_own, extended, corner, tile_rows, tile_cols):
    size = own.shape[0]
    order = LEAD_TILES * size
    lanes = 128
    parts = size // lanes
    half = len(rows)

    def kernel(ids_ref, *refs):
        own_ref, column_ref, last_own_ref, ext_ref, corner_ref, out_ref, xh, xl = refs[2 * half : 2 * half + 8]
        landed, sems = refs[2 * half + 8 : -1], refs[-1]
        copies = [pltpu.make_async_copy(refs[n], landed[n], sems.at[n]) for n in range(2 * half)]
        for copy in copies:
            copy.start()
        row_pieces, col_pieces = landed[:half], landed[half:]
        row, col = ids_ref[0], ids_ref[1]

        def put(a, b, tile):
            for part in range(parts):
                start = (a * size * tile_cols + b) * parts + part
                out_ref[pl.ds(start, size, stride=tile_cols * parts), :] = tile[:, part * lanes : (part + 1) * lanes]

        zero = jnp.zeros((size, size), jnp.float32)
        for a, b in ((0, 1), (0, 2), (1, 2)):
            put(a, b, zero)
        for pieces, place, first in ((row_pieces, col, 0), (col_pieces, row, tile_rows * size)):
            for ref, inner, chunk in pair_pieces(pieces, place):
                if inner == 0:
                    copies[next(n for n in range(2 * half) if landed[n] is ref)].wait()
                for q in range(LEAD_TILES):
                    value = decode(ref[inner, q])
                    thin = value.shape[0]
                    start = pl.multiple_of(first + chunk * thin, 32)
                    high, low = split(value)
                    xh[pl.ds(start, thin), q * size : (q + 1) * size] = high
                    xl[pl.ds(start, thin), q * size : (q + 1) * size] = low

        def take(ref, n):
            return ref[n * size : (n + 1) * size, :]

        def update(a, b, base):
            x, y = a, tile_rows + b
            put(a, b, base - nt3((take(xh, x), take(xl, x)), (take(xh, y), take(xl, y))))

        def put_panel(a):
            for q in range(LEAD_TILES):

                @pl.when(col == q)
                def _():
                    high = xh[a * size : (a + 1) * size, q * size : (q + 1) * size].astype(jnp.float32)
                    low = xl[a * size : (a + 1) * size, q * size : (q + 1) * size].astype(jnp.float32)
                    put(a, 0, high + low)

        in_panel = col < LEAD_TILES
        lead_row = row < LEAD_TILES
        last_tile = LEAD_TILES - 1
        put_panel(1)
        put_panel(2)

        @pl.when(jnp.logical_not(in_panel))
        def _():
            update(1, 0, ext_ref[0])
            update(2, 0, ext_ref[2])

        @pl.when(row < col)
        def _():
            put(0, 0, zero)
            put(1, 1, zero)
            put(2, 2, zero)

        @pl.when(row >= col)
        def _():
            @pl.when(lead_row)
            def _():
                start = pl.multiple_of(jnp.clip(row - FIRST_TILES, 0, 1) * size, size)
                late = jnp.where(col == last_tile, last_own_ref[...], column_ref[pl.ds(start, size), :])
                put(0, 0, jnp.where(col < FIRST_TILES, own_ref[...], late))

            @pl.when(jnp.logical_not(lead_row))
            def _():
                put_panel(0)

            @pl.when(jnp.logical_not(in_panel))
            def _():
                update(0, 0, corner_ref[...].astype(jnp.float32))

            update(1, 1, ext_ref[1])
            update(2, 2, ext_ref[4])

        update(2, 1, ext_ref[3])

    return pl.pallas_call(
        kernel,
        name="finish",
        out_shape=jax.ShapeDtypeStruct((tile_rows * size * tile_cols * parts, lanes), jnp.float32),
        in_specs=[smem()] + [hbm()] * (2 * half) + [vmem()] * 5,
        out_specs=vmem(),
        scratch_shapes=[
            *[pltpu.VMEM((2 * tile_rows * size, order), jnp.bfloat16)] * 2,
            *[pltpu.VMEM(piece.shape, piece.dtype) for piece in (*rows, *cols)],
            pltpu.SemaphoreType.DMA((2 * half,)),
        ],
        compiler_params=pltpu.CompilerParams(vmem_limit_bytes=VMEM_BYTES),
    )(ids, *rows, *cols, own, column, last_own, extended, corner)


def exchange(value, axis):
    return lax.all_to_all(value, axis, split_axis=0, concat_axis=0, tiled=True)


def permute(value, axis, target):
    return lax.ppermute(value, axis, [(i, target(i)) for i in range(lax.axis_size(axis))])


def ring_gather(value, axis):
    ring = lax.axis_size(axis) // 2
    half = value.shape[0] // 2

    def shift(array, steps):
        return permute(array, axis, lambda i: (i // 2 + steps) % ring * 2 + i % 2)

    before, after = shift(value, 1), shift(value, ring - 1)
    return (value, before, after, shift(before[:half], 1), shift(after[half:], ring - 1))


def ring_pieces(pieces, place, length):
    ring = len(pieces) - 1
    for ref, step, first in zip(pieces, (0, 1, 3, 2, 2), (0, 0, 0, 0, length // 2), strict=True):
        yield ref, first, lax.rem(place + (ring - step), ring)


def pair_pieces(pieces, place):
    side = lax.rem(place, 2)
    for ref, first, source in ring_pieces(pieces, lax.div(place, 2), 2):
        for position in range(ref.shape[0]):
            yield ref, position, 2 * source + (side if first + position == 0 else 1 - side)


def per_device(front_matrix, contributions, target_front, target_row, target_col, live_count):
    _, tile_rows, _, size, tile_cols, _, _ = front_matrix.shape
    n_front, n_row, n_col = (lax.axis_size(name) for name in ("front", "row", "col"))
    slots = contributions.shape[3]
    front = front_matrix.reshape(tile_rows, size, tile_cols, size).transpose(0, 2, 1, 3)
    ids = jnp.stack([lax.axis_index("row"), lax.axis_index("col")]).astype(jnp.int32)

    ring = n_col // 2
    thin = size // ring
    chunks = jnp.repeat(front[0, 0].reshape(ring, thin, size), 2, axis=0)
    chunk = exchange(chunks, "col")[:LEAD_TILES]
    owners = range(LEAD_TILES)
    partner = lax.ppermute(chunk, "row", [(i, i ^ 1) for i in owners])
    pair = jnp.stack([chunk, partner])
    leading = [pair]
    for step in range(1, n_row // 2):
        leading.append(lax.ppermute(pair, "row", [(i, (i + 2 * step) % n_row) for i in owners]))

    packed = pack(
        contributions.reshape(slots, size, size),
        target_front.reshape(slots), target_row.reshape(slots), target_col.reshape(slots),
        live_count.reshape(1), n_front, n_row, n_col, tile_cols,
    )
    received = exchange(packed, ("front", "row"))

    lead = ring_gather(collect(ids, leading), "col")
    *first, rest, own, begun = factorize_first(ids, lead, size)
    received, rest = lax.optimization_barrier((received, rest))

    extended, panel = assemble(received, front, n_col)
    mine = exchange(panel, "col")[:LEAD_TILES]
    *second, rest, column = factorize_second(rest, begun, size)
    turned = lax.ppermute(
        mine, ("row", "col"), [(r * n_col + c, c * n_col + r) for r in range(n_row) for c in range(n_col)]
    )
    beside = permute(mine, "col", lambda i: i ^ 1)
    rest, first_inverse = factorize_next(rest)
    turned_beside = permute(turned, "row", lambda i: i ^ 1)
    last_own, *last = factorize_last(rest, first_inverse)
    row_pair, col_pair = solve((mine, beside, turned, turned_beside), first, second, last)
    rows = ring_gather(row_pair, "col")
    cols = ring_gather(col_pair, "row")
    factor = finish(ids, rows, cols, own, column, last_own, extended, front[0, 0], tile_rows, tile_cols)
    return factor.reshape(1, tile_rows, 1, size, tile_cols, 1, size)


def solution(mesh):
    in_specs = (
        P("front", None, "row", None, None, "col", None),
        P("front", "row", "col", None, None, None),
        P("front", "row", "col", None),
        P("front", "row", "col", None),
        P("front", "row", "col", None),
        P("front", "row", "col"),
    )
    out_specs = P("front", None, "row", None, None, "col", None)
    return jax.shard_map(per_device, mesh=mesh, in_specs=in_specs, out_specs=out_specs, check_vma=False)
```

```python
import jax
import jax.numpy as jnp
from jax import lax
from jax.experimental import pallas as pl
from jax.experimental.pallas import tpu as pltpu
from jax.sharding import PartitionSpec as P


LEAD_TILES = 4
BLOCK = 128
HALF = 64
RUN = 32
STRIP = 8
LANES = 128
VMEM_BYTES = 56 * 1024 * 1024


def vmem():
    return pl.BlockSpec(memory_space=pltpu.VMEM)


def smem():
    return pl.BlockSpec(memory_space=pltpu.SMEM)


def hbm():
    return pl.BlockSpec(memory_space=pl.ANY)


def nt(left, right, precision=None):
    return lax.dot_general(
        left, right, (((1,), (1,)), ((), ())), precision=precision, preferred_element_type=jnp.float32
    )


def split(value):
    high = value.astype(jnp.bfloat16)
    return high, (value - high.astype(jnp.float32)).astype(jnp.bfloat16)


def nt3(left, right):
    return nt(left[0], right[0]) + (nt(left[0], right[1]) + nt(left[1], right[0]))


NOTE_ROWS = 8


def pack(contributions, target_front, target_row, target_col, live_count, n_front, n_row, n_col, tile_cols):
    slots, size, _ = contributions.shape
    capacity = max(2, -(-slots // (n_front * n_row)))
    buckets = n_front * n_row * capacity
    kind = contributions.dtype

    def kernel(
        front_ref, row_ref, col_ref, live_ref, tiles_ref, packed_ref,
        counts, bucket_of, stage, notes, sems_in, sems_out, note_sem,
    ):
        live = live_ref[0]

        def fetch(slot):
            return pltpu.make_async_copy(tiles_ref.at[slot], stage.at[slot], sems_in.at[slot])

        def store(slot, bucket):
            return pltpu.make_async_copy(stage.at[slot], packed_ref.at[bucket, pl.ds(0, size)], sems_out.at[slot])

        def start(slot, carry):
            fetch(slot).start()
            return carry

        lax.fori_loop(0, live, start, 0)
        notes[...] = jnp.full(notes.shape, -1.0, kind)

        def clear(i, carry):
            counts[i] = 0
            return carry

        lax.fori_loop(0, n_front * n_row, clear, 0)

        def assign(slot, carry):
            row, col = row_ref[slot], col_ref[slot]
            destination = front_ref[slot] * n_row + lax.rem(row, n_row)
            position = counts[destination]
            counts[destination] = position + 1
            bucket = destination * capacity + position
            bucket_of[slot] = bucket
            target = lax.div(row, n_row) * tile_cols + lax.div(col, n_col)
            notes[bucket] = jnp.full(notes.shape[1:], target, jnp.int32).astype(jnp.float32).astype(kind)
            return carry

        lax.fori_loop(0, live, assign, 0)
        note_copy = pltpu.make_async_copy(notes, packed_ref.at[:, pl.ds(size, NOTE_ROWS)], note_sem)
        note_copy.start()

        def forward(slot, carry):
            fetch(slot).wait()
            store(slot, bucket_of[slot]).start()
            return carry

        lax.fori_loop(0, live, forward, 0)

        def drain(slot, carry):
            store(slot, bucket_of[slot]).wait()
            return carry

        lax.fori_loop(0, live, drain, 0)
        note_copy.wait()

    return pl.pallas_call(
        kernel,
        name="pack",
        out_shape=jax.ShapeDtypeStruct((buckets, size + NOTE_ROWS, size), kind),
        in_specs=[smem()] * 4 + [hbm()],
        out_specs=hbm(),
        scratch_shapes=[
            pltpu.SMEM((n_front * n_row,), jnp.int32),
            pltpu.SMEM((slots,), jnp.int32),
            pltpu.VMEM((slots, size, size), kind),
            pltpu.VMEM((buckets, NOTE_ROWS, size), kind),
            pltpu.SemaphoreType.DMA((slots,)),
            pltpu.SemaphoreType.DMA((slots,)),
            pltpu.SemaphoreType.DMA,
        ],
        compiler_params=pltpu.CompilerParams(vmem_limit_bytes=VMEM_BYTES),
    )(target_front, target_row, target_col, live_count, contributions)


SCALE_ROWS = 8
SCALE_STEPS = 64


def picked(n):
    shape = (n, LANES)
    return lax.broadcasted_iota(jnp.int32, shape, 0) == lax.broadcasted_iota(jnp.int32, shape, 1)


def encode(values):
    n, m = values.shape
    top = jnp.max(jnp.abs(values), axis=1, keepdims=True)
    code = jnp.floor(jnp.log2(jnp.maximum(top, 2.0**-110)) * SCALE_STEPS) + 1.0
    coded = jnp.round(values * jnp.exp2(15.0 - 1e-3 - code / SCALE_STEPS))
    line = jnp.sum(jnp.where(picked(n), code, 0.0), axis=0, keepdims=True)
    lines = jnp.broadcast_to(jnp.concatenate([line] * (m // LANES), axis=1), (SCALE_ROWS, m))
    return jnp.concatenate([coded, lines], axis=0).astype(jnp.int32).astype(jnp.int16)


def decode(coded):
    wide = coded.astype(jnp.int32).astype(jnp.float32)
    n = wide.shape[0] - SCALE_ROWS
    scales = jnp.exp2(wide[n : n + 1, 0:LANES] / SCALE_STEPS - 15.0 + 1e-3)
    scale = jnp.sum(jnp.where(picked(n), jnp.broadcast_to(scales, (n, LANES)), 0.0), axis=1, keepdims=True)
    return wide[:n] * scale


EXTENDED = ((1, 0), (1, 1), (2, 0), (2, 1), (2, 2))


def assemble(received, front, chunks):
    total, _, size = received.shape
    thin = front.shape[0] * size // chunks

    def kernel(
        received_ref, front_ref, ext_ref, panel_ref, landed, column, notes, numbers, arrived_ref, sems, note_sem
    ):
        note_copy = pltpu.make_async_copy(received_ref.at[:, pl.ds(size, NOTE_ROWS)], notes, note_sem)
        note_copy.start()

        def copy(i):
            return pltpu.make_async_copy(received_ref.at[i, pl.ds(0, size)], landed.at[i], sems.at[i])

        def fetch(i, carry):
            @pl.when(arrived_ref[i, 0] >= 0)
            def _():
                copy(i).start()

            return carry

        note_copy.wait()
        for i in range(total):
            numbers[i : i + 1, :] = notes[i, 0:1, 0 : numbers.shape[1]].astype(jnp.float32).astype(jnp.int32)
        number_copy = pltpu.make_async_copy(numbers, arrived_ref, note_sem)
        number_copy.start()
        for slot, (a, b) in enumerate(EXTENDED):
            ext_ref[slot] = front_ref[a, b].astype(jnp.float32)
        number_copy.wait()
        lax.fori_loop(0, total, fetch, 0)

        def add(i, carry):
            target = arrived_ref[i, 0]

            @pl.when(target >= 0)
            def _():
                copy(i).wait()
                slot = jnp.where(target >= 6, target - 4, target - 3)
                ext_ref[slot] = ext_ref[slot] + landed[i].astype(jnp.float32)

            return carry

        lax.fori_loop(0, total, add, 0)
        column[0:size] = front_ref[0, 0].astype(jnp.float32)
        column[size : 2 * size] = ext_ref[0]
        column[2 * size : 3 * size] = ext_ref[2]
        for chunk in range(chunks):
            panel_ref[chunk] = encode(column[chunk * thin : (chunk + 1) * thin, :])

    return pl.pallas_call(
        kernel,
        name="assemble",
        out_shape=(
            jax.ShapeDtypeStruct((len(EXTENDED), size, size), jnp.float32),
            jax.ShapeDtypeStruct((chunks, thin + SCALE_ROWS, size), jnp.int16),
        ),
        in_specs=[hbm(), vmem()],
        out_specs=(vmem(), vmem()),
        scratch_shapes=[
            pltpu.VMEM((total, size, size), jnp.bfloat16),
            pltpu.VMEM((3 * size, size), jnp.float32),
            pltpu.VMEM((total, NOTE_ROWS, size), jnp.bfloat16),
            pltpu.VMEM((total, 128), jnp.int32),
            pltpu.SMEM((total, 128), jnp.int32),
            pltpu.SemaphoreType.DMA((total,)),
            pltpu.SemaphoreType.DMA,
        ],
        compiler_params=pltpu.CompilerParams(vmem_limit_bytes=VMEM_BYTES),
    )(received, front)


def pick_lane(value, lane):
    index = jnp.full(value.shape, lane, jnp.int32)
    return jnp.take_along_axis(value, index, axis=1, mode="promise_in_bounds")


def factor_block(work):
    lanes = lax.broadcasted_iota(jnp.int32, (STRIP, BLOCK), 1)
    strip_rows = lax.broadcasted_iota(jnp.int32, (STRIP, BLOCK), 0)

    def spread(value, i):
        return jnp.broadcast_to(value[i : i + 1, :], value.shape)

    def step(number, top, bottom):
        base = pl.multiple_of(number * STRIP, STRIP)
        strip = work[pl.ds(base, STRIP), :]
        own = [pick_lane(strip, base + i) for i in range(STRIP)]
        whole = work[top:bottom, :]
        below = lax.broadcasted_iota(jnp.int32, whole.shape, 0) + top >= base + STRIP
        columns = [jnp.where(below, pick_lane(whole, base + i), 0.0) for i in range(STRIP)]
        for i in range(STRIP):
            pivot = spread(own[i], i)
            inverse = 1.0 / pivot
            factors = jnp.where(strip_rows > i, own[i] * inverse, 0.0)
            line = jnp.where(lanes == base + i, pivot + pivot, spread(strip, i))
            strip = strip - factors * line
            lower = columns[i] * jnp.broadcast_to(inverse[0:1], whole.shape)
            for j in range(i + 1, STRIP):
                entry = spread(own[j], i)
                own[j] = own[j] - factors * entry
                columns[j] = columns[j] - lower * jnp.broadcast_to(entry[0:1], whole.shape)
            whole = whole - lower * jnp.broadcast_to(line[0:1], whole.shape)
        work[top:bottom, :] = whole
        work[pl.ds(base, STRIP), :] = strip

    for first in range(0, BLOCK, HALF):
        last = first + HALF
        for top in range(first, last, RUN):

            def run(number, carry, top=top):
                step(number, top, last)
                return carry

            lax.fori_loop(top // STRIP, (top + RUN) // STRIP, run, 0)
        if last < BLOCK:
            done = work[first:last, :]
            at_pivot = lax.broadcasted_iota(jnp.int32, done.shape, 0) + first == lax.broadcasted_iota(
                jnp.int32, done.shape, 1
            )
            pivots = jnp.where(at_pivot, done, 0.0)
            scaled = done / jnp.sum(pivots, axis=1, keepdims=True)
            change = lax.dot_general(
                scaled, done + pivots, (((0,), (0,)), ((), ())),
                precision=lax.Precision.HIGHEST, preferred_element_type=jnp.float32,
            )
            work[last:BLOCK, :] = work[last:BLOCK, :] - change[last:BLOCK, :]


def eliminate(full, inverses, work, blocks):
    order = full.shape[0]
    r = lax.broadcasted_iota(jnp.int32, (BLOCK, BLOCK), 0)
    c = lax.broadcasted_iota(jnp.int32, (BLOCK, BLOCK), 1)
    for k in blocks:
        s, e = k * BLOCK, (k + 1) * BLOCK
        work[...] = full[s:e, s:e]
        factor_block(work)
        done = work[...]
        diagonal = jnp.where(r == c, done, 0.0)
        root = lax.rsqrt(jnp.sum(diagonal, axis=1, keepdims=True))
        inverse = jnp.where(r >= c, done, 0.0) * root * (1.0 / jnp.sum(diagonal, axis=0, keepdims=True))
        inverses[k] = inverse
        full[s:e, s:e] = (jnp.where(r <= c, done, 0.0) * root).T
        if e < order:
            panel = nt3(split(full[e:order, s:e]), split(inverse))
            full[e:order, s:e] = panel
            high, low = split(panel)
            for o in range(e, order, BLOCK):
                y = slice(o - e, o - e + BLOCK)
                full[o:order, o : o + BLOCK] = full[o:order, o : o + BLOCK] - nt3(
                    (high[o - e :], low[o - e :]), (high[y], low[y])
                )


def tile_inverse(first, second, between):
    def product(left, right):
        return jnp.dot(left, right, precision=lax.Precision.HIGHEST, preferred_element_type=jnp.float32)

    corner = -product(second, product(between, first))
    above = jnp.concatenate([first, jnp.zeros_like(first)], axis=1)
    return split(jnp.concatenate([above, jnp.concatenate([corner, second], axis=1)], axis=0))


PAIRS = tuple((i, j) for i in range(LEAD_TILES) for j in range(i + 1))


def collect(ids, pairs):
    _, _, thin, size = pairs[0].shape
    ring = len(pairs)

    def kernel(ids_ref, *refs):
        *pair_refs, out_ref, sems = refs
        place, side = lax.div(ids_ref[0], 2), lax.rem(ids_ref[0], 2)
        copies = []
        for i in range(LEAD_TILES):
            first = PAIRS.index((i, 0))
            inner = lax.rem(side + i, 2)
            steps = lax.rem(place - i // 2 + ring, ring)

            def copy(ref, i=i, first=first, inner=inner):
                return pltpu.make_async_copy(
                    ref.at[inner, pl.ds(0, i + 1)], out_ref.at[pl.ds(first, i + 1)], sems.at[i]
                )

            for s in range(ring):

                @pl.when(steps == s)
                def _():
                    copy(pair_refs[s]).start()

            copies.append(copy(pair_refs[0]))
        for one in copies:
            one.wait()

    return pl.pallas_call(
        kernel,
        name="collect",
        out_shape=jax.ShapeDtypeStruct((len(PAIRS), thin, size), pairs[0].dtype),
        in_specs=[smem()] + [hbm()] * ring,
        out_specs=vmem(),
        scratch_shapes=[pltpu.SemaphoreType.DMA((LEAD_TILES,))],
    )(ids, *pairs)


FIRST_TILES = 2


def columns_out(full, inverses, tiles, high_ref, low_ref, ih_ref, il_ref, rest_ref):
    order = full.shape[0]
    size = ih_ref.shape[1]
    half = size // BLOCK
    for q in range(tiles):
        s, e = q * size, (q + 1) * size
        full[s : s + BLOCK, s + BLOCK : e] = jnp.zeros((BLOCK, size - BLOCK), jnp.float32)
        ih_ref[q], il_ref[q] = tile_inverse(inverses[q * half], inverses[q * half + 1], full[s + BLOCK : e, s : s + BLOCK])
        if e < order:
            high_ref[e:order, s:e], low_ref[e:order, s:e] = split(full[e:order, s:e])
    done = tiles * size
    rest_ref[...] = full[done:order, done:order]


def columns_shapes(order, tiles, size):
    wide = jax.ShapeDtypeStruct((order, tiles * size), jnp.bfloat16)
    inv = jax.ShapeDtypeStruct((tiles, size, size), jnp.bfloat16)
    left = order - tiles * size
    return (wide, wide, inv, inv, jax.ShapeDtypeStruct((left, left), jnp.float32))


def columns_scratch(order, tiles, size):
    return [
        pltpu.VMEM((order, order), jnp.float32),
        pltpu.VMEM((tiles * size // BLOCK + 1, BLOCK, BLOCK), jnp.float32),
        pltpu.VMEM((BLOCK, BLOCK), jnp.float32),
    ]


def factorize_first(ids, lead, size):
    order = LEAD_TILES * size

    def kernel(ids_ref, *refs):
        *pieces, high_ref, low_ref, ih_ref, il_ref, rest_ref, own_ref, begun_ref, full, inverses, work = refs
        for ref, first, source in ring_pieces(pieces, lax.div(ids_ref[1], 2), len(PAIRS)):
            for number in range(ref.shape[0]):
                i, j = PAIRS[first + number]
                tile = ref[number].astype(jnp.float32)
                thin = tile.shape[0]
                start = pl.multiple_of(i * size + source * thin, thin)
                full[pl.ds(start, thin), j * size : (j + 1) * size] = tile
        steps = FIRST_TILES * size // BLOCK
        eliminate(full, inverses, work, range(steps + 1))
        begun_ref[...] = inverses[steps]
        columns_out(full, inverses, FIRST_TILES, high_ref, low_ref, ih_ref, il_ref, rest_ref)
        for i, j in PAIRS:
            if j < FIRST_TILES:

                @pl.when((ids_ref[0] == i) & (ids_ref[1] == j))
                def _():
                    own_ref[...] = full[i * size : (i + 1) * size, j * size : (j + 1) * size]

    return pl.pallas_call(
        kernel,
        name="factorize_first",
        out_shape=(
            *columns_shapes(order, FIRST_TILES, size),
            jax.ShapeDtypeStruct((size, size), jnp.float32),
            jax.ShapeDtypeStruct((BLOCK, BLOCK), jnp.float32),
        ),
        in_specs=[smem()] + [vmem()] * len(lead),
        out_specs=(vmem(),) * 7,
        scratch_shapes=columns_scratch(order, FIRST_TILES, size),
        compiler_params=pltpu.CompilerParams(vmem_limit_bytes=VMEM_BYTES),
    )(ids, *lead)


def factorize_second(rest, begun, size):
    order = rest.shape[0]

    def kernel(rest_ref, begun_ref, high_ref, low_ref, ih_ref, il_ref, out_ref, column_ref, full, inverses, work):
        full[...] = rest_ref[...]
        inverses[0] = begun_ref[...]
        eliminate(full, inverses, work, range(1, size // BLOCK))
        columns_out(full, inverses, 1, high_ref, low_ref, ih_ref, il_ref, out_ref)
        column_ref[...] = full[:, 0:size]

    return pl.pallas_call(
        kernel,
        name="factorize_second",
        out_shape=(*columns_shapes(order, 1, size), jax.ShapeDtypeStruct((order, size), jnp.float32)),
        in_specs=[vmem()] * 2,
        out_specs=(vmem(),) * 6,
        scratch_shapes=columns_scratch(order, 1, size),
        compiler_params=pltpu.CompilerParams(vmem_limit_bytes=VMEM_BYTES),
    )(rest, begun)


def factorize_next(rest):
    def kernel(rest_ref, out_ref, inverses, work):
        out_ref[...] = rest_ref[...]
        eliminate(out_ref, inverses, work, range(1))

    return pl.pallas_call(
        kernel,
        name="factorize_next",
        out_shape=(
            jax.ShapeDtypeStruct(rest.shape, jnp.float32),
            jax.ShapeDtypeStruct((1, BLOCK, BLOCK), jnp.float32),
        ),
        in_specs=[vmem()],
        out_specs=(vmem(),) * 2,
        scratch_shapes=[pltpu.VMEM((BLOCK, BLOCK), jnp.float32)],
        compiler_params=pltpu.CompilerParams(vmem_limit_bytes=VMEM_BYTES),
    )(rest)


def factorize_last(rest, first_inverse):
    size = rest.shape[0]

    def kernel(rest_ref, first_ref, own_ref, ih_ref, il_ref, inverses, work):
        own_ref[...] = rest_ref[...]
        eliminate(own_ref, inverses, work, range(1, 2))
        own_ref[0:BLOCK, BLOCK:size] = jnp.zeros((BLOCK, size - BLOCK), jnp.float32)
        ih_ref[...], il_ref[...] = tile_inverse(first_ref[0], inverses[1], own_ref[BLOCK:size, 0:BLOCK])

    inv = jax.ShapeDtypeStruct((size, size), jnp.bfloat16)
    return pl.pallas_call(
        kernel,
        name="factorize_last",
        out_shape=(jax.ShapeDtypeStruct((size, size), jnp.float32), inv, inv),
        in_specs=[vmem()] * 2,
        out_specs=(vmem(),) * 3,
        scratch_shapes=[
            pltpu.VMEM((size // BLOCK, BLOCK, BLOCK), jnp.float32),
            pltpu.VMEM((BLOCK, BLOCK), jnp.float32),
        ],
        compiler_params=pltpu.CompilerParams(vmem_limit_bytes=VMEM_BYTES),
    )(rest, first_inverse)


def solve(panels, first, second, last):
    _, coded_rows, size = panels[0].shape
    thin, order = coded_rows - SCALE_ROWS, LEAD_TILES * size
    count = len(panels)
    inner = FIRST_TILES * size

    def kernel(*refs):
        panel_refs = refs[:count]
        high1, low1, ih1, il1, high2, low2, ih2, il2, ih3, il3 = refs[count : count + 10]
        *out_refs, xh, xl = refs[count + 10 :]
        for q in range(LEAD_TILES):
            s, e = q * size, (q + 1) * size
            acc = jnp.concatenate([decode(ref[q]) for ref in panel_refs], axis=0)
            if q:
                k = min(s, inner)
                acc = acc - nt3((xh[:, 0:k], xl[:, 0:k]), (high1[s:e, 0:k], low1[s:e, 0:k]))
            if s > inner:
                y = slice(s - inner, e - inner)
                acc = acc - nt3((xh[:, inner:s], xl[:, inner:s]), (high2[y, :], low2[y, :]))
            if q < FIRST_TILES:
                inverse = (ih1[q], il1[q])
            elif q == FIRST_TILES:
                inverse = (ih2[0], il2[0])
            else:
                inverse = (ih3[...], il3[...])
            x = nt3(split(acc), inverse)
            if e < order:
                xh[:, s:e], xl[:, s:e] = split(x)
            for number in range(count):
                out_refs[number // 2][number % 2, q] = encode(x[number * thin : (number + 1) * thin])

    return pl.pallas_call(
        kernel,
        name="solve",
        out_shape=(jax.ShapeDtypeStruct((2, LEAD_TILES, coded_rows, size), jnp.int16),) * (count // 2),
        in_specs=[vmem()] * (count + 10),
        out_specs=(vmem(),) * (count // 2),
        scratch_shapes=[pltpu.VMEM((count * thin, order - size), jnp.bfloat16)] * 2,
        compiler_params=pltpu.CompilerParams(vmem_limit_bytes=VMEM_BYTES),
    )(*panels, *first, *second, *last)


def finish(ids, rows, cols, own, column, last_own, extended, corner, tile_rows, tile_cols):
    size = own.shape[0]
    order = LEAD_TILES * size
    lanes = 128
    parts = size // lanes
    half = len(rows)

    def kernel(ids_ref, *refs):
        row_pieces, col_pieces = refs[:half], refs[half : 2 * half]
        own_ref, column_ref, last_own_ref, ext_ref, corner_ref, out_ref, xh, xl = refs[2 * half :]
        row, col = ids_ref[0], ids_ref[1]

        def put(a, b, tile):
            for part in range(parts):
                start = (a * size * tile_cols + b) * parts + part
                out_ref[pl.ds(start, size, stride=tile_cols * parts), :] = tile[:, part * lanes : (part + 1) * lanes]

        for pieces, place, first in ((row_pieces, col, 0), (col_pieces, row, tile_rows * size)):
            for ref, inner, chunk in pair_pieces(pieces, place):
                for q in range(LEAD_TILES):
                    value = decode(ref[inner, q])
                    thin = value.shape[0]
                    start = pl.multiple_of(first + chunk * thin, 32)
                    high, low = split(value)
                    xh[pl.ds(start, thin), q * size : (q + 1) * size] = high
                    xl[pl.ds(start, thin), q * size : (q + 1) * size] = low

        def take(ref, n):
            return ref[n * size : (n + 1) * size, :]

        def update(a, b, base):
            x, y = a, tile_rows + b
            put(a, b, base - nt3((take(xh, x), take(xl, x)), (take(xh, y), take(xl, y))))

        def put_panel(a):
            for q in range(LEAD_TILES):

                @pl.when(col == q)
                def _():
                    high = xh[a * size : (a + 1) * size, q * size : (q + 1) * size].astype(jnp.float32)
                    low = xl[a * size : (a + 1) * size, q * size : (q + 1) * size].astype(jnp.float32)
                    put(a, 0, high + low)

        zero = jnp.zeros((size, size), jnp.float32)
        for a, b in ((0, 1), (0, 2), (1, 2)):
            put(a, b, zero)
        in_panel = col < LEAD_TILES
        lead_row = row < LEAD_TILES
        last_tile = LEAD_TILES - 1
        put_panel(1)
        put_panel(2)

        @pl.when(jnp.logical_not(in_panel))
        def _():
            update(1, 0, ext_ref[0])
            update(2, 0, ext_ref[2])

        @pl.when(row < col)
        def _():
            put(0, 0, zero)
            put(1, 1, zero)
            put(2, 2, zero)

        @pl.when(row >= col)
        def _():
            @pl.when(lead_row)
            def _():
                start = pl.multiple_of(jnp.clip(row - FIRST_TILES, 0, 1) * size, size)
                late = jnp.where(col == last_tile, last_own_ref[...], column_ref[pl.ds(start, size), :])
                put(0, 0, jnp.where(col < FIRST_TILES, own_ref[...], late))

            @pl.when(jnp.logical_not(lead_row))
            def _():
                put_panel(0)

            @pl.when(jnp.logical_not(in_panel))
            def _():
                update(0, 0, corner_ref[...].astype(jnp.float32))

            update(1, 1, ext_ref[1])
            update(2, 2, ext_ref[4])

        update(2, 1, ext_ref[3])

    return pl.pallas_call(
        kernel,
        name="finish",
        out_shape=jax.ShapeDtypeStruct((tile_rows * size * tile_cols * parts, lanes), jnp.float32),
        in_specs=[smem()] + [vmem()] * (2 * half + 5),
        out_specs=vmem(),
        scratch_shapes=[pltpu.VMEM((2 * tile_rows * size, order), jnp.bfloat16)] * 2,
        compiler_params=pltpu.CompilerParams(vmem_limit_bytes=VMEM_BYTES),
    )(ids, *rows, *cols, own, column, last_own, extended, corner)


def exchange(value, axis):
    return lax.all_to_all(value, axis, split_axis=0, concat_axis=0, tiled=True)


def permute(value, axis, target):
    return lax.ppermute(value, axis, [(i, target(i)) for i in range(lax.axis_size(axis))])


def ring_gather(value, axis):
    ring = lax.axis_size(axis) // 2
    half = value.shape[0] // 2

    def shift(array, steps):
        return permute(array, axis, lambda i: (i // 2 + steps) % ring * 2 + i % 2)

    before, after = shift(value, 1), shift(value, ring - 1)
    return (value, before, after, shift(before[:half], 1), shift(after[half:], ring - 1))


def ring_pieces(pieces, place, length):
    ring = len(pieces) - 1
    for ref, step, first in zip(pieces, (0, 1, 3, 2, 2), (0, 0, 0, 0, length // 2), strict=True):
        yield ref, first, lax.rem(place + (ring - step), ring)


def pair_pieces(pieces, place):
    side = lax.rem(place, 2)
    for ref, first, source in ring_pieces(pieces, lax.div(place, 2), 2):
        for position in range(ref.shape[0]):
            yield ref, position, 2 * source + (side if first + position == 0 else 1 - side)


def per_device(front_matrix, contributions, target_front, target_row, target_col, live_count):
    _, tile_rows, _, size, tile_cols, _, _ = front_matrix.shape
    n_front, n_row, n_col = (lax.axis_size(name) for name in ("front", "row", "col"))
    slots = contributions.shape[3]
    front = front_matrix.reshape(tile_rows, size, tile_cols, size).transpose(0, 2, 1, 3)
    ids = jnp.stack([lax.axis_index("row"), lax.axis_index("col")]).astype(jnp.int32)

    ring = n_col // 2
    thin = size // ring
    chunks = jnp.repeat(front[0, 0].reshape(ring, thin, size), 2, axis=0)
    chunk = exchange(chunks, "col")[:LEAD_TILES]
    owners = range(LEAD_TILES)
    partner = lax.ppermute(chunk, "row", [(i, i ^ 1) for i in owners])
    pair = jnp.stack([chunk, partner])
    leading = [pair]
    for step in range(1, n_row // 2):
        leading.append(lax.ppermute(pair, "row", [(i, (i + 2 * step) % n_row) for i in owners]))

    packed = pack(
        contributions.reshape(slots, size, size),
        target_front.reshape(slots), target_row.reshape(slots), target_col.reshape(slots),
        live_count.reshape(1), n_front, n_row, n_col, tile_cols,
    )
    received = exchange(packed, ("front", "row"))

    lead = ring_gather(collect(ids, leading), "col")
    *first, rest, own, begun = factorize_first(ids, lead, size)
    received, rest = lax.optimization_barrier((received, rest))

    extended, panel = assemble(received, front, n_col)
    mine = exchange(panel, "col")[:LEAD_TILES]
    *second, rest, column = factorize_second(rest, begun, size)
    turned = lax.ppermute(
        mine, ("row", "col"), [(r * n_col + c, c * n_col + r) for r in range(n_row) for c in range(n_col)]
    )
    beside = permute(mine, "col", lambda i: i ^ 1)
    rest, first_inverse = factorize_next(rest)
    turned_beside = permute(turned, "row", lambda i: i ^ 1)
    last_own, *last = factorize_last(rest, first_inverse)
    row_pair, col_pair = solve((mine, beside, turned, turned_beside), first, second, last)
    rows = ring_gather(row_pair, "col")
    cols = ring_gather(col_pair, "row")
    factor = finish(ids, rows, cols, own, column, last_own, extended, front[0, 0], tile_rows, tile_cols)
    return factor.reshape(1, tile_rows, 1, size, tile_cols, 1, size)


def solution(mesh):
    in_specs = (
        P("front", None, "row", None, None, "col", None),
        P("front", "row", "col", None, None, None),
        P("front", "row", "col", None),
        P("front", "row", "col", None),
        P("front", "row", "col", None),
        P("front", "row", "col"),
    )
    out_specs = P("front", None, "row", None, None, "col", None)
    return jax.shard_map(per_device, mesh=mesh, in_specs=in_specs, out_specs=out_specs, check_vma=False)
```
